32 devices in a mesh: dp: 16 (over z, y, x), tensor: 2 (over core).
Axes of the slice: x: 2, y: 2, z: 4, core: 2. Of those that a mesh axis runs over, the one named last changes fastest.
Arguments:
- tokens: bfloat16 [32768, 768], P(('dp', 'tensor')), may hold values from -6 to 6
- cotangent: bfloat16 [32768, 768], P(('dp', 'tensor')), may hold values from -6 to 6
- lengths: int32 [64], P('dp'), may hold values from 128 to 512, as said below
- query_weight: bfloat16 [768, 768], P('dp', 'tensor'), may hold values from -0.21875 to 0.21875
- key_weight: bfloat16 [768, 768], P('dp', 'tensor'), may hold values from -0.21875 to 0.21875
- value_weight: bfloat16 [768, 768], P('dp', 'tensor'), may hold values from -0.21875 to 0.21875
- out_weight: bfloat16 [768, 768], P('tensor', 'dp'), may hold values from -2.5 to 2.5
- query_bias: bfloat16 [768], P('dp'), may hold values from -3 to 3
- value_bias: bfloat16 [768], P('dp'), may hold values from -0.29882812 to 0.29882812
- out_bias: bfloat16 [768], P('dp'), may hold values from -3 to 3
- first_gain: bfloat16 [768], P('dp'), may hold values from 0.5 to 1.5
- first_shift: bfloat16 [768], P('dp'), may hold values from -2 to 2
- inner_weight: bfloat16 [768, 3072], P('dp', 'tensor'), may hold values from -0.21875 to 0.21875
- inner_bias: bfloat16 [3072], P('dp'), may hold values from -3 to 3
- outer_weight: bfloat16 [3072, 768], P('tensor', 'dp'), may hold values from -0.109375 to 0.109375
- outer_bias: bfloat16 [768], P('dp'), may hold values from -2 to 2
- second_gain: bfloat16 [768], P('dp'), may hold values from 0.5 to 1.5
- second_shift: bfloat16 [768], P('dp'), may hold values from -2 to 2
Outputs:
- layer_out: float32 [32768, 768], P(('dp', 'tensor'))
- token_grad: float32 [32768, 768], P(('dp', 'tensor'))
- query_weight_grad: float32 [768, 768], P('dp', 'tensor')
- key_weight_grad: float32 [768, 768], P('dp', 'tensor')
- value_weight_grad: float32 [768, 768], P('dp', 'tensor')
- out_weight_grad: float32 [768, 768], P('tensor', 'dp')
- query_bias_grad: float32 [768], P('dp')
- value_bias_grad: float32 [768], P('dp')
- out_bias_grad: float32 [768], P('dp')
- first_gain_grad: float32 [768], P('dp')
- first_shift_grad: float32 [768], P('dp')
- inner_weight_grad: float32 [768, 3072], P('dp', 'tensor')
- inner_bias_grad: float32 [3072], P('dp')
- outer_weight_grad: float32 [3072, 768], P('tensor', 'dp')
- outer_bias_grad: float32 [768], P('dp')
- second_gain_grad: float32 [768], P('dp')
- second_shift_grad: float32 [768], P('dp')
The draws below stay inside these ranges and needn't reach their ends.
Inputs may be any that keep to these rules, and one draw needn't show every extreme that they name: `lengths`: at least one sequence has all 512 positions valid.
All inputs are finite; a program needn't handle non-finite values.
Results may differ from the reference program's by a relative error of at most 0.014.
Values may be sent and summed in bfloat16 or wider, within the bound.
No kernel may reach another device: no remote copies, remote signals or barrier semaphores. Data moves between devices by JAX's collectives and lax.ppermute only.
A program may use at most 192 MiB of HBM per device.

```python
import jax
import jax.numpy as jnp
from jax import lax

D = 768
H = 12
HD = 64
FF = 3072
SEQ = 512
SEQS = 64
TOKENS = 32768


def draw_lengths(key, part):
    first_key, second_key = jax.random.split(jax.random.fold_in(key, 17))
    drawn = jax.random.randint(first_key, (SEQS,), SEQ // 4, SEQ + 1)
    chosen = jax.random.randint(second_key, (), 0, SEQS)
    return drawn.at[chosen].set(SEQ).astype(jnp.int32)


def levels(own_key, shape, cuts, least, largest):
    level = 1.0
    for axis_at, parts in cuts:
        steps = jax.random.uniform(jax.random.fold_in(jax.random.fold_in(own_key, 6), axis_at), (parts,), jnp.float32, least / len(cuts), largest / len(cuts))
        level = level * jnp.repeat(jnp.exp(steps), shape[axis_at] // parts).reshape((-1,) + (1,) * (len(shape) - 1 - axis_at))
    return level


def gaussian(own_key, extent, width, reach, cuts=(), kind=jnp.bfloat16):
    values = jax.random.normal(own_key, extent, jnp.float32) * width
    if len(cuts) > 0:
        values = levels(own_key, extent, cuts, -0.22, 0.18) * values
    return jnp.clip(values, min=-reach, max=reach).astype(kind)


def setup_inputs(seed: int = 0) -> dict:
    keys = jax.random.split(jax.random.key(seed), 19)
    tokens = gaussian(keys[0], (TOKENS, D), 1.0, 6.0, ((0, 32),))
    cotangent = gaussian(keys[1], (TOKENS, D), 1.0, 6.0, ((0, 32),))
    lengths = draw_lengths(jax.random.fold_in(keys[18], 71), 0)
    query_weight = gaussian(keys[3], (D, D), D ** -0.5, 0.21875, ((0, 16), (1, 2)))
    key_weight = gaussian(keys[4], (D, D), D ** -0.5, 0.21875, ((0, 16), (1, 2)))
    value_weight = gaussian(keys[5], (D, D), D ** -0.5, 0.21875, ((0, 16), (1, 2)))
    out_weight = gaussian(keys[6], (D, D), (D // 128) ** -0.5, 2.5, ((0, 2), (1, 16)))
    query_bias = gaussian(keys[7], (D,), 0.5, 3.0, ((0, 16),))
    value_bias = gaussian(keys[8], (D,), 0.05, 0.29882812, ((0, 16),))
    out_bias = gaussian(keys[9], (D,), 0.5, 3.0, ((0, 16),))
    first_gain = jnp.clip(1.0 + 0.1 * jax.random.normal(keys[10], (D,), jnp.float32), 0.5, 1.5).astype(jnp.bfloat16)
    first_shift = gaussian(keys[11], (D,), 0.3, 2.0, ((0, 16),))
    inner_weight = gaussian(keys[12], (D, FF), D ** -0.5, 0.21875, ((0, 16), (1, 2)))
    inner_bias = gaussian(keys[13], (FF,), 0.5, 3.0, ((0, 16),))
    outer_weight = gaussian(keys[14], (FF, D), FF ** -0.5, 0.109375, ((0, 2), (1, 16)))
    outer_bias = gaussian(keys[15], (D,), 0.3, 2.0, ((0, 16),))
    second_gain = jnp.clip(1.0 + 0.1 * jax.random.normal(keys[16], (D,), jnp.float32), 0.5, 1.5).astype(jnp.bfloat16)
    second_shift = gaussian(keys[17], (D,), 0.3, 2.0, ((0, 16),))
    return {"tokens": tokens, "cotangent": cotangent, "lengths": lengths, "query_weight": query_weight, "key_weight": key_weight, "value_weight": value_weight, "out_weight": out_weight, "query_bias": query_bias, "value_bias": value_bias, "out_bias": out_bias, "first_gain": first_gain, "first_shift": first_shift, "inner_weight": inner_weight, "inner_bias": inner_bias, "outer_weight": outer_weight, "outer_bias": outer_bias, "second_gain": second_gain, "second_shift": second_shift}


norm_eps = 1e-12
masked_score = -1000000000.0
group_seqs = 8

@jax.custom_vjp
def low(v):
    return lax.optimization_barrier(v.astype(jnp.bfloat16)).astype(jnp.float32)

@jax.custom_vjp
def low_back(v):
    return v

def low_keep(v):
    return (low(v), None)

def low_pass(kept, grad):
    return (grad,)

def back_keep(v):
    return (v, None)

def back_low(kept, grad):
    return (low(grad),)
low.defvjp(low_keep, low_pass)
low_back.defvjp(back_keep, back_low)

def matmul(left, right):
    return jnp.dot(left, right, precision=lax.Precision.HIGHEST)

def normalize(values, gain_vec, shift_vec):
    row_mean = lax.optimization_barrier(jnp.mean(values, axis=-1, keepdims=True))
    centred = values - row_mean
    row_var = lax.optimization_barrier(jnp.mean(centred * centred, axis=-1, keepdims=True))
    return centred * lax.rsqrt(row_var + norm_eps) * gain_vec + shift_vec

def attend_one(operands):
    query_seq, key_seq, value_seq, valid_seq = operands
    raw_scores = jnp.einsum('qhd,khd->hqk', query_seq, key_seq, precision=lax.Precision.HIGHEST) * HD ** (-0.5)
    raw_scores = low_back(raw_scores)
    scores = jnp.where(valid_seq[None, None, :], raw_scores, masked_score)
    top_score = lax.optimization_barrier(jnp.max(scores, axis=-1, keepdims=True))
    expo = jnp.exp(scores - top_score)
    probs = low(expo / lax.optimization_barrier(jnp.sum(expo, axis=-1, keepdims=True)))
    return jnp.einsum('hqk,khd->qhd', probs, value_seq, precision=lax.Precision.HIGHEST)

def forward(token_rows, params, valid_keys):
    query_weight, key_weight, value_weight, out_weight, query_bias, value_bias, out_bias, first_gain, first_shift, inner_weight, inner_bias, outer_weight, outer_bias, second_gain, second_shift = params
    row_total = token_rows.shape[0]
    seq_total = valid_keys.shape[0]
    seq_shape = (seq_total, row_total // seq_total, H, HD)
    query_rows = low(low_back(matmul(token_rows, query_weight) + query_bias))
    key_rows = low(low_back(matmul(token_rows, key_weight)))
    value_rows = low(low_back(matmul(token_rows, value_weight) + value_bias))
    context = lax.map(jax.checkpoint(attend_one), (query_rows.reshape(seq_shape), key_rows.reshape(seq_shape), value_rows.reshape(seq_shape), valid_keys))
    context = low(low_back(context.reshape(row_total, D)))
    branch = low_back(matmul(context, out_weight))
    hidden = low(normalize(token_rows + branch + out_bias, first_gain, first_shift))
    inner_pre = low_back(matmul(hidden, inner_weight) + inner_bias)
    active = low(jax.nn.gelu(inner_pre, approximate=False))
    feed_out = low_back(matmul(active, outer_weight))
    return normalize(hidden + feed_out + outer_bias, second_gain, second_shift)

def reference(tokens, cotangent, lengths, query_weight, key_weight, value_weight, out_weight, query_bias, value_bias, out_bias, first_gain, first_shift, inner_weight, inner_bias, outer_weight, outer_bias, second_gain, second_shift):
    params = tuple((item.astype(jnp.float32) for item in (query_weight, key_weight, value_weight, out_weight, query_bias, value_bias, out_bias, first_gain, first_shift, inner_weight, inner_bias, outer_weight, outer_bias, second_gain, second_shift)))
    groups = lengths.shape[0] // group_seqs
    token_blocks = tokens.astype(jnp.float32).reshape(groups, group_seqs * SEQ, D)
    grad_blocks = cotangent.astype(jnp.float32).reshape(groups, group_seqs * SEQ, D)
    length_blocks = lengths.reshape(groups, group_seqs)

    def scan_step(totals, block_data):
        token_block, grad_block, length_block = block_data
        valid_keys = jnp.arange(SEQ, dtype=jnp.int32)[None, :] < length_block[:, None]
        layer_block, pullback = jax.vjp(lambda rows, weights: forward(rows, weights, valid_keys), token_block, params)
        input_block, weight_grads = pullback(grad_block)
        totals = jax.tree.map(lambda first, second: first + second, totals, weight_grads)
        return (totals, (layer_block, input_block))
    zeros = jax.tree.map(jnp.zeros_like, params)
    totals, (layer_blocks, input_blocks) = lax.scan(scan_step, zeros, (token_blocks, grad_blocks, length_blocks))
    return (layer_blocks.reshape(-1, D), input_blocks.reshape(-1, D), totals[0], totals[1], totals[2], totals[3], totals[4], totals[5], totals[6], totals[7], totals[8], totals[9], totals[10], totals[11], totals[12], totals[13], totals[14])
```

```python
import jax
import jax.numpy as jnp
from jax import lax
from jax.experimental import pallas as pl
from jax.experimental.pallas import tpu as pltpu
from jax.sharding import PartitionSpec as P

HD = 64
norm_eps = 1e-12
masked_score = -1000000000.0
score_scale = HD ** (-0.5)
f32 = jnp.float32
bf16 = jnp.bfloat16
NT = (((1,), (1,)), ((), ()))
TN = (((0,), (0,)), ((), ()))
NN = (((1,), (0,)), ((), ()))


def dot(left, right, dims):
    return lax.dot_general(left, right, dims, preferred_element_type=f32)


def stage_orders(size):
    up = [1 << k for k in range(size.bit_length() - 1)]
    down = up[::-1]
    return (down, down[:-2] + [down[-1], down[-2]], [down[0]] + up[:-1])


def swap_dp(value, mask, size):
    return lax.ppermute(value, "dp", [(i, i ^ mask) for i in range(size)])


def swap_core(value):
    return lax.ppermute(value, "tensor", [(0, 1), (1, 0)])


def gather_rows(shard, order, size, index):
    rows, cols = shard.shape
    have = []
    buf = shard
    for mask in order:
        received = swap_dp(buf, mask, size)
        have = sorted(have + [mask], reverse=True)
        axis = have.index(mask)
        buf = jnp.where(
            (index & mask) != 0,
            jnp.stack([received, buf], axis),
            jnp.stack([buf, received], axis),
        )
    return buf.reshape(size * rows, cols)


def scatter_rows(own, order, size, index):
    total, cols = own.shape
    have = sorted(order, reverse=True)
    buf = own.reshape([2] * len(have) + [total // size, cols])
    for mask in order[::-1]:
        axis = have.index(mask)
        bit = ((index & mask) != 0).astype(jnp.int32)
        keep = lax.dynamic_index_in_dim(buf, bit, axis, keepdims=False)
        give = lax.dynamic_index_in_dim(buf, 1 - bit, axis, keepdims=False)
        received = swap_dp(give, mask, size)
        buf = keep.astype(f32) + received.astype(f32)
        have.remove(mask)
        if have:
            buf = buf.astype(own.dtype)
    return buf


def attend_forward_kernel(lens, q_ref, k_ref, v_ref, ctx_ref, lse_ref):
    seq_len, lanes = q_ref.shape
    lane = lax.broadcasted_iota(jnp.int32, (seq_len, lanes), 1)
    valid = lax.broadcasted_iota(jnp.int32, (seq_len, seq_len), 0) < lens[pl.program_id(0)]
    query = q_ref[...] * jnp.bfloat16(score_scale)
    keys = k_ref[...]
    value_t = v_ref[...].T
    pieces = []
    for h in range(lanes // HD):
        query_h = jnp.where(lane // HD == h, query, jnp.bfloat16(0))
        scores = jnp.where(valid, dot(keys, query_h, NT), masked_score)
        top = jnp.max(scores, axis=0, keepdims=True)
        expo = jnp.exp(scores - top)
        total = jnp.sum(expo, axis=0, keepdims=True)
        context_t = dot(value_t[h * HD : (h + 1) * HD], expo.astype(bf16), NN)
        pieces.append(context_t / total)
        lse_ref[0, 0, h : h + 1, :] = top + jnp.log(total)
    ctx_ref[...] = jnp.concatenate(pieces, 0).T.astype(bf16)


def attend_backward_kernel(lens, q_ref, k_ref, v_ref, d_ref, lse_ref, dq_ref, dk_ref, dv_ref):
    seq_len, lanes = q_ref.shape
    lane = lax.broadcasted_iota(jnp.int32, (seq_len, lanes), 1)
    valid = lax.broadcasted_iota(jnp.int32, (seq_len, seq_len), 0) < lens[pl.program_id(0)]
    query = q_ref[...] * jnp.bfloat16(score_scale)
    delta = d_ref[...]
    keys = k_ref[...]
    values = v_ref[...]
    keys_t = keys.T
    dq = []
    dk = jnp.zeros((seq_len, lanes), f32)
    dv = jnp.zeros((seq_len, lanes), f32)
    for h in range(lanes // HD):
        query_h = jnp.where(lane // HD == h, query, jnp.bfloat16(0))
        delta_h = jnp.where(lane // HD == h, delta, jnp.bfloat16(0))
        scores = jnp.where(valid, dot(keys, query_h, NT), masked_score)
        probs = jnp.exp(scores - lse_ref[0, 0, h : h + 1, :])
        prob_delta = dot(values, delta_h, NT)
        inner = jnp.sum(probs * prob_delta, axis=0, keepdims=True)
        score_delta = (probs * (prob_delta - inner)).astype(bf16)
        dv = dv + dot(probs.astype(bf16), delta_h, NN)
        dk = dk + dot(score_delta, query_h, NN)
        dq.append(dot(keys_t[h * HD : (h + 1) * HD], score_delta, NN))
    dq_ref[...] = (jnp.concatenate(dq, 0).T * score_scale).astype(bf16)
    dk_ref[...] = dk.astype(bf16)
    dv_ref[...] = dv.astype(bf16)


def attend_call(kernel, lens, operands, lse_in, n_out, lse_out, seq_count):
    rows, cols = operands[0].shape
    seq_len = rows // seq_count
    pairs = cols // (2 * HD)
    tile = pl.BlockSpec((seq_len, 2 * HD), lambda s, p, *_: (s, p))
    stat = pl.BlockSpec((1, 1, 2, seq_len), lambda s, p, *_: (s, p, 0, 0))
    stat_shape = jax.ShapeDtypeStruct((seq_count, pairs, 2, seq_len), f32)
    out = [jax.ShapeDtypeStruct((rows, cols), bf16)] * n_out
    return pl.pallas_call(
        kernel,
        out_shape=out + [stat_shape] * lse_out,
        grid_spec=pltpu.PrefetchScalarGridSpec(
            num_scalar_prefetch=1,
            grid=(seq_count, pairs),
            in_specs=[tile] * len(operands) + [stat] * len(lse_in),
            out_specs=[tile] * n_out + [stat] * lse_out,
        ),
        compiler_params=pltpu.CompilerParams(dimension_semantics=("arbitrary", "arbitrary")),
    )(lens, *operands, *lse_in)


def on_device(
    tokens,
    cotangent,
    lengths,
    query_weight,
    key_weight,
    value_weight,
    out_weight,
    query_bias,
    value_bias,
    out_bias,
    first_gain,
    first_shift,
    inner_weight,
    inner_bias,
    outer_weight,
    outer_bias,
    second_gain,
    second_shift,
):
    size = lax.axis_size("dp")
    index = lax.axis_index("dp")
    core = lax.axis_index("tensor")
    orders = stage_orders(size)
    seq_count = lengths.shape[0] // 2
    lens = lax.dynamic_slice_in_dim(lengths, core * seq_count, seq_count, 0)

    vectors = (
        query_bias,
        value_bias,
        out_bias,
        first_gain,
        first_shift,
        outer_bias,
        second_gain,
        second_shift,
        inner_bias,
    )
    own_vec = jnp.concatenate(vectors)[None, :]
    all_vec = gather_rows(own_vec, orders[0], size, index).astype(f32)
    bounds = [0]
    for item in vectors:
        bounds.append(bounds[-1] + item.shape[0])
    full_vec = [all_vec[:, a:b].reshape(-1) for a, b in zip(bounds[:-1], bounds[1:])]
    qb, vb, ob, g1, s1, ob2, g2, s2, ib = full_vec

    def sides(vector):
        half = vector.shape[0] // 2
        return (
            lax.dynamic_slice_in_dim(vector, core * half, half, 0),
            lax.dynamic_slice_in_dim(vector, (1 - core) * half, half, 0),
        )

    def fetch(shard, order):
        mine = gather_rows(shard, order, size, index)
        return (mine, swap_core(mine))

    wq = fetch(query_weight, orders[0])
    wk = fetch(key_weight, orders[1])
    wv = fetch(value_weight, orders[2])
    wo = fetch(out_weight.T, orders[2])
    wi = fetch(inner_weight, orders[0])
    wu = fetch(outer_weight.T, orders[1])
    qb = sides(qb)
    vb = sides(vb)
    ib = sides(ib)

    q, k, v, ctx, lse = [], [], [], [], []
    for t in range(2):
        q.append((dot(tokens, wq[t], NN) + qb[t]).astype(bf16))
        k.append(dot(tokens, wk[t], NN).astype(bf16))
        v.append((dot(tokens, wv[t], NN) + vb[t]).astype(bf16))
        c, l = attend_call(
            attend_forward_kernel, lens, (q[t], k[t], v[t]), (), 1, 1, seq_count
        )
        ctx.append(c)
        lse.append(l)
    first_in = tokens.astype(f32) + dot(ctx[0], wo[0], NT) + dot(ctx[1], wo[1], NT) + ob

    def center(values):
        mean = jnp.mean(values, axis=-1, keepdims=True)
        centred = values - mean
        var = jnp.mean(centred * centred, axis=-1, keepdims=True)
        rinv = lax.rsqrt(var + norm_eps)
        return centred * rinv, rinv

    def norm_back(grad, normed, rinv, gain):
        scaled = grad * gain
        return rinv * (
            scaled
            - jnp.mean(scaled, axis=-1, keepdims=True)
            - normed * jnp.mean(scaled * normed, axis=-1, keepdims=True)
        )

    n1, r1 = center(first_in)
    hidden = (n1 * g1 + s1).astype(bf16)
    act, slope = [], []
    feed = ob2
    for t in range(2):
        u = dot(hidden, wi[t], NN) + ib[t]
        cdf = 0.5 * (1.0 + lax.erf(u * (0.5**0.5)))
        act.append((u * cdf).astype(bf16))
        pdf = jnp.exp(-0.5 * u * u) * 0.3989422804014327
        slope.append((cdf + u * pdf).astype(bf16))
        feed = feed + dot(act[t], wu[t], NT)
    second_in = hidden.astype(f32) + feed
    n2, r2 = center(second_in)
    layer_out = n2 * g2 + s2
    cot = cotangent.astype(f32)
    second_delta = norm_back(cot, n2, r2, g2)
    grad_g2 = jnp.sum(cot * n2, axis=0)
    grad_s2 = jnp.sum(cot, axis=0)
    grad_ob2 = jnp.sum(second_delta, axis=0)
    feed_delta = second_delta.astype(bf16)
    gu = [dot(feed_delta, act[t], TN).astype(bf16) for t in range(2)]
    inner_delta = [
        (dot(feed_delta, wu[t], NN) * slope[t].astype(f32)).astype(bf16) for t in range(2)
    ]
    gi = [dot(hidden, inner_delta[t], TN).astype(bf16) for t in range(2)]
    grad_ib = [jnp.sum(inner_delta[t].astype(f32), axis=0) for t in range(2)]
    hidden_delta = (
        second_delta + dot(inner_delta[0], wi[0], NT) + dot(inner_delta[1], wi[1], NT)
    )
    first_delta = norm_back(hidden_delta, n1, r1, g1)
    grad_g1 = jnp.sum(hidden_delta * n1, axis=0)
    grad_s1 = jnp.sum(hidden_delta, axis=0)
    grad_ob = jnp.sum(first_delta, axis=0)
    branch_delta = first_delta.astype(bf16)
    go = [dot(branch_delta, ctx[t], TN).astype(bf16) for t in range(2)]
    dq, dk, dv = [], [], []
    for t in range(2):
        ctx_delta = dot(branch_delta, wo[t], NN).astype(bf16)
        a, b, c = attend_call(
            attend_backward_kernel, lens, (q[t], k[t], v[t], ctx_delta), (lse[t],), 3, 0, seq_count
        )
        dq.append(a)
        dk.append(b)
        dv.append(c)
    token_grad = first_delta
    for t in range(2):
        token_grad = (
            token_grad + dot(dq[t], wq[t], NT) + dot(dk[t], wk[t], NT) + dot(dv[t], wv[t], NT)
        )
    gq = [dot(tokens, dq[t], TN).astype(bf16) for t in range(2)]
    gk = [dot(tokens, dk[t], TN).astype(bf16) for t in range(2)]
    gv = [dot(tokens, dv[t], TN).astype(bf16) for t in range(2)]

    def reduce(pair, order):
        mine, other = pair
        summed = (mine.astype(f32) + swap_core(other).astype(f32)).astype(bf16)
        return scatter_rows(summed, order, size, index)

    out_gu = reduce(gu, orders[1]).T
    out_gi = reduce(gi, orders[0])
    out_go = reduce(go, orders[2]).T
    out_gq = reduce(gq, orders[0])
    out_gk = reduce(gk, orders[1])
    out_gv = reduce(gv, orders[2])

    def joined(pair):
        return jnp.where(
            core == 0, jnp.concatenate([pair[0], pair[1]]), jnp.concatenate([pair[1], pair[0]])
        )

    grad_qb = joined([jnp.sum(dq[t].astype(f32), axis=0) for t in range(2)])
    grad_vb = joined([jnp.sum(dv[t].astype(f32), axis=0) for t in range(2)])
    grads = (grad_qb, grad_vb, grad_ob, grad_g1, grad_s1, grad_ob2, grad_g2, grad_s2, joined(grad_ib))
    packed = jnp.concatenate([item.reshape(size, -1) for item in grads], axis=1)
    packed = packed + swap_core(packed)
    mine = scatter_rows(packed, orders[0], size, index).reshape(-1)
    vec_out = [mine[a:b] for a, b in zip(bounds[:-1], bounds[1:])]
    return (
        layer_out,
        token_grad,
        out_gq,
        out_gk,
        out_gv,
        out_go,
        vec_out[0],
        vec_out[1],
        vec_out[2],
        vec_out[3],
        vec_out[4],
        out_gi,
        vec_out[8],
        out_gu,
        vec_out[5],
        vec_out[6],
        vec_out[7],
    )


def solution(mesh):
    both = P(("dp", "tensor"), None)
    cols = P("dp", "tensor")
    rows = P("tensor", "dp")
    vec = P("dp")
    in_specs = (
        both, both, vec, cols, cols, cols, rows, vec, vec, vec, vec, vec, cols, vec, rows, vec, vec, vec,
    )
    out_specs = (
        both, both, cols, cols, cols, rows, vec, vec, vec, vec, vec, cols, vec, rows, vec, vec, vec,
    )
    return jax.shard_map(
        on_device, mesh=mesh, in_specs=in_specs, out_specs=out_specs, check_vma=False
    )
```

```python
import jax
import jax.numpy as jnp
from jax import lax
from jax.experimental import pallas as pl
from jax.experimental.pallas import tpu as pltpu
from jax.sharding import PartitionSpec as P

HD = 64
norm_eps = 1e-12
masked_score = -1000000000.0
score_scale = HD ** (-0.5)
f32 = jnp.float32
bf16 = jnp.bfloat16
NT = (((1,), (1,)), ((), ()))
TN = (((0,), (0,)), ((), ()))
NN = (((1,), (0,)), ((), ()))
ROWS = 256


def dot(left, right, dims):
    return lax.dot_general(left, right, dims, preferred_element_type=f32)


def stage_orders(size):
    up = [1 << k for k in range(size.bit_length() - 1)]
    down = up[::-1]
    return (down, down[:-2] + [down[-1], down[-2]], [down[0]] + up[:-1])


def swap_dp(value, mask, size):
    return lax.ppermute(value, "dp", [(i, i ^ mask) for i in range(size)])


def swap_core(value):
    return lax.ppermute(value, "tensor", [(0, 1), (1, 0)])


def after(value, *others):
    return lax.optimization_barrier((value, *others))[0]


def gather_rows(shard, order, size, index):
    rows, cols = shard.shape
    have = []
    buf = shard
    for mask in order:
        received = swap_dp(buf, mask, size)
        have = sorted(have + [mask], reverse=True)
        axis = have.index(mask)
        buf = jnp.where(
            (index & mask) != 0,
            jnp.stack([received, buf], axis),
            jnp.stack([buf, received], axis),
        )
    return buf.reshape(size * rows, cols)


def scatter_rows(own, order, size, index):
    total, cols = own.shape
    have = sorted(order, reverse=True)
    buf = own.reshape([2] * len(have) + [total // size, cols])
    for mask in order[::-1]:
        axis = have.index(mask)
        bit = ((index & mask) != 0).astype(jnp.int32)
        keep = lax.dynamic_index_in_dim(buf, bit, axis, keepdims=False)
        give = lax.dynamic_index_in_dim(buf, 1 - bit, axis, keepdims=False)
        received = swap_dp(give, mask, size)
        buf = keep.astype(f32) + received.astype(f32)
        have.remove(mask)
        if have:
            buf = buf.astype(own.dtype)
    return buf


def distance_of(piece, k):
    return (4 * (piece % 2) + 8 * k) ^ piece // 2


def vmem(shape):
    return pl.BlockSpec(shape, lambda *_: (0,) * len(shape))


def pack_first(weights, vectors):
    rows, cols = weights[0].shape
    count = len(weights)

    def kernel(*refs):
        ins, out_ref, table = refs[: count + len(vectors)], refs[-2], refs[-1]
        for g in range(count):
            out_ref[g * rows : (g + 1) * rows, :] = ins[g][...]
        table[...] = jnp.zeros(table.shape, f32)
        for i, ref in enumerate(ins[count:]):
            table[i : i + 1, : ref.shape[1]] = ref[...].astype(f32)
        out_ref[count * rows :, :] = table[...].astype(bf16)

    return pl.pallas_call(
        kernel,
        out_shape=jax.ShapeDtypeStruct((count * rows + 16, cols), bf16),
        scratch_shapes=[pltpu.VMEM((16, cols), f32)],
    )(*weights, *[item.reshape(1, -1) for item in vectors])


def place_first(pieces, index, count, size, lengths):
    total_rows, cols = pieces[0].shape[1:]
    rows = (total_rows - 16) // count

    def kernel(index_ref, *refs):
        ins = refs[: len(pieces)]
        w_ref, v_ref, last_ref, table = refs[len(pieces) :]
        for n, ref in enumerate(ins):
            for k in range(ref.shape[0]):
                block = index_ref[0] ^ distance_of(n, k)
                at = pl.ds(pl.multiple_of(block * rows, 16), rows)
                for g in range(count):
                    w_ref[g, at, :] = ref[k, g * rows : (g + 1) * rows, :]
                table[block] = ref[k, count * rows :, :].astype(f32)
        one, last = lengths
        for c in range(size):
            v_ref[:, c * one : (c + 1) * one] = table[c][:, :one]
            last_ref[:, c * last : (c + 1) * last] = table[c][8:9, :last]

    out = [(count, size * rows, cols), (16, size * lengths[0]), (1, size * lengths[1])]
    return pl.pallas_call(
        kernel,
        out_shape=[jax.ShapeDtypeStruct(o, d) for o, d in zip(out, (bf16, f32, f32))],
        grid_spec=pltpu.PrefetchScalarGridSpec(
            num_scalar_prefetch=1,
            grid=(1,),
            in_specs=[vmem(p.shape) for p in pieces],
            out_specs=[vmem(o) for o in out],
            scratch_shapes=[pltpu.VMEM((size, 16, cols), f32)],
        ),
    )(index[None], *pieces)


def place_cols(pieces, index, widths, size):
    rows = pieces[0].shape[1]

    def kernel(index_ref, *refs):
        ins, outs = refs[: len(pieces)], refs[len(pieces) :]
        for n, ref in enumerate(ins):
            for k in range(ref.shape[0]):
                block = index_ref[0] ^ distance_of(n, k)
                at = 0
                for out_ref, width in zip(outs, widths):
                    here = pl.ds(pl.multiple_of(block * rows, 16), rows)
                    out_ref[here, :] = ref[k, :, at : at + width]
                    at += width

    out = [(size * rows, w) for w in widths]
    return pl.pallas_call(
        kernel,
        out_shape=[jax.ShapeDtypeStruct(o, bf16) for o in out],
        grid_spec=pltpu.PrefetchScalarGridSpec(
            num_scalar_prefetch=1,
            grid=(1,),
            in_specs=[vmem(p.shape) for p in pieces],
            out_specs=[vmem(o) for o in out],
        ),
    )(index[None], *pieces)


PARTS = (
    ((3, (0, 1)), (1, (0, 1))),
    ((3, (2, 3)), (2, (2, 3))),
    ((1, (2, 3)),),
    ((2, (0, 1)),),
    ((0, (0, 1, 2, 3)),),
)


def split_out_specs(rows, step):
    return [
        pl.BlockSpec((sum(len(ks) for _, ks in part), rows, step), lambda i, *_: (0, 0, i))
        for part in PARTS
    ]


def split_shapes(rows, cols):
    return [
        jax.ShapeDtypeStruct(
            (sum(len(ks) for _, ks in part), rows, cols), bf16
        )
        for part in PARTS
    ]


def split_cols(pairs, index, size, step):
    total = pairs[0][0].shape[0]
    rows = total // size
    counts = [a.shape[1] // step for a, _ in pairs]
    starts = [sum(counts[:i]) for i in range(len(counts))]

    def kernel(index_ref, *refs):
        ins, outs = refs[: 2 * len(pairs)], refs[2 * len(pairs) :]
        for n, (first, count) in enumerate(zip(starts, counts)):

            @pl.when((pl.program_id(0) >= first) & (pl.program_id(0) < first + count))
            def _(n=n):
                for part, out_ref in zip(PARTS, outs):
                    at = 0
                    for offset, ks in part:
                        for k in ks:
                            block = index_ref[0] ^ (4 * k ^ offset)
                            here = pl.ds(pl.multiple_of(block * rows, 16), rows)
                            out_ref[at] = ins[2 * n][here, :] + ins[2 * n + 1][here, :]
                            at += 1

    specs = []
    for a, n in zip(starts, counts):
        spec = pl.BlockSpec((total, step), lambda i, *_, a=a, n=n: (0, jnp.clip(i - a, 0, n - 1)))
        specs += [spec, spec]
    return pl.pallas_call(
        kernel,
        out_shape=split_shapes(rows, sum(counts) * step),
        grid_spec=pltpu.PrefetchScalarGridSpec(
            num_scalar_prefetch=1,
            grid=(sum(counts),),
            in_specs=specs,
            out_specs=split_out_specs(rows, step),
        ),
    )(index[None], *[item for pair in pairs for item in pair])


def gradients_other(tokens_t, deltas):
    width, rows = tokens_t.shape
    count, _, cols = deltas.shape

    def kernel(t_ref, d_ref, o_ref, s_ref):
        o_ref[0] = dot(t_ref[...], d_ref[0], NN).astype(bf16)
        s_ref[0] = dot(jnp.ones((8, rows), bf16), d_ref[0], NN)

    return pl.pallas_call(
        kernel,
        out_shape=[
            jax.ShapeDtypeStruct((count, width, cols), bf16),
            jax.ShapeDtypeStruct((count, 8, cols), f32),
        ],
        grid=(count,),
        in_specs=[vmem(tokens_t.shape), pl.BlockSpec((1, rows, cols), lambda g: (g, 0, 0))],
        out_specs=[
            pl.BlockSpec((1, width, cols), lambda g: (g, 0, 0)),
            pl.BlockSpec((1, 8, cols), lambda g: (g, 0, 0)),
        ],
        cost_estimate=pl.CostEstimate(
            flops=2 * count * rows * width * cols, transcendentals=0, bytes_accessed=8 * rows * cols
        ),
    )(tokens_t, deltas)


def gradients_own(tokens_t, deltas, others, other_sums, table, index, core, size, one):
    width, rows = tokens_t.shape
    count, _, cols = deltas.shape
    part_rows = width // size
    height = count * part_rows + 16

    def kernel(at_ref, t_ref, d_ref, other_ref, sums_ref, table_ref, *refs):
        outs, total, own_sums, vec = refs[: len(PARTS)], refs[-3], refs[-2], refs[-1]
        g = pl.program_id(0)
        total[...] = dot(t_ref[...], d_ref[0], NN) + other_ref[0].astype(f32)
        own_sums[g] = dot(jnp.ones((8, rows), bf16), d_ref[0], NN)

        def blocks():
            for part, out_ref in zip(PARTS, outs):
                at = 0
                for offset, ks in part:
                    for k in ks:
                        yield at_ref[0] ^ (4 * k ^ offset), out_ref, at
                        at += 1

        for block, out_ref, at in blocks():
            value = total[pl.ds(pl.multiple_of(block * part_rows, 16), part_rows), :]
            out_ref[at, pl.ds(pl.multiple_of(g * part_rows, 16), part_rows), :] = value.astype(bf16)

        @pl.when(g == count - 1)
        def _():
            vec[...] = table_ref[...]
            for row, which in ((0, 0), (1, 2)):
                for ref, side in ((own_sums, 0), (sums_ref, 1)):
                    first = (at_ref[1] ^ side) * (size // 2)
                    for j in range(size // 2):
                        vec[first + j, row : row + 1, :one] = ref[which, 0:1, j * one : (j + 1) * one]
            for block, out_ref, at in blocks():
                out_ref[at, count * part_rows :, :] = vec[block].astype(bf16)

    return pl.pallas_call(
        kernel,
        out_shape=split_shapes(height, cols),
        grid_spec=pltpu.PrefetchScalarGridSpec(
            num_scalar_prefetch=1,
            grid=(count,),
            in_specs=[
                vmem(tokens_t.shape),
                pl.BlockSpec((1, rows, cols), lambda g, *_: (g, 0, 0)),
                pl.BlockSpec((1, width, cols), lambda g, *_: (g, 0, 0)),
                vmem(other_sums.shape),
                vmem(table.shape),
            ],
            out_specs=[vmem(shape.shape) for shape in split_shapes(height, cols)],
            scratch_shapes=[
                pltpu.VMEM((width, cols), f32),
                pltpu.VMEM((count, 8, cols), f32),
                pltpu.VMEM(table.shape, f32),
            ],
        ),
        cost_estimate=pl.CostEstimate(
            flops=2 * count * rows * width * cols, transcendentals=0, bytes_accessed=8 * rows * cols
        ),
    )(jnp.stack([index, core]), tokens_t, deltas, others, other_sums, table)


def pack_table(rows, last, size, cols):
    one = rows[0].shape[1] // size
    end = last.shape[1] // size

    def kernel(*refs):
        ins, out_ref, table = refs[: len(rows) + 1], refs[-2], refs[-1]
        table[...] = jnp.zeros(table.shape, f32)
        out_ref[...] = jnp.zeros(out_ref.shape, f32)
        for i, ref in enumerate(ins[:-1]):
            table[i + 2 : i + 3, :] = ref[...]
        for c in range(size):
            out_ref[c, :, :one] = table[:, c * one : (c + 1) * one]
            out_ref[c, 8:9, :end] = ins[-1][:, c * end : (c + 1) * end]

    return pl.pallas_call(
        kernel,
        out_shape=jax.ShapeDtypeStruct((size, 16, cols), f32),
        scratch_shapes=[pltpu.VMEM((16, rows[0].shape[1]), f32)],
    )(*rows, last)


def whole_call(kernel, outs, ins, blocks):
    return pl.pallas_call(
        kernel,
        out_shape=[jax.ShapeDtypeStruct(o, d) for o, d in outs],
        grid=(1,),
        in_specs=[vmem((n, *a.shape[1:])) for a, n in zip(ins, blocks)],
        out_specs=[vmem(o) for o, _ in outs],
    )(*ins)


def corner_back(parts, size):
    return swap_dp(parts[0], 1, size), swap_dp(parts[1], 2, size)


def corner_add(parts, got):
    keep = parts[2:4]

    def kernel(one_ref, two_ref, r1_ref, r2_ref, o1_ref, o2_ref):
        o1_ref[...] = one_ref[...] + r2_ref[...]
        o2_ref[...] = two_ref[...] + r1_ref[...]

    return whole_call(
        kernel, [(item.shape, bf16) for item in keep], [*keep, *got], (2, 2, 2, 2)
    )


def near_back(sums, size):
    return swap_dp(sums[0], 1, size), swap_dp(sums[1], 2, size)


def near_add(own, first, got):
    def kernel(own_ref, f1_ref, f2_ref, r1_ref, r2_ref, keep_ref, *outs):
        def total(k):
            early = f1_ref[2 + k] if k < 2 else f2_ref[k]
            late = r2_ref[k] if k < 2 else r1_ref[k - 2]
            return own_ref[k].astype(f32) + early.astype(f32) + late.astype(f32)

        keep_ref[...] = total(0)
        for k in (1, 2, 3):
            outs[k - 1][...] = total(k).astype(bf16)

    shape = own.shape[1:]
    return whole_call(
        kernel, [(shape, f32)] + [(shape, bf16)] * 3, [own, *first, *got], (4, 4, 4, 2, 2)
    )


def far_back(sums, size):
    return [swap_dp(item, 4 * (k + 1), size) for k, item in enumerate(sums[1:])]


def project(tokens, weights, vectors, core, side):
    rows, width = tokens.shape
    cols = weights.shape[2]

    def kernel(core_ref, x_ref, w_ref, v_ref, q_out, k_out, v_out):
        half = core_ref[0] ^ side
        bias = jnp.where(half == 0, v_ref[0:8, :cols], v_ref[0:8, cols:])
        x = x_ref[...]
        q_out[...] = (dot(x, w_ref[0], NN) + bias[0:1]).astype(bf16)
        k_out[...] = dot(x, w_ref[1], NN).astype(bf16)
        v_out[...] = (dot(x, w_ref[2], NN) + bias[1:2]).astype(bf16)

    tile = pl.BlockSpec((ROWS, cols), lambda i, *_: (i, 0))
    return pl.pallas_call(
        kernel,
        out_shape=[jax.ShapeDtypeStruct((rows, cols), bf16)] * 3,
        grid_spec=pltpu.PrefetchScalarGridSpec(
            num_scalar_prefetch=1,
            grid=(rows // ROWS,),
            in_specs=[
                pl.BlockSpec((ROWS, width), lambda i, *_: (i, 0)),
                vmem(weights.shape),
                vmem(vectors.shape),
            ],
            out_specs=[tile] * 3,
        ),
        cost_estimate=pl.CostEstimate(
            flops=6 * rows * width * cols, transcendentals=0, bytes_accessed=8 * rows * cols
        ),
    )(core[None], tokens, weights, vectors)


def token_gradient(first_delta, deltas, weights, part, parts):
    count, rows, cols = deltas[0].shape
    width = weights[0].shape[1]
    steps = rows // ROWS // parts

    def kernel(f_ref, d0_ref, d1_ref, w0_ref, w1_ref, *refs):
        o_ref = refs[-1]
        total = f_ref[...]
        for d_ref, w_ref in ((d0_ref, w0_ref), (d1_ref, w1_ref)):
            for g in range(count):
                total = total + dot(d_ref[g], w_ref[g], NT)
        o_ref[...] = total

    tile = pl.BlockSpec((ROWS, width), lambda i: (i + part * steps, 0))
    delta_part = pl.BlockSpec((count, ROWS, cols), lambda i: (0, i + part * steps, 0))
    return pl.pallas_call(
        kernel,
        out_shape=jax.ShapeDtypeStruct((rows, width), f32),
        grid=(steps,),
        in_specs=[tile, delta_part, delta_part] + [vmem(weights[0].shape)] * 2,
        out_specs=tile,
        input_output_aliases={0: 0},
        cost_estimate=pl.CostEstimate(
            flops=4 * count * rows * width * cols // parts,
            transcendentals=0,
            bytes_accessed=8 * rows * cols // parts,
        ),
    )(first_delta, *deltas, *weights)


def attend_forward_kernel(lens, q_ref, k_ref, v_ref, ctx_ref, lse_ref):
    seq_len, lanes = q_ref.shape
    lane = lax.broadcasted_iota(jnp.int32, (seq_len, lanes), 1)
    valid = lax.broadcasted_iota(jnp.int32, (seq_len, seq_len), 0) < lens[pl.program_id(0)]
    query = q_ref[...] * jnp.bfloat16(score_scale)
    keys = k_ref[...]
    value_t = v_ref[...].T
    pieces = []
    for h in range(lanes // HD):
        query_h = jnp.where(lane // HD == h, query, jnp.bfloat16(0))
        scores = jnp.where(valid, dot(keys, query_h, NT), masked_score)
        top = jnp.max(scores, axis=0, keepdims=True)
        expo = jnp.exp(scores - top)
        total = jnp.sum(expo, axis=0, keepdims=True)
        context_t = dot(value_t[h * HD : (h + 1) * HD], expo.astype(bf16), NN)
        pieces.append(context_t / total)
        lse_ref[0, 0, h : h + 1, :] = top + jnp.log(total)
    ctx_ref[...] = jnp.concatenate(pieces, 0).T.astype(bf16)


def attend_backward_kernel(lens, q_ref, k_ref, v_ref, d_ref, lse_ref, out_ref):
    seq_len, lanes = q_ref.shape
    lane = lax.broadcasted_iota(jnp.int32, (seq_len, lanes), 1)
    valid = lax.broadcasted_iota(jnp.int32, (seq_len, seq_len), 0) < lens[pl.program_id(0)]
    query = q_ref[...] * jnp.bfloat16(score_scale)
    delta = d_ref[...]
    keys = k_ref[...]
    values = v_ref[...]
    keys_t = keys.T
    dq = []
    dk = jnp.zeros((seq_len, lanes), f32)
    dv = jnp.zeros((seq_len, lanes), f32)
    for h in range(lanes // HD):
        query_h = jnp.where(lane // HD == h, query, jnp.bfloat16(0))
        delta_h = jnp.where(lane // HD == h, delta, jnp.bfloat16(0))
        scores = jnp.where(valid, dot(keys, query_h, NT), masked_score)
        probs = jnp.exp(scores - lse_ref[0, 0, h : h + 1, :])
        prob_delta = dot(values, delta_h, NT)
        inner = jnp.sum(probs * prob_delta, axis=0, keepdims=True)
        score_delta = (probs * (prob_delta - inner)).astype(bf16)
        dv = dv + dot(probs.astype(bf16), delta_h, NN)
        dk = dk + dot(score_delta, query_h, NN)
        dq.append(dot(keys_t[h * HD : (h + 1) * HD], score_delta, NN))
    out_ref[0] = (jnp.concatenate(dq, 0).T * score_scale).astype(bf16)
    out_ref[1] = dk.astype(bf16)
    out_ref[2] = dv.astype(bf16)


def attend_call(kernel, lens, operands, lse_in, seq_count):
    rows, cols = operands[0].shape
    seq_len = rows // seq_count
    pairs = cols // (2 * HD)
    tile = pl.BlockSpec((seq_len, 2 * HD), lambda s, p, *_: (s, p))
    stat = pl.BlockSpec((1, 1, 2, seq_len), lambda s, p, *_: (s, p, 0, 0))
    if lse_in:
        out_shape = jax.ShapeDtypeStruct((3, rows, cols), bf16)
        out_specs = pl.BlockSpec((3, seq_len, 2 * HD), lambda s, p, *_: (0, s, p))
    else:
        out_shape = [
            jax.ShapeDtypeStruct((rows, cols), bf16),
            jax.ShapeDtypeStruct((seq_count, pairs, 2, seq_len), f32),
        ]
        out_specs = [tile, stat]
    cells = rows * seq_len * cols // HD
    return pl.pallas_call(
        kernel,
        out_shape=out_shape,
        grid_spec=pltpu.PrefetchScalarGridSpec(
            num_scalar_prefetch=1,
            grid=(seq_count, pairs),
            in_specs=[tile] * len(operands) + [stat] * len(lse_in),
            out_specs=out_specs,
        ),
        cost_estimate=pl.CostEstimate(
            flops=cells * HD * (40 if lse_in else 30),
            transcendentals=cells,
            bytes_accessed=8 * rows * cols,
        ),
    )(lens, *operands, *lse_in)


def on_device(
    tokens,
    cotangent,
    lengths,
    query_weight,
    key_weight,
    value_weight,
    out_weight,
    query_bias,
    value_bias,
    out_bias,
    first_gain,
    first_shift,
    inner_weight,
    inner_bias,
    outer_weight,
    outer_bias,
    second_gain,
    second_shift,
):
    size = lax.axis_size("dp")
    index = lax.axis_index("dp")
    core = lax.axis_index("tensor")
    orders = stage_orders(size)
    seq_count = lengths.shape[0] // 2
    lens = lax.dynamic_slice_in_dim(lengths, core * seq_count, seq_count, 0)
    fast = size == 16 and query_weight.shape[0] % 16 == 0
    half = query_weight.shape[1]
    step = half

    vectors = (
        query_bias,
        value_bias,
        out_bias,
        first_gain,
        first_shift,
        outer_bias,
        second_gain,
        second_shift,
        inner_bias,
    )
    bounds = [0]
    for item in vectors:
        bounds.append(bounds[-1] + item.shape[0])
    projections = (query_weight, key_weight, value_weight)
    out_t = out_weight.T
    outer_t = outer_weight.T

    if fast:
        shard = pack_first(projections, vectors)
        far = [swap_dp(shard, d, size) for d in (8, 4, 12)]
        low, high = jnp.stack([shard, far[0]]), jnp.stack(far[1:])
        two_low, one_high = swap_dp(low, 2, size), swap_dp(high, 1, size)
        one_low, two_high = swap_dp(low, 1, size), swap_dp(high, 2, size)
        shard_a = jnp.concatenate([out_t, inner_weight], 1)
        far_a = swap_dp(after(shard_a, low, high), 8, size)
        tokens_t = tokens.T
        pieces = [low, high, one_low, one_high, two_low, two_high]
        pieces += [swap_dp(two_low, 1, size), swap_dp(one_high, 2, size)]
        far_a, *pieces, tokens_t = lax.optimization_barrier((far_a, *pieces, tokens_t))
        low_a = jnp.stack([shard_a, far_a])
        high_a = swap_dp(low_a, 4, size)
        two_low_a, one_low_a = swap_dp(low_a, 2, size), swap_dp(low_a, 1, size)
        wqkv0, vecs, ib = place_first(
            pieces, index, 3, size, (query_bias.shape[0], inner_bias.shape[0])
        )
    else:
        own_vec = jnp.concatenate(vectors)[None, :]
        all_vec = gather_rows(own_vec, orders[0], size, index).astype(f32)
        found = [all_vec[:, a:b].reshape(1, -1) for a, b in zip(bounds[:-1], bounds[1:])]
        vecs = jnp.concatenate(found[:-1] + [jnp.zeros_like(found[0])] * 8, 0)
        ib = found[-1]
        wqkv0 = jnp.stack(
            [gather_rows(w, o, size, index) for w, o in zip(projections, orders)]
        )
        wo0 = gather_rows(out_t, orders[2], size, index)
        wi0 = gather_rows(inner_weight, orders[0], size, index)
        wu0 = gather_rows(outer_t, orders[1], size, index)

    wqkv = (wqkv0, swap_core(wqkv0))
    ob, g1, s1, ob2, g2, s2 = [vecs[i : i + 1] for i in range(2, 8)]
    hidden_half = inner_weight.shape[1]
    ib = (
        jnp.where(core == 0, ib[:, :hidden_half], ib[:, hidden_half:]),
        jnp.where(core == 0, ib[:, hidden_half:], ib[:, :hidden_half]),
    )

    q, k, v, ctx, lse = [], [], [], [], []
    for t in range(2):
        found = project(tokens, wqkv[t], vecs, core, t)
        if fast and t == 0:
            high_a, other, *found = lax.optimization_barrier((high_a, wqkv[1], *found))
            wqkv = (wqkv[0], other)
            one_high_a, two_high_a = swap_dp(high_a, 1, size), swap_dp(high_a, 2, size)
            far_b = swap_dp(after(outer_t, other), 8, size)
        q.append(found[0])
        k.append(found[1])
        v.append(found[2])
    if fast:
        q[0], q[1] = lax.optimization_barrier((q[0], q[1]))
    for t in range(2):
        if fast and t == 1:
            q[1] = after(q[1], ctx[0])
        c, s = attend_call(attend_forward_kernel, lens, (q[t], k[t], v[t]), (), seq_count)
        lse.append(s)
        if fast and t == 0:
            pieces_a = [low_a, high_a, one_low_a, one_high_a, two_low_a, two_high_a]
            *pieces_a, far_b, c = lax.optimization_barrier((*pieces_a, far_b, c))
            pieces_a += [swap_dp(pieces_a[4], 1, size), swap_dp(pieces_a[3], 2, size)]
            low_b = jnp.stack([outer_t, far_b])
            high_b = swap_dp(low_b, 4, size)
            two_low_b, one_low_b = swap_dp(low_b, 2, size), swap_dp(low_b, 1, size)
        if fast and t == 1:
            *pieces_a, high_b, two_low_b, one_low_b, c = lax.optimization_barrier(
                (*pieces_a, high_b, two_low_b, one_low_b, c)
            )
            one_high_b, two_high_b = swap_dp(high_b, 1, size), swap_dp(high_b, 2, size)
            last_low_b = swap_dp(two_low_b, 1, size)
            wo0, wi0 = place_cols(pieces_a, index, (half, inner_weight.shape[1]), size)
        ctx.append(c)

    wo = (wo0, swap_core(wo0))
    wi = (wi0, swap_core(wi0))
    first_in = tokens.astype(f32) + dot(ctx[0], wo[0], NT) + dot(ctx[1], wo[1], NT) + ob

    def center(values):
        mean = jnp.mean(values, axis=-1, keepdims=True)
        centred = values - mean
        var = jnp.mean(centred * centred, axis=-1, keepdims=True)
        rinv = lax.rsqrt(var + norm_eps)
        return centred * rinv, rinv

    def norm_back(grad, normed, rinv, gain):
        scaled = grad * gain
        return rinv * (
            scaled
            - jnp.mean(scaled, axis=-1, keepdims=True)
            - normed * jnp.mean(scaled * normed, axis=-1, keepdims=True)
        )

    n1, r1 = center(first_in)
    hidden = (n1 * g1 + s1).astype(bf16)
    if fast:
        *pieces_b, hidden = lax.optimization_barrier(
            (low_b, high_b, one_low_b, one_high_b, two_low_b, two_high_b, last_low_b, hidden)
        )
        pieces_b.append(swap_dp(pieces_b[3], 2, size))
    else:
        wu = (wu0, swap_core(wu0))
    act, slope = [], []
    feed = ob2
    for t in range(2):
        u = dot(hidden, wi[t], NN) + ib[t]
        cdf = 0.5 * (1.0 + lax.erf(u * (0.5**0.5)))
        act.append((u * cdf).astype(bf16))
        pdf = jnp.exp(-0.5 * u * u) * 0.3989422804014327
        slope.append((cdf + u * pdf).astype(bf16))
        if fast and t == 0:
            *pieces_b, act[0] = lax.optimization_barrier((*pieces_b, act[0]))
            (wu0,) = place_cols(pieces_b, index, (inner_weight.shape[1],), size)
            wu = (wu0, swap_core(wu0))
            hidden = after(hidden, wu0)
        feed = feed + dot(act[t], wu[t], NT)
    second_in = hidden.astype(f32) + feed
    n2, r2 = center(second_in)
    layer_out = n2 * g2 + s2
    cot = cotangent.astype(f32)
    second_delta = norm_back(cot, n2, r2, g2)
    grad_g2 = jnp.sum(cot * n2, axis=0, keepdims=True)
    grad_s2 = jnp.sum(cot, axis=0, keepdims=True)
    grad_ob2 = jnp.sum(second_delta, axis=0, keepdims=True)
    feed_delta = second_delta.astype(bf16)

    def product(left, right):
        other = dot(left, right[1], TN).astype(bf16)
        other = swap_core(other)
        return dot(left, right[0], TN).astype(bf16), other

    gu = product(feed_delta, act)
    feed_delta, *gu = lax.optimization_barrier((feed_delta, *gu))
    inner_delta = [None, None]
    for t in (1, 0):
        inner_delta[t] = (dot(feed_delta, wu[t], NN) * slope[t].astype(f32)).astype(bf16)
        if fast and t == 1:
            parts_u = split_cols([gu], index, size, 2 * step)
            first_u = corner_back(parts_u, size)
            feed_delta = after(feed_delta, inner_delta[1], parts_u[4])
    gi = product(hidden, inner_delta)
    inner_delta[0], inner_delta[1], *gi = lax.optimization_barrier((*inner_delta, *gi))
    grad_ib = [jnp.sum(inner_delta[t].astype(f32), axis=0, keepdims=True) for t in range(2)]
    if fast:
        *first_u, _ = lax.optimization_barrier((*first_u, gi[0]))
        sums_u = corner_add(parts_u, first_u)
        got_u = near_back(sums_u, size)
        inner_delta[0], inner_delta[1] = [after(d, sums_u[0]) for d in inner_delta]
    hidden_delta = (
        second_delta + dot(inner_delta[0], wi[0], NT) + dot(inner_delta[1], wi[1], NT)
    )
    first_delta = norm_back(hidden_delta, n1, r1, g1)
    grad_g1 = jnp.sum(hidden_delta * n1, axis=0, keepdims=True)
    grad_s1 = jnp.sum(hidden_delta, axis=0, keepdims=True)
    grad_ob = jnp.sum(first_delta, axis=0, keepdims=True)
    branch_delta = first_delta.astype(bf16)
    if fast:
        *got_u, branch_delta = lax.optimization_barrier((*got_u, branch_delta))
        last_u = near_add(parts_u[4], first_u, got_u)
        branch_delta = after(branch_delta, last_u[0])
        got_u = far_back(last_u, size)
    go = product(branch_delta, ctx)
    ctx_delta = [dot(branch_delta, wo[t], NN).astype(bf16) for t in range(2)]

    def joined(pair):
        return jnp.where(
            core == 0, jnp.concatenate(pair, 1), jnp.concatenate(pair[::-1], 1)
        )

    grads = [grad_ob, grad_g1, grad_s1, grad_ob2, grad_g2, grad_s2, joined(grad_ib)]
    if fast:
        table = pack_table(grads[:-1], grads[-1], size, half)
        parts_i = split_cols([gi, go], index, size, step)
        first_i = corner_back(parts_i, size)
        ctx_delta[1] = after(ctx_delta[1], parts_i[4], table)

    def attend_back(t):
        return attend_call(
            attend_backward_kernel, lens, (q[t], k[t], v[t], ctx_delta[t]), (lse[t],), seq_count
        )

    deltas = [None, None]
    deltas[1] = attend_back(1)
    if fast:
        arrived = lax.optimization_barrier((*first_i, *got_u, deltas[1]))
        first_i, got_u, deltas[1] = arrived[:2], arrived[2:5], arrived[5]
        sums_i = corner_add(parts_i, first_i)
        got_i = near_back(sums_i, size)
        deltas[1] = after(deltas[1], sums_i[0])
        others, other_sums = gradients_other(tokens_t, deltas[1])
        *got_i, others = lax.optimization_barrier((*got_i, others))
        last_i = near_add(parts_i[4], first_i, got_i)
        others = swap_core(others)
        got_i = far_back(last_i, size)
        ctx_delta[0] = after(ctx_delta[0], last_i[0])
        deltas[0] = attend_back(0)
        *got_i, deltas[0] = lax.optimization_barrier((*got_i, deltas[0]))
        parts_q = gradients_own(
            tokens_t,
            deltas[0],
            others,
            other_sums,
            table,
            index,
            core,
            size,
            query_bias.shape[0],
        )
        first_q = corner_back(parts_q, size)
        token_grad = token_gradient(
            after(first_delta, parts_q[4]), [after(d, parts_q[4]) for d in deltas], wqkv, 0, 2
        )
        *first_q, token_grad = lax.optimization_barrier((*first_q, token_grad))

        def total(last, got):
            return last[0] + got[0].astype(f32) + got[1].astype(f32) + got[2].astype(f32)

        out_gu = total(last_u, got_u).T
        out_gi = total(last_i, got_i)
        hidden_half = out_gi.shape[1] - half
        out_go = out_gi[:, hidden_half:].T
        out_gi = out_gi[:, :hidden_half]
        sums_q = corner_add(parts_q, first_q)
        got_q = near_back(sums_q, size)
        last_q = near_add(parts_q[4], first_q, got_q)
        got_q = far_back(last_q, size)
        token_grad = token_gradient(token_grad, [after(d, last_q[0]) for d in deltas], wqkv, 1, 2)
        out_q = total(last_q, got_q)
        n = query_weight.shape[0]
        out_qkv = [out_q[g * n : (g + 1) * n] for g in range(3)]
        vec = out_q[3 * n :]
        vec = vec + swap_core(vec)
        vec_out = [vec[i, : item.shape[0]] for i, item in enumerate(vectors)]
    else:
        deltas[0] = attend_back(0)
        token_grad = token_gradient(first_delta, deltas, wqkv, 0, 1)

        def reduce(pair, order):
            summed = (pair[0].astype(f32) + pair[1].astype(f32)).astype(bf16)
            return scatter_rows(summed, order, size, index)

        out_gu = reduce(gu, orders[1]).T
        out_gi = reduce(gi, orders[0])
        out_go = reduce(go, orders[2]).T
        out_qkv = [
            reduce(product(tokens, [d[g] for d in deltas]), order) for g, order in enumerate(orders)
        ]
        bias_grads = [
            joined([jnp.sum(d[g].astype(f32), axis=0, keepdims=True) for d in deltas]) for g in (0, 2)
        ]
        packed = jnp.concatenate([item.reshape(size, -1) for item in bias_grads + grads], axis=1)
        packed = packed + swap_core(packed)
        own = scatter_rows(packed, orders[0], size, index).reshape(-1)
        vec_out = [own[a:b] for a, b in zip(bounds[:-1], bounds[1:])]
    return (
        layer_out,
        token_grad,
        out_qkv[0],
        out_qkv[1],
        out_qkv[2],
        out_go,
        vec_out[0],
        vec_out[1],
        vec_out[2],
        vec_out[3],
        vec_out[4],
        out_gi,
        vec_out[8],
        out_gu,
        vec_out[5],
        vec_out[6],
        vec_out[7],
    )


def solution(mesh):
    both = P(("dp", "tensor"), None)
    cols = P("dp", "tensor")
    rows = P("tensor", "dp")
    vec = P("dp")
    in_specs = (
        both, both, vec, cols, cols, cols, rows, vec, vec, vec, vec, vec, cols, vec, rows, vec, vec, vec,
    )
    out_specs = (
        both, both, cols, cols, cols, rows, vec, vec, vec, vec, vec, cols, vec, rows, vec, vec, vec,
    )
    return jax.shard_map(
        on_device, mesh=mesh, in_specs=in_specs, out_specs=out_specs, check_vma=False
    )
```

```python
import jax
import jax.numpy as jnp
from jax import lax
from jax.experimental import pallas as pl
from jax.experimental.pallas import tpu as pltpu
from jax.sharding import PartitionSpec as P

HD = 64
norm_eps = 1e-12
masked_score = -1000000000.0
score_scale = HD ** (-0.5)
f32 = jnp.float32
bf16 = jnp.bfloat16
NT = (((1,), (1,)), ((), ()))
TN = (((0,), (0,)), ((), ()))
NN = (((1,), (0,)), ((), ()))
ROWS = 256


def dot(left, right, dims):
    return lax.dot_general(left, right, dims, preferred_element_type=f32)


def stage_orders(size):
    up = [1 << k for k in range(size.bit_length() - 1)]
    down = up[::-1]
    return (down, down[:-2] + [down[-1], down[-2]], [down[0]] + up[:-1])


def swap_dp(value, mask, size):
    return lax.ppermute(value, "dp", [(i, i ^ mask) for i in range(size)])


def swap_core(value):
    return lax.ppermute(value, "tensor", [(0, 1), (1, 0)])


def after(value, *others):
    return lax.optimization_barrier((value, *others))[0]


def gather_rows(shard, order, size, index):
    rows, cols = shard.shape
    have = []
    buf = shard
    for mask in order:
        received = swap_dp(buf, mask, size)
        have = sorted(have + [mask], reverse=True)
        axis = have.index(mask)
        buf = jnp.where(
            (index & mask) != 0,
            jnp.stack([received, buf], axis),
            jnp.stack([buf, received], axis),
        )
    return buf.reshape(size * rows, cols)


def scatter_rows(own, order, size, index):
    total, cols = own.shape
    have = sorted(order, reverse=True)
    buf = own.reshape([2] * len(have) + [total // size, cols])
    for mask in order[::-1]:
        axis = have.index(mask)
        bit = ((index & mask) != 0).astype(jnp.int32)
        keep = lax.dynamic_index_in_dim(buf, bit, axis, keepdims=False)
        give = lax.dynamic_index_in_dim(buf, 1 - bit, axis, keepdims=False)
        received = swap_dp(give, mask, size)
        buf = keep.astype(f32) + received.astype(f32)
        have.remove(mask)
        if have:
            buf = buf.astype(own.dtype)
    return buf


def distance_of(piece, k):
    return (4 * (piece % 2) + 8 * k) ^ piece // 2


def vmem(shape):
    return pl.BlockSpec(shape, lambda *_: (0,) * len(shape))


def pack_first(weights, vectors):
    rows, cols = weights[0].shape
    count = len(weights)

    def kernel(*refs):
        ins, out_ref, table = refs[: count + len(vectors)], refs[-2], refs[-1]
        for g in range(count):
            out_ref[g * rows : (g + 1) * rows, :] = ins[g][...]
        table[...] = jnp.zeros(table.shape, f32)
        for i, ref in enumerate(ins[count:]):
            table[i : i + 1, : ref.shape[1]] = ref[...].astype(f32)
        out_ref[count * rows :, :] = table[...].astype(bf16)

    return pl.pallas_call(
        kernel,
        out_shape=jax.ShapeDtypeStruct((count * rows + 16, cols), bf16),
        scratch_shapes=[pltpu.VMEM((16, cols), f32)],
    )(*weights, *[item.reshape(1, -1) for item in vectors])


def place_first(pieces, index, count, size, lengths):
    total_rows, cols = pieces[0].shape[1:]
    rows = (total_rows - 16) // count

    def kernel(index_ref, *refs):
        ins = refs[: len(pieces)]
        w_ref, v_ref, last_ref, table = refs[len(pieces) :]
        for n, ref in enumerate(ins):
            for k in range(ref.shape[0]):
                block = index_ref[0] ^ distance_of(n, k)
                at = pl.ds(pl.multiple_of(block * rows, 16), rows)
                for g in range(count):
                    w_ref[g, at, :] = ref[k, g * rows : (g + 1) * rows, :]
                table[block] = ref[k, count * rows :, :].astype(f32)
        one, last = lengths
        for c in range(size):
            v_ref[:, c * one : (c + 1) * one] = table[c][:, :one]
            last_ref[:, c * last : (c + 1) * last] = table[c][8:9, :last]

    out = [(count, size * rows, cols), (16, size * lengths[0]), (1, size * lengths[1])]
    return pl.pallas_call(
        kernel,
        out_shape=[jax.ShapeDtypeStruct(o, d) for o, d in zip(out, (bf16, f32, f32))],
        grid_spec=pltpu.PrefetchScalarGridSpec(
            num_scalar_prefetch=1,
            grid=(1,),
            in_specs=[vmem(p.shape) for p in pieces],
            out_specs=[vmem(o) for o in out],
            scratch_shapes=[pltpu.VMEM((size, 16, cols), f32)],
        ),
    )(index[None], *pieces)


def place_cols(pieces, index, widths, size):
    rows = pieces[0].shape[1]

    def kernel(index_ref, *refs):
        ins, outs = refs[: len(pieces)], refs[len(pieces) :]
        for n, ref in enumerate(ins):
            for k in range(ref.shape[0]):
                block = index_ref[0] ^ distance_of(n, k)
                at = 0
                for out_ref, width in zip(outs, widths):
                    here = pl.ds(pl.multiple_of(block * rows, 16), rows)
                    out_ref[here, :] = ref[k, :, at : at + width]
                    at += width

    out = [(size * rows, w) for w in widths]
    return pl.pallas_call(
        kernel,
        out_shape=[jax.ShapeDtypeStruct(o, bf16) for o in out],
        grid_spec=pltpu.PrefetchScalarGridSpec(
            num_scalar_prefetch=1,
            grid=(1,),
            in_specs=[vmem(p.shape) for p in pieces],
            out_specs=[vmem(o) for o in out],
        ),
    )(index[None], *pieces)


PARTS = (
    ((3, (0, 1)), (1, (0, 1))),
    ((3, (2, 3)), (2, (2, 3))),
    ((1, (2, 3)),),
    ((2, (0, 1)),),
    ((0, (0, 1, 2, 3)),),
)


def split_out_specs(rows, step):
    return [
        pl.BlockSpec((sum(len(ks) for _, ks in part), rows, step), lambda i, *_: (0, 0, i))
        for part in PARTS
    ]


def split_shapes(rows, cols):
    return [
        jax.ShapeDtypeStruct(
            (sum(len(ks) for _, ks in part), rows, cols), bf16
        )
        for part in PARTS
    ]


def split_cols(pairs, index, size, step):
    total = pairs[0][0].shape[0]
    rows = total // size
    counts = [a.shape[1] // step for a, _ in pairs]
    starts = [sum(counts[:i]) for i in range(len(counts))]

    def kernel(index_ref, *refs):
        ins, outs = refs[: 2 * len(pairs)], refs[2 * len(pairs) :]
        for n, (first, count) in enumerate(zip(starts, counts)):

            @pl.when((pl.program_id(0) >= first) & (pl.program_id(0) < first + count))
            def _(n=n):
                for part, out_ref in zip(PARTS, outs):
                    at = 0
                    for offset, ks in part:
                        for k in ks:
                            block = index_ref[0] ^ (4 * k ^ offset)
                            here = pl.ds(pl.multiple_of(block * rows, 16), rows)
                            out_ref[at] = ins[2 * n][here, :] + ins[2 * n + 1][here, :]
                            at += 1

    specs = []
    for a, n in zip(starts, counts):
        spec = pl.BlockSpec((total, step), lambda i, *_, a=a, n=n: (0, jnp.clip(i - a, 0, n - 1)))
        specs += [spec, spec]
    return pl.pallas_call(
        kernel,
        out_shape=split_shapes(rows, sum(counts) * step),
        grid_spec=pltpu.PrefetchScalarGridSpec(
            num_scalar_prefetch=1,
            grid=(sum(counts),),
            in_specs=specs,
            out_specs=split_out_specs(rows, step),
        ),
    )(index[None], *[item for pair in pairs for item in pair])


def gradients_other(tokens_t, deltas):
    width, rows = tokens_t.shape
    count, _, cols = deltas.shape

    def kernel(t_ref, d_ref, o_ref, s_ref):
        o_ref[0] = dot(t_ref[...], d_ref[0], NN).astype(bf16)
        s_ref[0] = dot(jnp.ones((8, rows), bf16), d_ref[0], NN)

    return pl.pallas_call(
        kernel,
        out_shape=[
            jax.ShapeDtypeStruct((count, width, cols), bf16),
            jax.ShapeDtypeStruct((count, 8, cols), f32),
        ],
        grid=(count,),
        in_specs=[vmem(tokens_t.shape), pl.BlockSpec((1, rows, cols), lambda g: (g, 0, 0))],
        out_specs=[
            pl.BlockSpec((1, width, cols), lambda g: (g, 0, 0)),
            pl.BlockSpec((1, 8, cols), lambda g: (g, 0, 0)),
        ],
        cost_estimate=pl.CostEstimate(
            flops=2 * count * rows * width * cols, transcendentals=0, bytes_accessed=8 * rows * cols
        ),
    )(tokens_t, deltas)


def gradients_own(tokens_t, deltas, others, other_sums, table, index, core, size, one):
    width, rows = tokens_t.shape
    count, _, cols = deltas.shape
    part_rows = width // size
    height = count * part_rows + 16

    def kernel(at_ref, t_ref, d_ref, other_ref, sums_ref, table_ref, *refs):
        outs, total, own_sums, vec = refs[: len(PARTS)], refs[-3], refs[-2], refs[-1]
        g = pl.program_id(0)
        total[...] = dot(t_ref[...], d_ref[0], NN) + other_ref[0].astype(f32)
        own_sums[g] = dot(jnp.ones((8, rows), bf16), d_ref[0], NN)

        def blocks():
            for part, out_ref in zip(PARTS, outs):
                at = 0
                for offset, ks in part:
                    for k in ks:
                        yield at_ref[0] ^ (4 * k ^ offset), out_ref, at
                        at += 1

        for block, out_ref, at in blocks():
            value = total[pl.ds(pl.multiple_of(block * part_rows, 16), part_rows), :]
            out_ref[at, pl.ds(pl.multiple_of(g * part_rows, 16), part_rows), :] = value.astype(bf16)

        @pl.when(g == count - 1)
        def _():
            vec[...] = table_ref[...]
            for row, which in ((0, 0), (1, 2)):
                for ref, side in ((own_sums, 0), (sums_ref, 1)):
                    first = (at_ref[1] ^ side) * (size // 2)
                    for j in range(size // 2):
                        vec[first + j, row : row + 1, :one] = ref[which, 0:1, j * one : (j + 1) * one]
            for block, out_ref, at in blocks():
                out_ref[at, count * part_rows :, :] = vec[block].astype(bf16)

    return pl.pallas_call(
        kernel,
        out_shape=split_shapes(height, cols),
        grid_spec=pltpu.PrefetchScalarGridSpec(
            num_scalar_prefetch=1,
            grid=(count,),
            in_specs=[
                vmem(tokens_t.shape),
                pl.BlockSpec((1, rows, cols), lambda g, *_: (g, 0, 0)),
                pl.BlockSpec((1, width, cols), lambda g, *_: (g, 0, 0)),
                vmem(other_sums.shape),
                vmem(table.shape),
            ],
            out_specs=[vmem(shape.shape) for shape in split_shapes(height, cols)],
            scratch_shapes=[
                pltpu.VMEM((width, cols), f32),
                pltpu.VMEM((count, 8, cols), f32),
                pltpu.VMEM(table.shape, f32),
            ],
        ),
        cost_estimate=pl.CostEstimate(
            flops=2 * count * rows * width * cols, transcendentals=0, bytes_accessed=8 * rows * cols
        ),
    )(jnp.stack([index, core]), tokens_t, deltas, others, other_sums, table)


def pack_table(rows, last, size, cols):
    one = rows[0].shape[1] // size
    end = last.shape[1] // size

    def kernel(*refs):
        ins, out_ref, table = refs[: len(rows) + 1], refs[-2], refs[-1]
        table[...] = jnp.zeros(table.shape, f32)
        out_ref[...] = jnp.zeros(out_ref.shape, f32)
        for i, ref in enumerate(ins[:-1]):
            table[i + 2 : i + 3, :] = ref[...]
        for c in range(size):
            out_ref[c, :, :one] = table[:, c * one : (c + 1) * one]
            out_ref[c, 8:9, :end] = ins[-1][:, c * end : (c + 1) * end]

    return pl.pallas_call(
        kernel,
        out_shape=jax.ShapeDtypeStruct((size, 16, cols), f32),
        scratch_shapes=[pltpu.VMEM((16, rows[0].shape[1]), f32)],
    )(*rows, last)


def whole_call(kernel, outs, ins, blocks):
    return pl.pallas_call(
        kernel,
        out_shape=[jax.ShapeDtypeStruct(o, d) for o, d in outs],
        grid=(1,),
        in_specs=[vmem((n, *a.shape[1:])) for a, n in zip(ins, blocks)],
        out_specs=[vmem(o) for o, _ in outs],
    )(*ins)


def corner_back(parts, size):
    return swap_dp(parts[0], 1, size), swap_dp(parts[1], 2, size)


def corner_add(parts, got):
    keep = parts[2:4]

    def kernel(one_ref, two_ref, r1_ref, r2_ref, o1_ref, o2_ref):
        o1_ref[...] = one_ref[...] + r2_ref[...]
        o2_ref[...] = two_ref[...] + r1_ref[...]

    return whole_call(
        kernel, [(item.shape, bf16) for item in keep], [*keep, *got], (2, 2, 2, 2)
    )


def near_back(sums, size):
    return swap_dp(sums[0], 1, size), swap_dp(sums[1], 2, size)


def near_add(own, first, got):
    def kernel(own_ref, f1_ref, f2_ref, r1_ref, r2_ref, keep_ref, *outs):
        def total(k):
            early = f1_ref[2 + k] if k < 2 else f2_ref[k]
            late = r2_ref[k] if k < 2 else r1_ref[k - 2]
            return own_ref[k].astype(f32) + early.astype(f32) + late.astype(f32)

        keep_ref[...] = total(0)
        for k in (1, 2, 3):
            outs[k - 1][...] = total(k).astype(bf16)

    shape = own.shape[1:]
    return whole_call(
        kernel, [(shape, f32)] + [(shape, bf16)] * 3, [own, *first, *got], (4, 4, 4, 2, 2)
    )


def far_back(sums, size):
    return [swap_dp(item, 4 * (k + 1), size) for k, item in enumerate(sums[1:])]


def project(tokens, weights, vectors, core, side):
    rows, width = tokens.shape
    cols = weights.shape[2]

    def kernel(core_ref, x_ref, w_ref, v_ref, q_out, k_out, v_out):
        half = core_ref[0] ^ side
        bias = jnp.where(half == 0, v_ref[0:8, :cols], v_ref[0:8, cols:])
        x = x_ref[...]
        q_out[...] = (dot(x, w_ref[0], NN) + bias[0:1]).astype(bf16)
        k_out[...] = dot(x, w_ref[1], NN).astype(bf16)
        v_out[...] = (dot(x, w_ref[2], NN) + bias[1:2]).astype(bf16)

    tile = pl.BlockSpec((ROWS, cols), lambda i, *_: (i, 0))
    return pl.pallas_call(
        kernel,
        out_shape=[jax.ShapeDtypeStruct((rows, cols), bf16)] * 3,
        grid_spec=pltpu.PrefetchScalarGridSpec(
            num_scalar_prefetch=1,
            grid=(rows // ROWS,),
            in_specs=[
                pl.BlockSpec((ROWS, width), lambda i, *_: (i, 0)),
                vmem(weights.shape),
                vmem(vectors.shape),
            ],
            out_specs=[tile] * 3,
        ),
        cost_estimate=pl.CostEstimate(
            flops=6 * rows * width * cols, transcendentals=0, bytes_accessed=8 * rows * cols
        ),
    )(core[None], tokens, weights, vectors)


def token_gradient(first_delta, deltas, weights, part, parts):
    count, rows, cols = deltas[0].shape
    width = weights[0].shape[1]
    steps = rows // ROWS // parts

    def kernel(f_ref, d0_ref, d1_ref, w0_ref, w1_ref, *refs):
        o_ref = refs[-1]
        total = f_ref[...]
        for d_ref, w_ref in ((d0_ref, w0_ref), (d1_ref, w1_ref)):
            for g in range(count):
                total = total + dot(d_ref[g], w_ref[g], NT)
        o_ref[...] = total

    tile = pl.BlockSpec((ROWS, width), lambda i: (i + part * steps, 0))
    delta_part = pl.BlockSpec((count, ROWS, cols), lambda i: (0, i + part * steps, 0))
    return pl.pallas_call(
        kernel,
        out_shape=jax.ShapeDtypeStruct((rows, width), f32),
        grid=(steps,),
        in_specs=[tile, delta_part, delta_part] + [vmem(weights[0].shape)] * 2,
        out_specs=tile,
        input_output_aliases={0: 0},
        cost_estimate=pl.CostEstimate(
            flops=4 * count * rows * width * cols // parts,
            transcendentals=0,
            bytes_accessed=8 * rows * cols // parts,
        ),
    )(first_delta, *deltas, *weights)


def three_parts(row):
    high = row.astype(bf16).astype(f32)
    middle = (row - high).astype(bf16).astype(f32)
    return [high, middle, row - high - middle]


def extra_lanes(shape, keys_valid):
    lane = lax.broadcasted_iota(jnp.int32, shape, 1) % HD
    row = lax.broadcasted_iota(jnp.int32, shape, 0)
    bias = jnp.where(row < keys_valid, 0.0, masked_score)
    return jnp.where(lane == 0, bias, jnp.where(lane < 4, 1.0, 0.0)).astype(bf16)


def extra_rows(first, row, length):
    rows = [jnp.full((1, length), first, f32)]
    rows += three_parts(row) if row is not None else []
    rows.append(jnp.zeros((16 - len(rows), length), f32))
    return jnp.concatenate(rows, 0).astype(bf16)


def with_rows(own_t, h, first, row):
    length = own_t.shape[1]
    own = own_t[h * HD : (h + 1) * HD]
    rest = [extra_rows(first, row, length), jnp.zeros((HD - 16, length), bf16)]
    return jnp.concatenate([own] + rest if h == 0 else rest + [own], 0)


def attend_forward_kernel(lens, q_ref, k_ref, v_ref, ctx_ref, lse_ref):
    seq_len, cols = q_ref.shape
    lanes = 2 * HD
    lane = lax.broadcasted_iota(jnp.int32, (seq_len, lanes), 1)
    extra = extra_lanes((seq_len, lanes), lens[pl.program_id(0)])
    ones = jnp.ones((16, seq_len), bf16)
    tasks = [(p, h) for p in range(cols // lanes) for h in range(2)]
    loaded = {}

    def scores(p, h):
        here = slice(p * lanes, (p + 1) * lanes)
        if h == 0:
            query_t = (q_ref[:, here] * jnp.bfloat16(score_scale)).T
            loaded[p] = (query_t, k_ref[:, here], v_ref[:, here].T)
        query_t, keys, _ = loaded[p]
        return dot(jnp.where(lane // HD == h, keys, extra), with_rows(query_t, h, 1.0, None), NN)

    pieces = []
    ahead = scores(*tasks[0])
    for n, (p, h) in enumerate(tasks):
        now = ahead
        if n + 1 < len(tasks):
            ahead = scores(*tasks[n + 1])
        top = jnp.max(now, axis=0, keepdims=True)
        expo = jnp.exp(now - top).astype(bf16)
        value_t = loaded[p][2][h * HD : (h + 1) * HD]
        found = dot(jnp.concatenate([value_t, ones], 0), expo, NN)
        total = found[HD : HD + 1]
        pieces.append(found[:HD] / total)
        lse_ref[0, p, h : h + 1, :] = top + jnp.log(total)
        if h == 1:
            ctx_ref[:, p * lanes : (p + 1) * lanes] = jnp.concatenate(pieces, 0).T.astype(bf16)
            pieces = []


def attend_backward_kernel(lens, q_ref, k_ref, v_ref, d_ref, c_ref, lse_ref, out_ref):
    seq_len, cols = q_ref.shape
    lanes = 2 * HD
    lane = lax.broadcasted_iota(jnp.int32, (seq_len, lanes), 1)
    extra = extra_lanes((seq_len, lanes), lens[pl.program_id(0)])
    tasks = [(p, h) for p in range(cols // lanes) for h in range(2)]
    loaded = {}

    def products(p, h):
        here = slice(p * lanes, (p + 1) * lanes)
        if h == 0:
            query = q_ref[:, here] * jnp.bfloat16(score_scale)
            delta = d_ref[:, here]
            delta_t = delta.T
            inner = delta_t.astype(f32) * c_ref[:, here].T.astype(f32)
            keys = k_ref[:, here]
            loaded[p] = (query, query.T, delta, delta_t, inner, keys, keys.T, v_ref[:, here])
        _, query_t, _, delta_t, inner, keys, _, values = loaded[p]
        own = lane // HD == h
        inner = jnp.sum(inner[h * HD : (h + 1) * HD], axis=0, keepdims=True)
        lse = lse_ref[0, p, h : h + 1, :]
        logs = dot(jnp.where(own, keys, extra), with_rows(query_t, h, 1.0, -lse), NN)
        centred = dot(jnp.where(own, values, extra), with_rows(delta_t, h, 0.0, -inner), NN)
        return logs, centred

    ahead = products(*tasks[0])
    for n, (p, h) in enumerate(tasks):
        logs, centred = ahead
        if n + 1 < len(tasks):
            ahead = products(*tasks[n + 1])
        query, _, delta, _, _, _, keys_t, _ = loaded[p]
        probs = jnp.exp(logs)
        score_delta = (probs * centred).astype(bf16)
        own = lane // HD == h
        part_v = dot(probs.astype(bf16), jnp.where(own, delta, jnp.bfloat16(0)), NN)
        part_k = dot(score_delta, jnp.where(own, query, jnp.bfloat16(0)), NN)
        part_q = dot(keys_t[h * HD : (h + 1) * HD], score_delta, NN)
        if h == 0:
            dv, dk, dq = part_v, part_k, part_q
        else:
            here = slice(p * lanes, (p + 1) * lanes)
            out_ref[0, :, here] = (jnp.concatenate([dq, part_q], 0).T * score_scale).astype(bf16)
            out_ref[1, :, here] = (dk + part_k).astype(bf16)
            out_ref[2, :, here] = (dv + part_v).astype(bf16)


def attend_call(kernel, lens, operands, lse_in, seq_count):
    rows, cols = operands[0].shape
    seq_len = rows // seq_count
    pairs = cols // (2 * HD)
    tile = pl.BlockSpec((seq_len, cols), lambda s, *_: (s, 0))
    stat = pl.BlockSpec((1, pairs, 2, seq_len), lambda s, *_: (s, 0, 0, 0))
    if lse_in:
        out_shape = jax.ShapeDtypeStruct((3, rows, cols), bf16)
        out_specs = pl.BlockSpec((3, seq_len, cols), lambda s, *_: (0, s, 0))
    else:
        out_shape = [
            jax.ShapeDtypeStruct((rows, cols), bf16),
            jax.ShapeDtypeStruct((seq_count, pairs, 2, seq_len), f32),
        ]
        out_specs = [tile, stat]
    cells = rows * seq_len * cols // HD
    return pl.pallas_call(
        kernel,
        out_shape=out_shape,
        grid_spec=pltpu.PrefetchScalarGridSpec(
            num_scalar_prefetch=1,
            grid=(seq_count,),
            in_specs=[tile] * len(operands) + [stat] * len(lse_in),
            out_specs=out_specs,
        ),
        cost_estimate=pl.CostEstimate(
            flops=cells * HD * (40 if lse_in else 30),
            transcendentals=cells,
            bytes_accessed=8 * rows * cols,
        ),
    )(lens, *operands, *lse_in)


def on_device(
    tokens,
    cotangent,
    lengths,
    query_weight,
    key_weight,
    value_weight,
    out_weight,
    query_bias,
    value_bias,
    out_bias,
    first_gain,
    first_shift,
    inner_weight,
    inner_bias,
    outer_weight,
    outer_bias,
    second_gain,
    second_shift,
):
    size = lax.axis_size("dp")
    index = lax.axis_index("dp")
    core = lax.axis_index("tensor")
    orders = stage_orders(size)
    seq_count = lengths.shape[0] // 2
    lens = lax.dynamic_slice_in_dim(lengths, core * seq_count, seq_count, 0)
    fast = size == 16 and query_weight.shape[0] % 16 == 0
    half = query_weight.shape[1]
    step = half

    vectors = (
        query_bias,
        value_bias,
        out_bias,
        first_gain,
        first_shift,
        outer_bias,
        second_gain,
        second_shift,
        inner_bias,
    )
    bounds = [0]
    for item in vectors:
        bounds.append(bounds[-1] + item.shape[0])
    projections = (query_weight, key_weight, value_weight)
    out_t = out_weight.T
    outer_t = outer_weight.T

    if fast:
        shard = pack_first(projections, vectors)
        far = [swap_dp(shard, d, size) for d in (8, 4, 12)]
        low, high = jnp.stack([shard, far[0]]), jnp.stack(far[1:])
        two_low, one_high = swap_dp(low, 2, size), swap_dp(high, 1, size)
        one_low, two_high = swap_dp(low, 1, size), swap_dp(high, 2, size)
        shard_a = jnp.concatenate([out_t, inner_weight], 1)
        far_a = swap_dp(after(shard_a, low, high), 8, size)
        tokens_t = tokens.T
        pieces = [low, high, one_low, one_high, two_low, two_high]
        pieces += [swap_dp(two_low, 1, size), swap_dp(one_high, 2, size)]
        far_a, *pieces, tokens_t = lax.optimization_barrier((far_a, *pieces, tokens_t))
        low_a = jnp.stack([shard_a, far_a])
        high_a = swap_dp(low_a, 4, size)
        two_low_a, one_low_a = swap_dp(low_a, 2, size), swap_dp(low_a, 1, size)
        wqkv0, vecs, ib = place_first(
            pieces, index, 3, size, (query_bias.shape[0], inner_bias.shape[0])
        )
    else:
        own_vec = jnp.concatenate(vectors)[None, :]
        all_vec = gather_rows(own_vec, orders[0], size, index).astype(f32)
        found = [all_vec[:, a:b].reshape(1, -1) for a, b in zip(bounds[:-1], bounds[1:])]
        vecs = jnp.concatenate(found[:-1] + [jnp.zeros_like(found[0])] * 8, 0)
        ib = found[-1]
        wqkv0 = jnp.stack(
            [gather_rows(w, o, size, index) for w, o in zip(projections, orders)]
        )
        wo0 = gather_rows(out_t, orders[2], size, index)
        wi0 = gather_rows(inner_weight, orders[0], size, index)
        wu0 = gather_rows(outer_t, orders[1], size, index)

    wqkv = (wqkv0, swap_core(wqkv0))
    ob, g1, s1, ob2, g2, s2 = [vecs[i : i + 1] for i in range(2, 8)]
    hidden_half = inner_weight.shape[1]
    ib = (
        jnp.where(core == 0, ib[:, :hidden_half], ib[:, hidden_half:]),
        jnp.where(core == 0, ib[:, hidden_half:], ib[:, :hidden_half]),
    )

    q, k, v, ctx, lse = [], [], [], [], []
    for t in range(2):
        found = project(tokens, wqkv[t], vecs, core, t)
        if fast and t == 0:
            high_a, other, *found = lax.optimization_barrier((high_a, wqkv[1], *found))
            wqkv = (wqkv[0], other)
            one_high_a, two_high_a = swap_dp(high_a, 1, size), swap_dp(high_a, 2, size)
            far_b = swap_dp(after(outer_t, other), 8, size)
        q.append(found[0])
        k.append(found[1])
        v.append(found[2])
    if fast:
        far_b, *q = lax.optimization_barrier((far_b, *q))
        low_b = jnp.stack([outer_t, far_b])
        high_b = swap_dp(low_b, 4, size)
    for t in range(2):
        if fast and t == 1:
            q[1] = after(q[1], ctx[0])
        c, s = attend_call(attend_forward_kernel, lens, (q[t], k[t], v[t]), (), seq_count)
        lse.append(s)
        if fast and t == 0:
            pieces_a = [low_a, high_a, one_low_a, one_high_a, two_low_a, two_high_a]
            *pieces_a, high_b, c = lax.optimization_barrier((*pieces_a, high_b, c))
            pieces_a += [swap_dp(pieces_a[4], 1, size), swap_dp(pieces_a[3], 2, size)]
            two_low_b, one_high_b = swap_dp(low_b, 2, size), swap_dp(high_b, 1, size)
            one_low_b = swap_dp(low_b, 1, size)
        if fast and t == 1:
            *pieces_a, one_low_b, one_high_b, two_low_b, c = lax.optimization_barrier(
                (*pieces_a, one_low_b, one_high_b, two_low_b, c)
            )
            pieces_b = [low_b, high_b, one_low_b, one_high_b, two_low_b, swap_dp(high_b, 2, size)]
            pieces_b += [swap_dp(two_low_b, 1, size), swap_dp(one_high_b, 2, size)]
            wo0, wi0 = place_cols(pieces_a, index, (half, inner_weight.shape[1]), size)
        ctx.append(c)

    wo = (wo0, swap_core(wo0))
    wi = (wi0, swap_core(wi0))
    first_in = tokens.astype(f32) + dot(ctx[0], wo[0], NT) + dot(ctx[1], wo[1], NT) + ob

    def center(values):
        mean = jnp.mean(values, axis=-1, keepdims=True)
        centred = values - mean
        var = jnp.mean(centred * centred, axis=-1, keepdims=True)
        rinv = lax.rsqrt(var + norm_eps)
        return centred * rinv, rinv

    def norm_back(grad, normed, rinv, gain):
        scaled = grad * gain
        return rinv * (
            scaled
            - jnp.mean(scaled, axis=-1, keepdims=True)
            - normed * jnp.mean(scaled * normed, axis=-1, keepdims=True)
        )

    n1, r1 = center(first_in)
    hidden = (n1 * g1 + s1).astype(bf16)
    if not fast:
        wu = (wu0, swap_core(wu0))
    act, slope = [], []
    feed = ob2
    for t in range(2):
        u = dot(hidden, wi[t], NN) + ib[t]
        cdf = 0.5 * (1.0 + lax.erf(u * (0.5**0.5)))
        act.append((u * cdf).astype(bf16))
        pdf = jnp.exp(-0.5 * u * u) * 0.3989422804014327
        slope.append((cdf + u * pdf).astype(bf16))
        if fast and t == 0:
            *pieces_b, act[0] = lax.optimization_barrier((*pieces_b, act[0]))
            (wu0,) = place_cols(pieces_b, index, (inner_weight.shape[1],), size)
            wu = (wu0, swap_core(wu0))
            hidden = after(hidden, wu0)
        feed = feed + dot(act[t], wu[t], NT)
    second_in = hidden.astype(f32) + feed
    n2, r2 = center(second_in)
    layer_out = n2 * g2 + s2
    cot = cotangent.astype(f32)
    second_delta = norm_back(cot, n2, r2, g2)
    grad_g2 = jnp.sum(cot * n2, axis=0, keepdims=True)
    grad_s2 = jnp.sum(cot, axis=0, keepdims=True)
    grad_ob2 = jnp.sum(second_delta, axis=0, keepdims=True)
    feed_delta = second_delta.astype(bf16)

    def product(left, right):
        other = dot(left, right[1], TN).astype(bf16)
        other = swap_core(other)
        return dot(left, right[0], TN).astype(bf16), other

    gu = product(feed_delta, act)
    feed_delta, *gu = lax.optimization_barrier((feed_delta, *gu))
    inner_delta = [None, None]
    for t in (1, 0):
        inner_delta[t] = (dot(feed_delta, wu[t], NN) * slope[t].astype(f32)).astype(bf16)
        if fast and t == 1:
            parts_u = split_cols([gu], index, size, 2 * step)
            first_u = corner_back(parts_u, size)
            feed_delta = after(feed_delta, inner_delta[1], parts_u[4])
    gi = product(hidden, inner_delta)
    inner_delta[0], inner_delta[1], *gi = lax.optimization_barrier((*inner_delta, *gi))
    grad_ib = [jnp.sum(inner_delta[t].astype(f32), axis=0, keepdims=True) for t in range(2)]
    if fast:
        *first_u, _ = lax.optimization_barrier((*first_u, gi[0]))
        sums_u = corner_add(parts_u, first_u)
        got_u = near_back(sums_u, size)
        inner_delta[0], inner_delta[1] = [after(d, sums_u[0]) for d in inner_delta]
    hidden_delta = (
        second_delta + dot(inner_delta[0], wi[0], NT) + dot(inner_delta[1], wi[1], NT)
    )
    first_delta = norm_back(hidden_delta, n1, r1, g1)
    grad_g1 = jnp.sum(hidden_delta * n1, axis=0, keepdims=True)
    grad_s1 = jnp.sum(hidden_delta, axis=0, keepdims=True)
    grad_ob = jnp.sum(first_delta, axis=0, keepdims=True)
    branch_delta = first_delta.astype(bf16)
    if fast:
        *got_u, branch_delta = lax.optimization_barrier((*got_u, branch_delta))
        last_u = near_add(parts_u[4], first_u, got_u)
        branch_delta = after(branch_delta, last_u[0])
        got_u = far_back(last_u, size)
    go = product(branch_delta, ctx)
    ctx_delta = [dot(branch_delta, wo[t], NN).astype(bf16) for t in range(2)]

    def joined(pair):
        return jnp.where(
            core == 0, jnp.concatenate(pair, 1), jnp.concatenate(pair[::-1], 1)
        )

    grads = [grad_ob, grad_g1, grad_s1, grad_ob2, grad_g2, grad_s2, joined(grad_ib)]
    if fast:
        table = pack_table(grads[:-1], grads[-1], size, half)
        parts_i = split_cols([gi, go], index, size, step)
        first_i = corner_back(parts_i, size)
        ctx_delta[1] = after(ctx_delta[1], parts_i[4], table)

    def attend_back(t):
        return attend_call(
            attend_backward_kernel,
            lens,
            (q[t], k[t], v[t], ctx_delta[t], ctx[t]),
            (lse[t],),
            seq_count,
        )

    deltas = [None, None]
    deltas[1] = attend_back(1)
    if fast:
        arrived = lax.optimization_barrier((*first_i, *got_u, deltas[1]))
        first_i, got_u, deltas[1] = arrived[:2], arrived[2:5], arrived[5]
        sums_i = corner_add(parts_i, first_i)
        got_i = near_back(sums_i, size)
        deltas[1] = after(deltas[1], sums_i[0])
        others, other_sums = gradients_other(tokens_t, deltas[1])
        *got_i, others = lax.optimization_barrier((*got_i, others))
        last_i = near_add(parts_i[4], first_i, got_i)
        others = swap_core(others)
        got_i = far_back(last_i, size)
        ctx_delta[0] = after(ctx_delta[0], last_i[0])
        deltas[0] = attend_back(0)
        *got_i, deltas[0] = lax.optimization_barrier((*got_i, deltas[0]))
        parts_q = gradients_own(
            tokens_t,
            deltas[0],
            others,
            other_sums,
            table,
            index,
            core,
            size,
            query_bias.shape[0],
        )
        first_q = corner_back(parts_q, size)
        token_grad = token_gradient(
            after(first_delta, parts_q[4]), [after(d, parts_q[4]) for d in deltas], wqkv, 0, 2
        )
        *first_q, token_grad = lax.optimization_barrier((*first_q, token_grad))

        def total(last, got):
            return last[0] + got[0].astype(f32) + got[1].astype(f32) + got[2].astype(f32)

        out_gu = total(last_u, got_u).T
        out_gi = total(last_i, got_i)
        hidden_half = out_gi.shape[1] - half
        out_go = out_gi[:, hidden_half:].T
        out_gi = out_gi[:, :hidden_half]
        sums_q = corner_add(parts_q, first_q)
        got_q = near_back(sums_q, size)
        last_q = near_add(parts_q[4], first_q, got_q)
        got_q = far_back(last_q, size)
        token_grad = token_gradient(token_grad, [after(d, last_q[0]) for d in deltas], wqkv, 1, 2)
        out_q = total(last_q, got_q)
        n = query_weight.shape[0]
        out_qkv = [out_q[g * n : (g + 1) * n] for g in range(3)]
        vec = out_q[3 * n :]
        vec = vec + swap_core(vec)
        vec_out = [vec[i, : item.shape[0]] for i, item in enumerate(vectors)]
    else:
        deltas[0] = attend_back(0)
        token_grad = token_gradient(first_delta, deltas, wqkv, 0, 1)

        def reduce(pair, order):
            summed = (pair[0].astype(f32) + pair[1].astype(f32)).astype(bf16)
            return scatter_rows(summed, order, size, index)

        out_gu = reduce(gu, orders[1]).T
        out_gi = reduce(gi, orders[0])
        out_go = reduce(go, orders[2]).T
        out_qkv = [
            reduce(product(tokens, [d[g] for d in deltas]), order) for g, order in enumerate(orders)
        ]
        bias_grads = [
            joined([jnp.sum(d[g].astype(f32), axis=0, keepdims=True) for d in deltas]) for g in (0, 2)
        ]
        packed = jnp.concatenate([item.reshape(size, -1) for item in bias_grads + grads], axis=1)
        packed = packed + swap_core(packed)
        own = scatter_rows(packed, orders[0], size, index).reshape(-1)
        vec_out = [own[a:b] for a, b in zip(bounds[:-1], bounds[1:])]
    return (
        layer_out,
        token_grad,
        out_qkv[0],
        out_qkv[1],
        out_qkv[2],
        out_go,
        vec_out[0],
        vec_out[1],
        vec_out[2],
        vec_out[3],
        vec_out[4],
        out_gi,
        vec_out[8],
        out_gu,
        vec_out[5],
        vec_out[6],
        vec_out[7],
    )


def solution(mesh):
    both = P(("dp", "tensor"), None)
    cols = P("dp", "tensor")
    rows = P("tensor", "dp")
    vec = P("dp")
    in_specs = (
        both, both, vec, cols, cols, cols, rows, vec, vec, vec, vec, vec, cols, vec, rows, vec, vec, vec,
    )
    out_specs = (
        both, both, cols, cols, cols, rows, vec, vec, vec, vec, vec, cols, vec, rows, vec, vec, vec,
    )
    return jax.shard_map(
        on_device, mesh=mesh, in_specs=in_specs, out_specs=out_specs, check_vma=False
    )
```

```python
import jax
import jax.numpy as jnp
from jax import lax
from jax.experimental import pallas as pl
from jax.experimental.pallas import tpu as pltpu
from jax.sharding import PartitionSpec as P

HD = 64
norm_eps = 1e-12
masked_score = -1000000000.0
score_scale = HD ** (-0.5)
f32 = jnp.float32
bf16 = jnp.bfloat16
NT = (((1,), (1,)), ((), ()))
TN = (((0,), (0,)), ((), ()))
NN = (((1,), (0,)), ((), ()))
ROWS = 256


def dot(left, right, dims):
    return lax.dot_general(left, right, dims, preferred_element_type=f32)


def stage_orders(size):
    up = [1 << k for k in range(size.bit_length() - 1)]
    down = up[::-1]
    return (down, down[:-2] + [down[-1], down[-2]], [down[0]] + up[:-1])


def swap_dp(value, mask, size):
    return lax.ppermute(value, "dp", [(i, i ^ mask) for i in range(size)])


def swap_core(value):
    return lax.ppermute(value, "tensor", [(0, 1), (1, 0)])


def after(value, *others):
    return lax.optimization_barrier((value, *others))[0]


def gather_rows(shard, order, size, index):
    rows, cols = shard.shape
    have = []
    buf = shard
    for mask in order:
        received = swap_dp(buf, mask, size)
        have = sorted(have + [mask], reverse=True)
        axis = have.index(mask)
        buf = jnp.where(
            (index & mask) != 0,
            jnp.stack([received, buf], axis),
            jnp.stack([buf, received], axis),
        )
    return buf.reshape(size * rows, cols)


def scatter_rows(own, order, size, index):
    total, cols = own.shape
    have = sorted(order, reverse=True)
    buf = own.reshape([2] * len(have) + [total // size, cols])
    for mask in order[::-1]:
        axis = have.index(mask)
        bit = ((index & mask) != 0).astype(jnp.int32)
        keep = lax.dynamic_index_in_dim(buf, bit, axis, keepdims=False)
        give = lax.dynamic_index_in_dim(buf, 1 - bit, axis, keepdims=False)
        received = swap_dp(give, mask, size)
        buf = keep.astype(f32) + received.astype(f32)
        have.remove(mask)
        if have:
            buf = buf.astype(own.dtype)
    return buf


HINT = pl.CostEstimate(flops=1, transcendentals=0, bytes_accessed=1)


def distance_of(piece, k):
    return (4 * (piece % 2) + 8 * k) ^ piece // 2


def vmem(shape):
    return pl.BlockSpec(shape, lambda *_: (0,) * len(shape))


def pack_first(weights, vectors):
    rows, cols = weights[0].shape
    count = len(weights)

    def kernel(*refs):
        ins, out_ref, table = refs[: count + len(vectors)], refs[-2], refs[-1]
        for g in range(count):
            out_ref[g * rows : (g + 1) * rows, :] = ins[g][...]
        table[...] = jnp.zeros(table.shape, f32)
        for i, ref in enumerate(ins[count:]):
            table[i : i + 1, : ref.shape[1]] = ref[...].astype(f32)
        out_ref[count * rows :, :] = table[...].astype(bf16)

    return pl.pallas_call(
        kernel,
        out_shape=jax.ShapeDtypeStruct((count * rows + 16, cols), bf16),
        scratch_shapes=[pltpu.VMEM((16, cols), f32)],
        cost_estimate=HINT,
    )(*weights, *[item.reshape(1, -1) for item in vectors])


def place_first(pieces, index, count, size, lengths):
    total_rows, cols = pieces[0].shape[1:]
    rows = (total_rows - 16) // count

    def kernel(index_ref, *refs):
        ins = refs[: len(pieces)]
        w_ref, v_ref, last_ref, table = refs[len(pieces) :]
        for n, ref in enumerate(ins):
            for k in range(ref.shape[0]):
                block = index_ref[0] ^ distance_of(n, k)
                at = pl.ds(pl.multiple_of(block * rows, 16), rows)
                for g in range(count):
                    w_ref[g, at, :] = ref[k, g * rows : (g + 1) * rows, :]
                table[block] = ref[k, count * rows :, :].astype(f32)
        one, last = lengths
        for c in range(size):
            v_ref[:, c * one : (c + 1) * one] = table[c][:, :one]
            last_ref[:, c * last : (c + 1) * last] = table[c][8:9, :last]

    out = [(count, size * rows, cols), (16, size * lengths[0]), (1, size * lengths[1])]
    return pl.pallas_call(
        kernel,
        out_shape=[jax.ShapeDtypeStruct(o, d) for o, d in zip(out, (bf16, f32, f32))],
        grid_spec=pltpu.PrefetchScalarGridSpec(
            num_scalar_prefetch=1,
            grid=(1,),
            in_specs=[vmem(p.shape) for p in pieces],
            out_specs=[vmem(o) for o in out],
            scratch_shapes=[pltpu.VMEM((size, 16, cols), f32)],
        ),
        cost_estimate=HINT,
    )(index[None], *pieces)


def place_cols(pieces, index, widths, size):
    rows = pieces[0].shape[1]

    def kernel(index_ref, *refs):
        ins, outs = refs[: len(pieces)], refs[len(pieces) :]
        for n, ref in enumerate(ins):
            for k in range(ref.shape[0]):
                block = index_ref[0] ^ distance_of(n, k)
                at = 0
                for out_ref, width in zip(outs, widths):
                    here = pl.ds(pl.multiple_of(block * rows, 16), rows)
                    out_ref[here, :] = ref[k, :, at : at + width]
                    at += width

    out = [(size * rows, w) for w in widths]
    return pl.pallas_call(
        kernel,
        out_shape=[jax.ShapeDtypeStruct(o, bf16) for o in out],
        grid_spec=pltpu.PrefetchScalarGridSpec(
            num_scalar_prefetch=1,
            grid=(1,),
            in_specs=[vmem(p.shape) for p in pieces],
            out_specs=[vmem(o) for o in out],
        ),
        cost_estimate=HINT,
    )(index[None], *pieces)


PARTS = (
    ((3, (0, 1)), (1, (0, 1))),
    ((3, (2, 3)), (2, (2, 3))),
    ((1, (2, 3)),),
    ((2, (0, 1)),),
    ((0, (0, 1, 2, 3)),),
)


def split_out_specs(rows, step):
    return [
        pl.BlockSpec((sum(len(ks) for _, ks in part), rows, step), lambda i, *_: (0, 0, i))
        for part in PARTS
    ]


def split_shapes(rows, cols):
    return [
        jax.ShapeDtypeStruct(
            (sum(len(ks) for _, ks in part), rows, cols), bf16
        )
        for part in PARTS
    ]


def split_cols(pairs, index, size, step):
    total = pairs[0][0].shape[0]
    rows = total // size
    counts = [a.shape[1] // step for a, _ in pairs]
    starts = [sum(counts[:i]) for i in range(len(counts))]

    def kernel(index_ref, *refs):
        ins, outs = refs[: 2 * len(pairs)], refs[2 * len(pairs) :]
        for n, (first, count) in enumerate(zip(starts, counts)):

            @pl.when((pl.program_id(0) >= first) & (pl.program_id(0) < first + count))
            def _(n=n):
                for part, out_ref in zip(PARTS, outs):
                    at = 0
                    for offset, ks in part:
                        for k in ks:
                            block = index_ref[0] ^ (4 * k ^ offset)
                            here = pl.ds(pl.multiple_of(block * rows, 16), rows)
                            out_ref[at] = ins[2 * n][here, :] + ins[2 * n + 1][here, :]
                            at += 1

    specs = []
    for a, n in zip(starts, counts):
        spec = pl.BlockSpec((total, step), lambda i, *_, a=a, n=n: (0, jnp.clip(i - a, 0, n - 1)))
        specs += [spec, spec]
    return pl.pallas_call(
        kernel,
        out_shape=split_shapes(rows, sum(counts) * step),
        grid_spec=pltpu.PrefetchScalarGridSpec(
            num_scalar_prefetch=1,
            grid=(sum(counts),),
            in_specs=specs,
            out_specs=split_out_specs(rows, step),
        ),
        cost_estimate=HINT,
    )(index[None], *[item for pair in pairs for item in pair])


def gradients_other(tokens_t, deltas):
    width, rows = tokens_t.shape
    count, _, cols = deltas.shape

    def kernel(t_ref, d_ref, o_ref, s_ref):
        o_ref[0] = dot(t_ref[...], d_ref[0], NN).astype(bf16)
        s_ref[0] = dot(jnp.ones((8, rows), bf16), d_ref[0], NN)

    return pl.pallas_call(
        kernel,
        out_shape=[
            jax.ShapeDtypeStruct((count, width, cols), bf16),
            jax.ShapeDtypeStruct((count, 8, cols), f32),
        ],
        grid=(count,),
        in_specs=[vmem(tokens_t.shape), pl.BlockSpec((1, rows, cols), lambda g: (g, 0, 0))],
        out_specs=[
            pl.BlockSpec((1, width, cols), lambda g: (g, 0, 0)),
            pl.BlockSpec((1, 8, cols), lambda g: (g, 0, 0)),
        ],
        cost_estimate=HINT,
    )(tokens_t, deltas)


def gradients_own(tokens_t, deltas, others, other_sums, table, index, core, size, one):
    width, rows = tokens_t.shape
    count, _, cols = deltas.shape
    part_rows = width // size
    height = count * part_rows + 16

    def kernel(at_ref, t_ref, d_ref, other_ref, sums_ref, table_ref, *refs):
        outs, total, own_sums, vec = refs[: len(PARTS)], refs[-3], refs[-2], refs[-1]
        g = pl.program_id(0)
        total[...] = dot(t_ref[...], d_ref[0], NN) + other_ref[0].astype(f32)
        own_sums[g] = dot(jnp.ones((8, rows), bf16), d_ref[0], NN)

        def blocks():
            for part, out_ref in zip(PARTS, outs):
                at = 0
                for offset, ks in part:
                    for k in ks:
                        yield at_ref[0] ^ (4 * k ^ offset), out_ref, at
                        at += 1

        for block, out_ref, at in blocks():
            value = total[pl.ds(pl.multiple_of(block * part_rows, 16), part_rows), :]
            out_ref[at, pl.ds(pl.multiple_of(g * part_rows, 16), part_rows), :] = value.astype(bf16)

        @pl.when(g == count - 1)
        def _():
            vec[...] = table_ref[...]
            for row, which in ((0, 0), (1, 2)):
                for ref, side in ((own_sums, 0), (sums_ref, 1)):
                    first = (at_ref[1] ^ side) * (size // 2)
                    for j in range(size // 2):
                        vec[first + j, row : row + 1, :one] = ref[which, 0:1, j * one : (j + 1) * one]
            for block, out_ref, at in blocks():
                out_ref[at, count * part_rows :, :] = vec[block].astype(bf16)

    return pl.pallas_call(
        kernel,
        out_shape=split_shapes(height, cols),
        grid_spec=pltpu.PrefetchScalarGridSpec(
            num_scalar_prefetch=1,
            grid=(count,),
            in_specs=[
                vmem(tokens_t.shape),
                pl.BlockSpec((1, rows, cols), lambda g, *_: (g, 0, 0)),
                pl.BlockSpec((1, width, cols), lambda g, *_: (g, 0, 0)),
                vmem(other_sums.shape),
                vmem(table.shape),
            ],
            out_specs=[vmem(shape.shape) for shape in split_shapes(height, cols)],
            scratch_shapes=[
                pltpu.VMEM((width, cols), f32),
                pltpu.VMEM((count, 8, cols), f32),
                pltpu.VMEM(table.shape, f32),
            ],
        ),
        cost_estimate=HINT,
    )(jnp.stack([index, core]), tokens_t, deltas, others, other_sums, table)


def pack_table(first_sums, second_sums, last, size, cols):
    one = first_sums.shape[1] // size
    end = last.shape[1] // size

    def kernel(a_ref, b_ref, last_ref, out_ref, table):
        table[...] = jnp.zeros(table.shape, f32)
        out_ref[...] = jnp.zeros(out_ref.shape, f32)
        table[2:5, :] = a_ref[0:3, :]
        table[5:8, :] = b_ref[0:3, :]
        for c in range(size):
            out_ref[c, :, :one] = table[:, c * one : (c + 1) * one]
            out_ref[c, 8:9, :end] = last_ref[:, c * end : (c + 1) * end]

    return pl.pallas_call(
        kernel,
        out_shape=jax.ShapeDtypeStruct((size, 16, cols), f32),
        scratch_shapes=[pltpu.VMEM((16, first_sums.shape[1]), f32)],
        cost_estimate=HINT,
    )(first_sums, second_sums, last)


def whole_call(kernel, outs, ins, blocks):
    return pl.pallas_call(
        kernel,
        out_shape=[jax.ShapeDtypeStruct(o, d) for o, d in outs],
        grid=(1,),
        in_specs=[vmem((n, *a.shape[1:])) for a, n in zip(ins, blocks)],
        out_specs=[vmem(o) for o, _ in outs],
        cost_estimate=HINT,
    )(*ins)


def corner_back(parts, size):
    return swap_dp(parts[0], 1, size), swap_dp(parts[1], 2, size)


def corner_add(parts, got):
    keep = parts[2:4]

    def kernel(one_ref, two_ref, r1_ref, r2_ref, o1_ref, o2_ref):
        o1_ref[...] = one_ref[...] + r2_ref[...]
        o2_ref[...] = two_ref[...] + r1_ref[...]

    return whole_call(
        kernel, [(item.shape, bf16) for item in keep], [*keep, *got], (2, 2, 2, 2)
    )


def near_back(sums, size):
    return swap_dp(sums[0], 1, size), swap_dp(sums[1], 2, size)


def near_add(own, first, got):
    def kernel(own_ref, f1_ref, f2_ref, r1_ref, r2_ref, keep_ref, *outs):
        def total(k):
            early = f1_ref[2 + k] if k < 2 else f2_ref[k]
            late = r2_ref[k] if k < 2 else r1_ref[k - 2]
            return own_ref[k].astype(f32) + early.astype(f32) + late.astype(f32)

        keep_ref[...] = total(0)
        for k in (1, 2, 3):
            outs[k - 1][...] = total(k).astype(bf16)

    shape = own.shape[1:]
    return whole_call(
        kernel, [(shape, f32)] + [(shape, bf16)] * 3, [own, *first, *got], (4, 4, 4, 2, 2)
    )


def far_back(sums, size):
    return [swap_dp(item, 4 * (k + 1), size) for k, item in enumerate(sums[1:])]


def project(tokens, weights, vectors, core, side):
    rows, width = tokens.shape
    cols = weights.shape[2]

    def kernel(core_ref, x_ref, w_ref, v_ref, q_out, k_out, v_out):
        half = core_ref[0] ^ side
        bias = jnp.where(half == 0, v_ref[0:8, :cols], v_ref[0:8, cols:])
        x = x_ref[...]
        q_out[...] = (dot(x, w_ref[0], NN) + bias[0:1]).astype(bf16)
        k_out[...] = dot(x, w_ref[1], NN).astype(bf16)
        v_out[...] = (dot(x, w_ref[2], NN) + bias[1:2]).astype(bf16)

    tile = pl.BlockSpec((ROWS, cols), lambda i, *_: (i, 0))
    return pl.pallas_call(
        kernel,
        out_shape=[jax.ShapeDtypeStruct((rows, cols), bf16)] * 3,
        grid_spec=pltpu.PrefetchScalarGridSpec(
            num_scalar_prefetch=1,
            grid=(rows // ROWS,),
            in_specs=[
                pl.BlockSpec((ROWS, width), lambda i, *_: (i, 0)),
                vmem(weights.shape),
                vmem(vectors.shape),
            ],
            out_specs=[tile] * 3,
        ),
        cost_estimate=HINT,
    )(core[None], tokens, weights, vectors)


def token_gradient(first_delta, deltas, weights, part, parts):
    count, rows, cols = deltas[0].shape
    width = weights[0].shape[1]
    steps = rows // ROWS // parts

    def kernel(f_ref, d0_ref, d1_ref, w0_ref, w1_ref, *refs):
        o_ref = refs[-1]
        total = f_ref[...]
        for d_ref, w_ref in ((d0_ref, w0_ref), (d1_ref, w1_ref)):
            for g in range(count):
                total = total + dot(d_ref[g], w_ref[g], NT)
        o_ref[...] = total

    tile = pl.BlockSpec((ROWS, width), lambda i: (i + part * steps, 0))
    delta_part = pl.BlockSpec((count, ROWS, cols), lambda i: (0, i + part * steps, 0))
    return pl.pallas_call(
        kernel,
        out_shape=jax.ShapeDtypeStruct((rows, width), f32),
        grid=(steps,),
        in_specs=[tile, delta_part, delta_part] + [vmem(weights[0].shape)] * 2,
        out_specs=tile,
        input_output_aliases={0: 0},
        cost_estimate=HINT,
    )(first_delta, *deltas, *weights)


def center(values):
    mean = jnp.mean(values, axis=-1, keepdims=True)
    centred = values - mean
    var = jnp.mean(centred * centred, axis=-1, keepdims=True)
    rinv = lax.rsqrt(var + norm_eps)
    return centred * rinv, rinv


def norm_back(grad, normed, rinv, gain):
    scaled = grad * gain
    return rinv * (
        scaled
        - jnp.mean(scaled, axis=-1, keepdims=True)
        - normed * jnp.mean(scaled * normed, axis=-1, keepdims=True)
    )


def add_rows(ref, items):
    @pl.when(pl.program_id(0) == 0)
    def _():
        ref[...] = jnp.zeros(ref.shape, f32)

    for i, item in enumerate(items):
        ref[i : i + 1, :] += jnp.sum(item, axis=0, keepdims=True)


def row_call(kernel, tiles, wholes, outs, sums=True):
    rows = tiles[0].shape[0]
    width = outs[0][0]

    def tile(cols):
        return pl.BlockSpec((ROWS, cols), lambda i: (i, 0))

    return pl.pallas_call(
        kernel,
        out_shape=[jax.ShapeDtypeStruct((rows, n), d) for n, d in outs]
        + [jax.ShapeDtypeStruct((8, width), f32)] * sums,
        grid=(rows // ROWS,),
        in_specs=[tile(a.shape[1]) for a in tiles] + [vmem(a.shape) for a in wholes],
        out_specs=[tile(n) for n, _ in outs] + [vmem((8, width))] * sums,
        cost_estimate=HINT,
    )(*tiles, *wholes)


def first_block(tokens, context, weights, vectors):
    def kernel(x_ref, c0_ref, c1_ref, w0_ref, w1_ref, v_ref, out, low):
        total = dot(c0_ref[...], w0_ref[...], NT) + dot(c1_ref[...], w1_ref[...], NT)
        total = x_ref[...].astype(f32) + total + v_ref[2:3]
        out[...] = total
        low[...] = (center(total)[0] * v_ref[3:4] + v_ref[4:5]).astype(bf16)

    width = tokens.shape[1]
    return row_call(
        kernel,
        [tokens, *context],
        [*weights, vectors],
        [(width, f32), (width, bf16)],
        sums=False,
    )


def outer_block(hidden, cotangent, act, weights, vectors):
    def kernel(h_ref, c_ref, a0_ref, a1_ref, w0_ref, w1_ref, v_ref, out, delta, low, sums):
        feed = v_ref[5:6] + dot(a0_ref[...], w0_ref[...], NT) + dot(a1_ref[...], w1_ref[...], NT)
        normed, rinv = center(h_ref[...].astype(f32) + feed)
        out[...] = normed * v_ref[6:7] + v_ref[7:8]
        cot = c_ref[...].astype(f32)
        found = norm_back(cot, normed, rinv, v_ref[6:7])
        delta[...] = found
        low[...] = found.astype(bf16)
        add_rows(sums, (found, cot * normed, cot))

    width = hidden.shape[1]
    return row_call(
        kernel,
        [hidden, cotangent, *act],
        [*weights, vectors],
        [(width, f32), (width, f32), (width, bf16)],
    )


def inner_back(second_delta, inner_delta, first_in, weights, vectors):
    def kernel(s_ref, d0_ref, d1_ref, f_ref, w0_ref, w1_ref, v_ref, delta, low, sums):
        grad = s_ref[...] + dot(d0_ref[...], w0_ref[...], NT) + dot(d1_ref[...], w1_ref[...], NT)
        normed, rinv = center(f_ref[...])
        found = norm_back(grad, normed, rinv, v_ref[3:4])
        delta[...] = found
        low[...] = found.astype(bf16)
        add_rows(sums, (found, grad * normed, grad))

    width = first_in.shape[1]
    return row_call(
        kernel,
        [second_delta, *inner_delta, first_in],
        [*weights, vectors],
        [(width, f32), (width, bf16)],
    )


def three_parts(row):
    high = row.astype(bf16).astype(f32)
    middle = (row - high).astype(bf16).astype(f32)
    return [high, middle, row - high - middle]


def extra_lanes(shape, keys_valid):
    lane = lax.broadcasted_iota(jnp.int32, shape, 1) % HD
    row = lax.broadcasted_iota(jnp.int32, shape, 0)
    bias = jnp.where(row < keys_valid, 0.0, masked_score)
    return jnp.where(lane == 0, bias, jnp.where(lane < 4, 1.0, 0.0)).astype(bf16)


def extra_rows(first, row, length):
    rows = [jnp.full((1, length), first, f32)]
    rows += three_parts(row) if row is not None else []
    rows.append(jnp.zeros((16 - len(rows), length), f32))
    return jnp.concatenate(rows, 0).astype(bf16)


def with_rows(own_t, h, first, row):
    length = own_t.shape[1]
    own = own_t[h * HD : (h + 1) * HD]
    rest = [extra_rows(first, row, length), jnp.zeros((HD - 16, length), bf16)]
    return jnp.concatenate([own] + rest if h == 0 else rest + [own], 0)


def attend_forward_kernel(lens, q_ref, k_ref, v_ref, ctx_ref, lse_ref):
    seq_len, lanes = q_ref.shape
    lane = lax.broadcasted_iota(jnp.int32, (seq_len, lanes), 1)
    extra = extra_lanes((seq_len, lanes), lens[pl.program_id(0)])
    ones = jnp.ones((16, seq_len), bf16)
    loaded = {}

    def scores(h):
        if h == 0:
            query_t = (q_ref[...] * jnp.bfloat16(score_scale)).T
            loaded[0] = (query_t, k_ref[...], v_ref[...].T)
        query_t, keys, _ = loaded[0]
        return dot(jnp.where(lane // HD == h, keys, extra), with_rows(query_t, h, 1.0, None), NN)

    pieces = []
    ahead = scores(0)
    for h in range(2):
        now = ahead
        if h == 0:
            ahead = scores(1)
        top = jnp.max(now, axis=0, keepdims=True)
        expo = jnp.exp(now - top).astype(bf16)
        value_t = loaded[0][2][h * HD : (h + 1) * HD]
        found = dot(jnp.concatenate([value_t, ones], 0), expo, NN)
        total = found[HD : HD + 1]
        pieces.append(found[:HD] / total)
        lse_ref[0, 0, h : h + 1, :] = top + jnp.log(total)
        if h == 1:
            ctx_ref[...] = jnp.concatenate(pieces, 0).T.astype(bf16)
            pieces = []


def attend_backward_kernel(lens, q_ref, k_ref, v_ref, d_ref, c_ref, lse_ref, out_ref):
    seq_len, lanes = q_ref.shape
    lane = lax.broadcasted_iota(jnp.int32, (seq_len, lanes), 1)
    extra = extra_lanes((seq_len, lanes), lens[pl.program_id(0)])
    loaded = {}

    def products(h):
        if h == 0:
            query = q_ref[...] * jnp.bfloat16(score_scale)
            delta = d_ref[...]
            delta_t = delta.T
            inner = delta_t.astype(f32) * c_ref[...].T.astype(f32)
            keys = k_ref[...]
            loaded[0] = (query, query.T, delta, delta_t, inner, keys, keys.T, v_ref[...])
        _, query_t, _, delta_t, inner, keys, _, values = loaded[0]
        own = lane // HD == h
        inner = jnp.sum(inner[h * HD : (h + 1) * HD], axis=0, keepdims=True)
        lse = lse_ref[0, 0, h : h + 1, :]
        logs = dot(jnp.where(own, keys, extra), with_rows(query_t, h, 1.0, -lse), NN)
        centred = dot(jnp.where(own, values, extra), with_rows(delta_t, h, 0.0, -inner), NN)
        return logs, centred

    ahead = products(0)
    for h in range(2):
        logs, centred = ahead
        if h == 0:
            ahead = products(1)
        query, _, delta, _, _, _, keys_t, _ = loaded[0]
        probs = jnp.exp(logs)
        score_delta = (probs * centred).astype(bf16)
        own = lane // HD == h
        part_v = dot(probs.astype(bf16), jnp.where(own, delta, jnp.bfloat16(0)), NN)
        part_k = dot(score_delta, jnp.where(own, query, jnp.bfloat16(0)), NN)
        part_q = dot(keys_t[h * HD : (h + 1) * HD], score_delta, NN)
        if h == 0:
            dv, dk, dq = part_v, part_k, part_q
        else:
            out_ref[0] = (jnp.concatenate([dq, part_q], 0).T * score_scale).astype(bf16)
            out_ref[1] = (dk + part_k).astype(bf16)
            out_ref[2] = (dv + part_v).astype(bf16)


def attend_call(kernel, lens, operands, lse_in, seq_count):
    rows, cols = operands[0].shape
    seq_len = rows // seq_count
    pairs = cols // (2 * HD)
    tile = pl.BlockSpec((seq_len, 2 * HD), lambda s, p, *_: (s, p))
    stat = pl.BlockSpec((1, 1, 2, seq_len), lambda s, p, *_: (s, p, 0, 0))
    if lse_in:
        out_shape = jax.ShapeDtypeStruct((3, rows, cols), bf16)
        out_specs = pl.BlockSpec((3, seq_len, 2 * HD), lambda s, p, *_: (0, s, p))
    else:
        out_shape = [
            jax.ShapeDtypeStruct((rows, cols), bf16),
            jax.ShapeDtypeStruct((seq_count, pairs, 2, seq_len), f32),
        ]
        out_specs = [tile, stat]
    return pl.pallas_call(
        kernel,
        out_shape=out_shape,
        grid_spec=pltpu.PrefetchScalarGridSpec(
            num_scalar_prefetch=1,
            grid=(seq_count, pairs),
            in_specs=[tile] * len(operands) + [stat] * len(lse_in),
            out_specs=out_specs,
        ),
        cost_estimate=HINT,
    )(lens, *operands, *lse_in)


def on_device(
    tokens,
    cotangent,
    lengths,
    query_weight,
    key_weight,
    value_weight,
    out_weight,
    query_bias,
    value_bias,
    out_bias,
    first_gain,
    first_shift,
    inner_weight,
    inner_bias,
    outer_weight,
    outer_bias,
    second_gain,
    second_shift,
):
    size = lax.axis_size("dp")
    index = lax.axis_index("dp")
    core = lax.axis_index("tensor")
    orders = stage_orders(size)
    seq_count = lengths.shape[0] // 2
    lens = lax.dynamic_slice_in_dim(lengths, core * seq_count, seq_count, 0)
    fast = size == 16 and query_weight.shape[0] % 16 == 0
    half = query_weight.shape[1]
    step = half

    vectors = (
        query_bias,
        value_bias,
        out_bias,
        first_gain,
        first_shift,
        outer_bias,
        second_gain,
        second_shift,
        inner_bias,
    )
    bounds = [0]
    for item in vectors:
        bounds.append(bounds[-1] + item.shape[0])
    projections = (query_weight, key_weight, value_weight)
    out_t = out_weight.T
    outer_t = outer_weight.T

    if fast:
        shard = pack_first(projections, vectors)
        far = [swap_dp(shard, d, size) for d in (8, 4, 12)]
        low, high = jnp.stack([shard, far[0]]), jnp.stack(far[1:])
        two_low, one_high = swap_dp(low, 2, size), swap_dp(high, 1, size)
        one_low, two_high = swap_dp(low, 1, size), swap_dp(high, 2, size)
        shard_a = jnp.concatenate([out_t, inner_weight], 1)
        far_a = swap_dp(after(shard_a, low, high), 8, size)
        tokens_t = tokens.T
        pieces = [low, high, one_low, one_high, two_low, two_high]
        pieces += [swap_dp(two_low, 1, size), swap_dp(one_high, 2, size)]
        far_a, *pieces, tokens_t = lax.optimization_barrier((far_a, *pieces, tokens_t))
        low_a = jnp.stack([shard_a, far_a])
        high_a = swap_dp(low_a, 4, size)
        two_low_a, one_low_a = swap_dp(low_a, 2, size), swap_dp(low_a, 1, size)
        wqkv0, vecs, ib = place_first(
            pieces, index, 3, size, (query_bias.shape[0], inner_bias.shape[0])
        )
    else:
        own_vec = jnp.concatenate(vectors)[None, :]
        all_vec = gather_rows(own_vec, orders[0], size, index).astype(f32)
        found = [all_vec[:, a:b].reshape(1, -1) for a, b in zip(bounds[:-1], bounds[1:])]
        vecs = jnp.concatenate(found[:-1] + [jnp.zeros_like(found[0])] * 8, 0)
        ib = found[-1]
        wqkv0 = jnp.stack(
            [gather_rows(w, o, size, index) for w, o in zip(projections, orders)]
        )
        wo0 = gather_rows(out_t, orders[2], size, index)
        wi0 = gather_rows(inner_weight, orders[0], size, index)
        wu0 = gather_rows(outer_t, orders[1], size, index)

    wqkv = (wqkv0, swap_core(wqkv0))
    hidden_half = inner_weight.shape[1]
    ib = (
        jnp.where(core == 0, ib[:, :hidden_half], ib[:, hidden_half:]),
        jnp.where(core == 0, ib[:, hidden_half:], ib[:, :hidden_half]),
    )

    q, k, v, ctx, lse = [], [], [], [], []
    for t in range(2):
        found = project(tokens, wqkv[t], vecs, core, t)
        if fast and t == 0:
            high_a, other, *found = lax.optimization_barrier((high_a, wqkv[1], *found))
            wqkv = (wqkv[0], other)
            one_high_a, two_high_a = swap_dp(high_a, 1, size), swap_dp(high_a, 2, size)
            far_b = swap_dp(after(outer_t, other), 8, size)
        q.append(found[0])
        k.append(found[1])
        v.append(found[2])
    if fast:
        far_b, one_low_a, two_low_a, *q = lax.optimization_barrier(
            (far_b, one_low_a, two_low_a, *q)
        )
        low_b = jnp.stack([outer_t, far_b])
        two_low_b, one_low_b = swap_dp(low_b, 2, size), swap_dp(low_b, 1, size)
        high_b = swap_dp(low_b, 4, size)
    for t in range(2):
        if fast and t == 1:
            q[1] = after(q[1], ctx[0])
        c, s = attend_call(attend_forward_kernel, lens, (q[t], k[t], v[t]), (), seq_count)
        lse.append(s)
        if fast and t == 0:
            pieces_a = [low_a, high_a, one_low_a, one_high_a, two_low_a, two_high_a]
            *pieces_a, high_b, two_low_b, one_low_b, c = lax.optimization_barrier(
                (*pieces_a, high_b, two_low_b, one_low_b, c)
            )
            pieces_a += [swap_dp(pieces_a[4], 1, size), swap_dp(pieces_a[3], 2, size)]
        if fast and t == 1:
            *pieces_a, c = lax.optimization_barrier((*pieces_a, c))
            one_high_b, two_high_b = swap_dp(high_b, 1, size), swap_dp(high_b, 2, size)
            pieces_b = [low_b, high_b, one_low_b, one_high_b, two_low_b, two_high_b]
            pieces_b.append(swap_dp(two_low_b, 1, size))
            wo0, wi0 = place_cols(pieces_a, index, (half, inner_weight.shape[1]), size)
        ctx.append(c)

    wo = (wo0, swap_core(wo0))
    wi = (wi0, swap_core(wi0))
    first_in, hidden = first_block(tokens, ctx, wo, vecs)
    if fast:
        *pieces_b, hidden = lax.optimization_barrier((*pieces_b, hidden))
        pieces_b.append(swap_dp(pieces_b[3], 2, size))
    act, slope = [], []
    for t in range(2):
        u = dot(hidden, wi[t], NN) + ib[t]
        cdf = 0.5 * (1.0 + lax.erf(u * (0.5**0.5)))
        act.append((u * cdf).astype(bf16))
        pdf = jnp.exp(-0.5 * u * u) * 0.3989422804014327
        slope.append((cdf + u * pdf).astype(bf16))
        if fast and t == 0:
            *pieces_b, act[0] = lax.optimization_barrier((*pieces_b, act[0]))
            (wu0,) = place_cols(pieces_b, index, (inner_weight.shape[1],), size)
            hidden = after(hidden, wu0)
    wu = (wu0, swap_core(wu0))
    layer_out, second_delta, feed_delta, second_sums = outer_block(
        hidden, cotangent, act, wu, vecs
    )

    def product(left, right):
        other = dot(left, right[1], TN).astype(bf16)
        other = swap_core(other)
        return dot(left, right[0], TN).astype(bf16), other

    gu = product(feed_delta, act)
    feed_delta, *gu = lax.optimization_barrier((feed_delta, *gu))
    inner_delta = [None, None]
    for t in (1, 0):
        inner_delta[t] = (dot(feed_delta, wu[t], NN) * slope[t].astype(f32)).astype(bf16)
    gi = product(hidden, inner_delta)
    inner_delta[0], inner_delta[1], *gi = lax.optimization_barrier((*inner_delta, *gi))
    grad_ib = [jnp.sum(inner_delta[t].astype(f32), axis=0, keepdims=True) for t in range(2)]
    if fast:
        parts_u = split_cols([gu, gi], index, size, 2 * step)
        first_u = corner_back(parts_u, size)
        inner_delta[0], inner_delta[1] = [after(d, parts_u[4]) for d in inner_delta]
    first_delta, branch_delta, first_sums = inner_back(
        second_delta, inner_delta, first_in, wi, vecs
    )
    go = product(branch_delta, ctx)
    ctx_delta = [dot(branch_delta, wo[t], NN).astype(bf16) for t in range(2)]

    def joined(pair):
        return jnp.where(
            core == 0, jnp.concatenate(pair, 1), jnp.concatenate(pair[::-1], 1)
        )

    grad_ib = joined(grad_ib)
    if fast:
        table = pack_table(first_sums, second_sums, grad_ib, size, half)
        parts_i = split_cols([go], index, size, step)
        first_i = corner_back(parts_i, size)
        *first_u, ctx_delta[1], _ = lax.optimization_barrier(
            (*first_u, ctx_delta[1], parts_i[4])
        )
        sums_u = corner_add(parts_u, first_u)
        got_u = near_back(sums_u, size)
        ctx_delta[1] = after(ctx_delta[1], table, sums_u[0])

    def attend_back(t):
        return attend_call(
            attend_backward_kernel,
            lens,
            (q[t], k[t], v[t], ctx_delta[t], ctx[t]),
            (lse[t],),
            seq_count,
        )

    deltas = [None, None]
    deltas[1] = attend_back(1)
    if fast:
        arrived = lax.optimization_barrier((*first_i, *got_u, deltas[1]))
        first_i, got_u, deltas[1] = arrived[:2], arrived[2:4], arrived[4]
        last_u = near_add(parts_u[4], first_u, got_u)
        got_u = far_back(last_u, size)
        sums_i = corner_add(parts_i, first_i)
        got_i = near_back(sums_i, size)
        deltas[1] = after(deltas[1], last_u[0], sums_i[0])
        others, other_sums = gradients_other(tokens_t, deltas[1])
        *got_i, others = lax.optimization_barrier((*got_i, others))
        last_i = near_add(parts_i[4], first_i, got_i)
        others = swap_core(others)
        got_i = far_back(last_i, size)
        ctx_delta[0] = after(ctx_delta[0], last_i[0])
        deltas[0] = attend_back(0)
        *got_u, deltas[0] = lax.optimization_barrier((*got_u, deltas[0]))
        parts_q = gradients_own(
            tokens_t,
            deltas[0],
            others,
            other_sums,
            table,
            index,
            core,
            size,
            query_bias.shape[0],
        )
        first_q = corner_back(parts_q, size)
        *got_i, _ = lax.optimization_barrier((*got_i, parts_q[4]))
        token_grad = token_gradient(
            after(first_delta, parts_q[4]), [after(d, parts_q[4]) for d in deltas], wqkv, 0, 2
        )
        *first_q, token_grad = lax.optimization_barrier((*first_q, token_grad))

        def total(last, got):
            return last[0] + got[0].astype(f32) + got[1].astype(f32) + got[2].astype(f32)

        out_ui = total(last_u, got_u)
        hidden_half = out_ui.shape[1] // 2
        out_gu = out_ui[:, :hidden_half].T
        out_gi = out_ui[:, hidden_half:]
        out_go = total(last_i, got_i).T
        sums_q = corner_add(parts_q, first_q)
        got_q = near_back(sums_q, size)
        last_q = near_add(parts_q[4], first_q, got_q)
        got_q = far_back(last_q, size)
        token_grad = token_gradient(token_grad, [after(d, last_q[0]) for d in deltas], wqkv, 1, 2)
        out_q = total(last_q, got_q)
        n = query_weight.shape[0]
        out_qkv = [out_q[g * n : (g + 1) * n] for g in range(3)]
        vec = out_q[3 * n :]
        vec = vec + swap_core(vec)
        vec_out = [vec[i, : item.shape[0]] for i, item in enumerate(vectors)]
    else:
        deltas[0] = attend_back(0)
        token_grad = token_gradient(first_delta, deltas, wqkv, 0, 1)

        def reduce(pair, order):
            summed = (pair[0].astype(f32) + pair[1].astype(f32)).astype(bf16)
            return scatter_rows(summed, order, size, index)

        out_gu = reduce(gu, orders[1]).T
        out_gi = reduce(gi, orders[0])
        out_go = reduce(go, orders[2]).T
        out_qkv = [
            reduce(product(tokens, [d[g] for d in deltas]), order) for g, order in enumerate(orders)
        ]
        bias_grads = [
            joined([jnp.sum(d[g].astype(f32), axis=0, keepdims=True) for d in deltas]) for g in (0, 2)
        ]
        bias_grads += [s[i : i + 1] for s in (first_sums, second_sums) for i in range(3)]
        bias_grads.append(grad_ib)
        packed = jnp.concatenate([item.reshape(size, -1) for item in bias_grads], axis=1)
        packed = packed + swap_core(packed)
        own = scatter_rows(packed, orders[0], size, index).reshape(-1)
        vec_out = [own[a:b] for a, b in zip(bounds[:-1], bounds[1:])]
    return (
        layer_out,
        token_grad,
        out_qkv[0],
        out_qkv[1],
        out_qkv[2],
        out_go,
        vec_out[0],
        vec_out[1],
        vec_out[2],
        vec_out[3],
        vec_out[4],
        out_gi,
        vec_out[8],
        out_gu,
        vec_out[5],
        vec_out[6],
        vec_out[7],
    )


def solution(mesh):
    both = P(("dp", "tensor"), None)
    cols = P("dp", "tensor")
    rows = P("tensor", "dp")
    vec = P("dp")
    in_specs = (
        both, both, vec, cols, cols, cols, rows, vec, vec, vec, vec, vec, cols, vec, rows, vec, vec, vec,
    )
    out_specs = (
        both, both, cols, cols, cols, rows, vec, vec, vec, vec, vec, cols, vec, rows, vec, vec, vec,
    )
    return jax.shard_map(
        on_device, mesh=mesh, in_specs=in_specs, out_specs=out_specs, check_vma=False
    )
```

```python
import jax
import jax.numpy as jnp
from jax import lax
from jax.experimental import pallas as pl
from jax.experimental.pallas import tpu as pltpu
from jax.sharding import PartitionSpec as P

HD = 64
norm_eps = 1e-12
masked_score = -1000000000.0
score_scale = HD ** (-0.5)
f32 = jnp.float32
bf16 = jnp.bfloat16
NT = (((1,), (1,)), ((), ()))
TN = (((0,), (0,)), ((), ()))
NN = (((1,), (0,)), ((), ()))
ROWS = 256


def dot(left, right, dims):
    return lax.dot_general(left, right, dims, preferred_element_type=f32)


def stage_orders(size):
    up = [1 << k for k in range(size.bit_length() - 1)]
    down = up[::-1]
    return (down, down[:-2] + [down[-1], down[-2]], [down[0]] + up[:-1])


def swap_dp(value, mask, size):
    return lax.ppermute(value, "dp", [(i, i ^ mask) for i in range(size)])


def swap_core(value):
    return lax.ppermute(value, "tensor", [(0, 1), (1, 0)])


def after(value, *others):
    return lax.optimization_barrier((value, *others))[0]


def gather_rows(shard, order, size, index):
    rows, cols = shard.shape
    have = []
    buf = shard
    for mask in order:
        received = swap_dp(buf, mask, size)
        have = sorted(have + [mask], reverse=True)
        axis = have.index(mask)
        buf = jnp.where(
            (index & mask) != 0,
            jnp.stack([received, buf], axis),
            jnp.stack([buf, received], axis),
        )
    return buf.reshape(size * rows, cols)


def scatter_rows(own, order, size, index):
    total, cols = own.shape
    have = sorted(order, reverse=True)
    buf = own.reshape([2] * len(have) + [total // size, cols])
    for mask in order[::-1]:
        axis = have.index(mask)
        bit = ((index & mask) != 0).astype(jnp.int32)
        keep = lax.dynamic_index_in_dim(buf, bit, axis, keepdims=False)
        give = lax.dynamic_index_in_dim(buf, 1 - bit, axis, keepdims=False)
        received = swap_dp(give, mask, size)
        buf = keep.astype(f32) + received.astype(f32)
        have.remove(mask)
        if have:
            buf = buf.astype(own.dtype)
    return buf


BLOCK = 256
PART = 128
HINT = pl.CostEstimate(flops=1, transcendentals=0, bytes_accessed=1)


def distance_of(piece, k):
    return (4 * (piece % 2) + 8 * k) ^ piece // 2


def vmem(shape):
    return pl.BlockSpec(shape, lambda *_: (0,) * len(shape))


def pack_first(weights, vectors):
    rows, cols = weights[0].shape
    count = len(weights)

    def kernel(*refs):
        ins, out_ref, table = refs[: count + len(vectors)], refs[-2], refs[-1]
        for g in range(count):
            out_ref[g * rows : (g + 1) * rows, :] = ins[g][...]
        table[...] = jnp.zeros(table.shape, f32)
        for i, ref in enumerate(ins[count:]):
            table[i : i + 1, : ref.shape[1]] = ref[...].astype(f32)
        out_ref[count * rows :, :] = table[...].astype(bf16)

    return pl.pallas_call(
        kernel,
        out_shape=jax.ShapeDtypeStruct((count * rows + 16, cols), bf16),
        scratch_shapes=[pltpu.VMEM((16, cols), f32)],
        cost_estimate=HINT,
    )(*weights, *[item.reshape(1, -1) for item in vectors])


def place_first(pieces, index, count, size, lengths):
    total_rows, cols = pieces[0].shape[1:]
    rows = (total_rows - 16) // count

    def kernel(index_ref, *refs):
        ins = refs[: len(pieces)]
        w_ref, v_ref, last_ref, table = refs[len(pieces) :]
        for n, ref in enumerate(ins):
            for k in range(ref.shape[0]):
                block = index_ref[0] ^ distance_of(n, k)
                at = pl.ds(pl.multiple_of(block * rows, 16), rows)
                for g in range(count):
                    w_ref[g, at, :] = ref[k, g * rows : (g + 1) * rows, :]
                table[block] = ref[k, count * rows :, :].astype(f32)
        one, last = lengths
        for c in range(size):
            v_ref[:, c * one : (c + 1) * one] = table[c][:, :one]
            last_ref[:, c * last : (c + 1) * last] = table[c][8:9, :last]

    out = [(count, size * rows, cols), (16, size * lengths[0]), (1, size * lengths[1])]
    return pl.pallas_call(
        kernel,
        out_shape=[jax.ShapeDtypeStruct(o, d) for o, d in zip(out, (bf16, f32, f32))],
        grid_spec=pltpu.PrefetchScalarGridSpec(
            num_scalar_prefetch=1,
            grid=(1,),
            in_specs=[vmem(p.shape) for p in pieces],
            out_specs=[vmem(o) for o in out],
            scratch_shapes=[pltpu.VMEM((size, 16, cols), f32)],
        ),
        cost_estimate=HINT,
    )(index[None], *pieces)


def place_cols(pieces, index, widths, size):
    rows = pieces[0].shape[1]

    def kernel(index_ref, *refs):
        ins, outs = refs[: len(pieces)], refs[len(pieces) :]
        for n, ref in enumerate(ins):
            for k in range(ref.shape[0]):
                block = index_ref[0] ^ distance_of(n, k)
                at = 0
                for out_ref, width in zip(outs, widths):
                    here = pl.ds(pl.multiple_of(block * rows, 16), rows)
                    out_ref[here, :] = ref[k, :, at : at + width]
                    at += width

    out = [(size * rows, w) for w in widths]
    return pl.pallas_call(
        kernel,
        out_shape=[jax.ShapeDtypeStruct(o, bf16) for o in out],
        grid_spec=pltpu.PrefetchScalarGridSpec(
            num_scalar_prefetch=1,
            grid=(1,),
            in_specs=[vmem(p.shape) for p in pieces],
            out_specs=[vmem(o) for o in out],
        ),
        cost_estimate=HINT,
    )(index[None], *pieces)


PARTS = (
    ((3, (0, 1)), (1, (0, 1))),
    ((3, (2, 3)), (2, (2, 3))),
    ((1, (2, 3)),),
    ((2, (0, 1)),),
    ((0, (0, 1, 2, 3)),),
)


def split_out_specs(rows, step):
    return [
        pl.BlockSpec((sum(len(ks) for _, ks in part), rows, step), lambda i, *_: (0, 0, i))
        for part in PARTS
    ]


def split_shapes(rows, cols):
    return [
        jax.ShapeDtypeStruct(
            (sum(len(ks) for _, ks in part), rows, cols), bf16
        )
        for part in PARTS
    ]


def split_cols(pairs, index, size, step):
    total = pairs[0][0].shape[0]
    rows = total // size
    counts = [a.shape[1] // step for a, _ in pairs]
    starts = [sum(counts[:i]) for i in range(len(counts))]

    def kernel(index_ref, *refs):
        ins, outs = refs[: 2 * len(pairs)], refs[2 * len(pairs) :]
        for n, (first, count) in enumerate(zip(starts, counts)):

            @pl.when((pl.program_id(0) >= first) & (pl.program_id(0) < first + count))
            def _(n=n):
                for part, out_ref in zip(PARTS, outs):
                    at = 0
                    for offset, ks in part:
                        for k in ks:
                            block = index_ref[0] ^ (4 * k ^ offset)
                            here = pl.ds(pl.multiple_of(block * rows, 16), rows)
                            out_ref[at] = ins[2 * n][here, :] + ins[2 * n + 1][here, :]
                            at += 1

    specs = []
    for a, n in zip(starts, counts):
        spec = pl.BlockSpec((total, step), lambda i, *_, a=a, n=n: (0, jnp.clip(i - a, 0, n - 1)))
        specs += [spec, spec]
    return pl.pallas_call(
        kernel,
        out_shape=split_shapes(rows, sum(counts) * step),
        grid_spec=pltpu.PrefetchScalarGridSpec(
            num_scalar_prefetch=1,
            grid=(sum(counts),),
            in_specs=specs,
            out_specs=split_out_specs(rows, step),
        ),
        cost_estimate=HINT,
    )(index[None], *[item for pair in pairs for item in pair])


def gradients_other(tokens_t, deltas):
    width, rows = tokens_t.shape
    count, _, cols = deltas.shape

    def kernel(t_ref, d_ref, o_ref, s_ref):
        o_ref[0] = dot(t_ref[...], d_ref[0], NN).astype(bf16)
        s_ref[0] = dot(jnp.ones((8, rows), bf16), d_ref[0], NN)

    return pl.pallas_call(
        kernel,
        out_shape=[
            jax.ShapeDtypeStruct((count, width, cols), bf16),
            jax.ShapeDtypeStruct((count, 8, cols), f32),
        ],
        grid=(count,),
        in_specs=[vmem(tokens_t.shape), pl.BlockSpec((1, rows, cols), lambda g: (g, 0, 0))],
        out_specs=[
            pl.BlockSpec((1, width, cols), lambda g: (g, 0, 0)),
            pl.BlockSpec((1, 8, cols), lambda g: (g, 0, 0)),
        ],
        cost_estimate=HINT,
    )(tokens_t, deltas)


def gradients_own(tokens_t, deltas, others, other_sums, table, index, core, size, one):
    width, rows = tokens_t.shape
    count, _, cols = deltas.shape
    part_rows = width // size
    height = count * part_rows + 16

    def kernel(at_ref, t_ref, d_ref, other_ref, sums_ref, table_ref, *refs):
        outs, total, own_sums, vec = refs[: len(PARTS)], refs[-3], refs[-2], refs[-1]
        g = pl.program_id(0)
        total[...] = dot(t_ref[...], d_ref[0], NN) + other_ref[0].astype(f32)
        own_sums[g] = dot(jnp.ones((8, rows), bf16), d_ref[0], NN)

        def blocks():
            for part, out_ref in zip(PARTS, outs):
                at = 0
                for offset, ks in part:
                    for k in ks:
                        yield at_ref[0] ^ (4 * k ^ offset), out_ref, at
                        at += 1

        for block, out_ref, at in blocks():
            value = total[pl.ds(pl.multiple_of(block * part_rows, 16), part_rows), :]
            out_ref[at, pl.ds(pl.multiple_of(g * part_rows, 16), part_rows), :] = value.astype(bf16)

        @pl.when(g == count - 1)
        def _():
            vec[...] = table_ref[...]
            for row, which in ((0, 0), (1, 2)):
                for ref, side in ((own_sums, 0), (sums_ref, 1)):
                    first = (at_ref[1] ^ side) * (size // 2)
                    for j in range(size // 2):
                        vec[first + j, row : row + 1, :one] = ref[which, 0:1, j * one : (j + 1) * one]
            for block, out_ref, at in blocks():
                out_ref[at, count * part_rows :, :] = vec[block].astype(bf16)

    return pl.pallas_call(
        kernel,
        out_shape=split_shapes(height, cols),
        grid_spec=pltpu.PrefetchScalarGridSpec(
            num_scalar_prefetch=1,
            grid=(count,),
            in_specs=[
                vmem(tokens_t.shape),
                pl.BlockSpec((1, rows, cols), lambda g, *_: (g, 0, 0)),
                pl.BlockSpec((1, width, cols), lambda g, *_: (g, 0, 0)),
                vmem(other_sums.shape),
                vmem(table.shape),
            ],
            out_specs=[vmem(shape.shape) for shape in split_shapes(height, cols)],
            scratch_shapes=[
                pltpu.VMEM((width, cols), f32),
                pltpu.VMEM((count, 8, cols), f32),
                pltpu.VMEM(table.shape, f32),
            ],
        ),
        cost_estimate=HINT,
    )(jnp.stack([index, core]), tokens_t, deltas, others, other_sums, table)


def pack_table(first_sums, second_sums, inner_sums, core, size, cols):
    one = first_sums.shape[1] // size
    end = inner_sums.shape[1] // size

    def kernel(core_ref, a_ref, b_ref, inner_ref, out_ref, table):
        table[...] = jnp.zeros(table.shape, f32)
        out_ref[...] = jnp.zeros(out_ref.shape, f32)
        table[2:5, :] = a_ref[0:3, :]
        table[5:8, :] = b_ref[0:3, :]
        for c in range(size):
            out_ref[c, :, :one] = table[:, c * one : (c + 1) * one]
            d = (c + size // 2) % size
            here = inner_ref[0:1, c * end : (c + 1) * end]
            there = inner_ref[0:1, d * end : (d + 1) * end]
            out_ref[c, 8:9, :end] = jnp.where(core_ref[0] == 0, here, there)

    ins = (first_sums, second_sums, inner_sums)
    return pl.pallas_call(
        kernel,
        out_shape=jax.ShapeDtypeStruct((size, 16, cols), f32),
        grid_spec=pltpu.PrefetchScalarGridSpec(
            num_scalar_prefetch=1,
            grid=(1,),
            in_specs=[vmem(a.shape) for a in ins],
            out_specs=vmem((size, 16, cols)),
            scratch_shapes=[pltpu.VMEM((16, first_sums.shape[1]), f32)],
        ),
        cost_estimate=HINT,
    )(core[None], *ins)


def whole_call(kernel, outs, ins, blocks):
    return pl.pallas_call(
        kernel,
        out_shape=[jax.ShapeDtypeStruct(o, d) for o, d in outs],
        grid=(1,),
        in_specs=[vmem((n, *a.shape[1:])) for a, n in zip(ins, blocks)],
        out_specs=[vmem(o) for o, _ in outs],
        cost_estimate=HINT,
    )(*ins)


def corner_back(parts, size):
    return swap_dp(parts[0], 1, size), swap_dp(parts[1], 2, size)


def corner_add(parts, got):
    keep = parts[2:4]

    def kernel(one_ref, two_ref, r1_ref, r2_ref, o1_ref, o2_ref):
        o1_ref[...] = one_ref[...] + r2_ref[...]
        o2_ref[...] = two_ref[...] + r1_ref[...]

    return whole_call(
        kernel, [(item.shape, bf16) for item in keep], [*keep, *got], (2, 2, 2, 2)
    )


def near_back(sums, size):
    return swap_dp(sums[0], 1, size), swap_dp(sums[1], 2, size)


def near_add(own, first, got):
    def kernel(own_ref, f1_ref, f2_ref, r1_ref, r2_ref, keep_ref, *outs):
        def total(k):
            early = f1_ref[2 + k] if k < 2 else f2_ref[k]
            late = r2_ref[k] if k < 2 else r1_ref[k - 2]
            return own_ref[k].astype(f32) + early.astype(f32) + late.astype(f32)

        keep_ref[...] = total(0)
        for k in (1, 2, 3):
            outs[k - 1][...] = total(k).astype(bf16)

    shape = own.shape[1:]
    return whole_call(
        kernel, [(shape, f32)] + [(shape, bf16)] * 3, [own, *first, *got], (4, 4, 4, 2, 2)
    )


def far_back(sums, size):
    return [swap_dp(item, 4 * (k + 1), size) for k, item in enumerate(sums[1:])]


def project(tokens, weights, vectors, core, side):
    rows, width = tokens.shape
    cols = weights.shape[2]

    def kernel(core_ref, x_ref, w_ref, v_ref, q_out, k_out, v_out):
        half = core_ref[0] ^ side
        bias = jnp.where(half == 0, v_ref[0:8, :cols], v_ref[0:8, cols:])
        x = x_ref[...]
        q_out[...] = (dot(x, w_ref[0], NN) + bias[0:1]).astype(bf16)
        k_out[...] = dot(x, w_ref[1], NN).astype(bf16)
        v_out[...] = (dot(x, w_ref[2], NN) + bias[1:2]).astype(bf16)

    tile = pl.BlockSpec((ROWS, cols), lambda i, *_: (i, 0))
    return pl.pallas_call(
        kernel,
        out_shape=[jax.ShapeDtypeStruct((rows, cols), bf16)] * 3,
        grid_spec=pltpu.PrefetchScalarGridSpec(
            num_scalar_prefetch=1,
            grid=(rows // ROWS,),
            in_specs=[
                pl.BlockSpec((ROWS, width), lambda i, *_: (i, 0)),
                vmem(weights.shape),
                vmem(vectors.shape),
            ],
            out_specs=[tile] * 3,
        ),
        cost_estimate=HINT,
    )(core[None], tokens, weights, vectors)


def token_gradient(first_delta, deltas, weights, part, parts):
    count, rows, cols = deltas[0].shape
    width = weights[0].shape[1]
    steps = rows // ROWS // parts

    def kernel(f_ref, d0_ref, d1_ref, w0_ref, w1_ref, *refs):
        o_ref = refs[-1]
        total = f_ref[...]
        for d_ref, w_ref in ((d0_ref, w0_ref), (d1_ref, w1_ref)):
            for g in range(count):
                total = total + dot(d_ref[g], w_ref[g], NT)
        o_ref[...] = total

    tile = pl.BlockSpec((ROWS, width), lambda i: (i + part * steps, 0))
    delta_part = pl.BlockSpec((count, ROWS, cols), lambda i: (0, i + part * steps, 0))
    return pl.pallas_call(
        kernel,
        out_shape=jax.ShapeDtypeStruct((rows, width), f32),
        grid=(steps,),
        in_specs=[tile, delta_part, delta_part] + [vmem(weights[0].shape)] * 2,
        out_specs=tile,
        input_output_aliases={0: 0},
        cost_estimate=HINT,
    )(first_delta, *deltas, *weights)


def center(values):
    mean = jnp.mean(values, axis=-1, keepdims=True)
    centred = values - mean
    var = jnp.mean(centred * centred, axis=-1, keepdims=True)
    rinv = lax.rsqrt(var + norm_eps)
    return centred * rinv, rinv


def norm_back(grad, normed, rinv, gain):
    scaled = grad * gain
    return rinv * (
        scaled
        - jnp.mean(scaled, axis=-1, keepdims=True)
        - normed * jnp.mean(scaled * normed, axis=-1, keepdims=True)
    )


def add_rows(ref, items):
    for i, item in enumerate(items):
        ref[i : i + 1, : item.shape[1]] += jnp.sum(item, axis=0, keepdims=True)


def clear(*refs):
    @pl.when(pl.program_id(0) == 0)
    def _():
        for ref in refs:
            ref[...] = jnp.zeros(ref.shape, f32)


def in_turns(product, finish):
    parts = [slice(i, i + PART) for i in range(0, BLOCK, PART)]
    ahead = product(parts[0])
    for n, part in enumerate(parts):
        now = ahead
        if n + 1 < len(parts):
            ahead = product(parts[n + 1])
        finish(part, now)


def row_call(kernel, tiles, wholes, outs, sums):
    rows = tiles[0].shape[0]

    def tile(cols):
        return pl.BlockSpec((BLOCK, cols), lambda i: (i, 0))

    return pl.pallas_call(
        kernel,
        out_shape=[jax.ShapeDtypeStruct((rows, n), d) for n, d in outs]
        + [jax.ShapeDtypeStruct((8, n), f32) for n in sums],
        grid=(rows // BLOCK,),
        in_specs=[tile(a.shape[1]) for a in tiles] + [vmem(a.shape) for a in wholes],
        out_specs=[tile(n) for n, _ in outs] + [vmem((8, n)) for n in sums],
        cost_estimate=HINT,
    )(*tiles, *wholes)


def first_block(tokens, context, weights, vectors):
    def kernel(x_ref, c0_ref, c1_ref, w0_ref, w1_ref, v_ref, out, low):
        def product(at):
            return dot(c0_ref[at], w0_ref[...], NT) + dot(c1_ref[at], w1_ref[...], NT)

        def finish(at, total):
            total = x_ref[at].astype(f32) + total + v_ref[2:3]
            out[at] = total
            low[at] = (center(total)[0] * v_ref[3:4] + v_ref[4:5]).astype(bf16)

        in_turns(product, finish)

    width = tokens.shape[1]
    return row_call(
        kernel, [tokens, *context], [*weights, vectors], [(width, f32), (width, bf16)], ()
    )


def outer_block(hidden, cotangent, act, weights, vectors):
    def kernel(h_ref, c_ref, a0_ref, a1_ref, w0_ref, w1_ref, v_ref, out, delta, low, sums):
        clear(sums)

        def product(at):
            return dot(a0_ref[at], w0_ref[...], NT) + dot(a1_ref[at], w1_ref[...], NT)

        def finish(at, feed):
            normed, rinv = center(h_ref[at].astype(f32) + (v_ref[5:6] + feed))
            out[at] = normed * v_ref[6:7] + v_ref[7:8]
            cot = c_ref[at].astype(f32)
            found = norm_back(cot, normed, rinv, v_ref[6:7])
            delta[at] = found
            low[at] = found.astype(bf16)
            add_rows(sums, (found, cot * normed, cot))

        in_turns(product, finish)

    width = hidden.shape[1]
    return row_call(
        kernel,
        [hidden, cotangent, *act],
        [*weights, vectors],
        [(width, f32), (width, f32), (width, bf16)],
        (width,),
    )


def inner_back(second_delta, inner_delta, first_in, weights, vectors):
    def kernel(s_ref, d0_ref, d1_ref, f_ref, w0_ref, w1_ref, v_ref, delta, low, sums, inner):
        clear(sums, inner)
        ones = jnp.ones((8, BLOCK), bf16)
        half = d0_ref.shape[1]
        inner[:, :half] += dot(ones, d0_ref[...], NN)
        inner[:, half:] += dot(ones, d1_ref[...], NN)

        def product(at):
            return dot(d0_ref[at], w0_ref[...], NT) + dot(d1_ref[at], w1_ref[...], NT)

        def finish(at, grad):
            grad = s_ref[at] + grad
            normed, rinv = center(f_ref[at])
            found = norm_back(grad, normed, rinv, v_ref[3:4])
            delta[at] = found
            low[at] = found.astype(bf16)
            add_rows(sums, (found, grad * normed, grad))

        in_turns(product, finish)

    width = first_in.shape[1]
    return row_call(
        kernel,
        [second_delta, *inner_delta, first_in],
        [*weights, vectors],
        [(width, f32), (width, bf16)],
        (width, 2 * inner_delta[0].shape[1]),
    )


def three_parts(row):
    high = row.astype(bf16).astype(f32)
    middle = (row - high).astype(bf16).astype(f32)
    return [high, middle, row - high - middle]


def extra_lanes(shape, keys_valid):
    lane = lax.broadcasted_iota(jnp.int32, shape, 1) % HD
    row = lax.broadcasted_iota(jnp.int32, shape, 0)
    bias = jnp.where(row < keys_valid, 0.0, masked_score)
    return jnp.where(lane == 0, bias, jnp.where(lane < 4, 1.0, 0.0)).astype(bf16)


def extra_rows(first, row, length):
    rows = [jnp.full((1, length), first, f32)]
    rows += three_parts(row) if row is not None else []
    rows.append(jnp.zeros((16 - len(rows), length), f32))
    return jnp.concatenate(rows, 0).astype(bf16)


def with_rows(own_t, h, first, row):
    length = own_t.shape[1]
    own = own_t[h * HD : (h + 1) * HD]
    rest = [extra_rows(first, row, length), jnp.zeros((HD - 16, length), bf16)]
    return jnp.concatenate([own] + rest if h == 0 else rest + [own], 0)


def attend_forward_kernel(lens, q_ref, k_ref, v_ref, ctx_ref, lse_ref):
    seq_len, lanes = q_ref.shape
    lane = lax.broadcasted_iota(jnp.int32, (seq_len, lanes), 1)
    extra = extra_lanes((seq_len, lanes), lens[pl.program_id(0)])
    ones = jnp.ones((16, seq_len), bf16)
    loaded = {}

    def scores(h):
        if h == 0:
            query_t = (q_ref[...] * jnp.bfloat16(score_scale)).T
            loaded[0] = (query_t, k_ref[...], v_ref[...].T)
        query_t, keys, _ = loaded[0]
        return dot(jnp.where(lane // HD == h, keys, extra), with_rows(query_t, h, 1.0, None), NN)

    pieces = []
    ahead = scores(0)
    for h in range(2):
        now = ahead
        if h == 0:
            ahead = scores(1)
        top = jnp.max(now, axis=0, keepdims=True)
        expo = jnp.exp(now - top).astype(bf16)
        value_t = loaded[0][2][h * HD : (h + 1) * HD]
        found = dot(jnp.concatenate([value_t, ones], 0), expo, NN)
        total = found[HD : HD + 1]
        pieces.append(found[:HD] / total)
        lse_ref[0, 0, h : h + 1, :] = top + jnp.log(total)
        if h == 1:
            ctx_ref[...] = jnp.concatenate(pieces, 0).T.astype(bf16)
            pieces = []


def attend_backward_kernel(lens, q_ref, k_ref, v_ref, d_ref, c_ref, lse_ref, out_ref):
    seq_len, lanes = q_ref.shape
    lane = lax.broadcasted_iota(jnp.int32, (seq_len, lanes), 1)
    extra = extra_lanes((seq_len, lanes), lens[pl.program_id(0)])
    loaded = {}

    def products(h):
        if h == 0:
            query = q_ref[...] * jnp.bfloat16(score_scale)
            delta = d_ref[...]
            delta_t = delta.T
            inner = delta_t.astype(f32) * c_ref[...].T.astype(f32)
            keys = k_ref[...]
            loaded[0] = (query, query.T, delta, delta_t, inner, keys, keys.T, v_ref[...])
        _, query_t, _, delta_t, inner, keys, _, values = loaded[0]
        own = lane // HD == h
        inner = jnp.sum(inner[h * HD : (h + 1) * HD], axis=0, keepdims=True)
        lse = lse_ref[0, 0, h : h + 1, :]
        logs = dot(jnp.where(own, keys, extra), with_rows(query_t, h, 1.0, -lse), NN)
        centred = dot(jnp.where(own, values, extra), with_rows(delta_t, h, 0.0, -inner), NN)
        return logs, centred

    ahead = products(0)
    for h in range(2):
        logs, centred = ahead
        if h == 0:
            ahead = products(1)
        query, _, delta, _, _, _, keys_t, _ = loaded[0]
        probs = jnp.exp(logs)
        score_delta = (probs * centred).astype(bf16)
        own = lane // HD == h
        part_v = dot(probs.astype(bf16), jnp.where(own, delta, jnp.bfloat16(0)), NN)
        part_k = dot(score_delta, jnp.where(own, query, jnp.bfloat16(0)), NN)
        part_q = dot(keys_t[h * HD : (h + 1) * HD], score_delta, NN)
        if h == 0:
            dv, dk, dq = part_v, part_k, part_q
        else:
            out_ref[0] = (jnp.concatenate([dq, part_q], 0).T * score_scale).astype(bf16)
            out_ref[1] = (dk + part_k).astype(bf16)
            out_ref[2] = (dv + part_v).astype(bf16)


def attend_call(kernel, lens, operands, lse_in, seq_count):
    rows, cols = operands[0].shape
    seq_len = rows // seq_count
    pairs = cols // (2 * HD)
    tile = pl.BlockSpec((seq_len, 2 * HD), lambda s, p, *_: (s, p))
    stat = pl.BlockSpec((1, 1, 2, seq_len), lambda s, p, *_: (s, p, 0, 0))
    if lse_in:
        out_shape = jax.ShapeDtypeStruct((3, rows, cols), bf16)
        out_specs = pl.BlockSpec((3, seq_len, 2 * HD), lambda s, p, *_: (0, s, p))
    else:
        out_shape = [
            jax.ShapeDtypeStruct((rows, cols), bf16),
            jax.ShapeDtypeStruct((seq_count, pairs, 2, seq_len), f32),
        ]
        out_specs = [tile, stat]
    return pl.pallas_call(
        kernel,
        out_shape=out_shape,
        grid_spec=pltpu.PrefetchScalarGridSpec(
            num_scalar_prefetch=1,
            grid=(seq_count, pairs),
            in_specs=[tile] * len(operands) + [stat] * len(lse_in),
            out_specs=out_specs,
        ),
        cost_estimate=HINT,
    )(lens, *operands, *lse_in)


def on_device(
    tokens,
    cotangent,
    lengths,
    query_weight,
    key_weight,
    value_weight,
    out_weight,
    query_bias,
    value_bias,
    out_bias,
    first_gain,
    first_shift,
    inner_weight,
    inner_bias,
    outer_weight,
    outer_bias,
    second_gain,
    second_shift,
):
    size = lax.axis_size("dp")
    index = lax.axis_index("dp")
    core = lax.axis_index("tensor")
    orders = stage_orders(size)
    seq_count = lengths.shape[0] // 2
    lens = lax.dynamic_slice_in_dim(lengths, core * seq_count, seq_count, 0)
    fast = size == 16 and query_weight.shape[0] % 16 == 0
    half = query_weight.shape[1]
    step = half

    vectors = (
        query_bias,
        value_bias,
        out_bias,
        first_gain,
        first_shift,
        outer_bias,
        second_gain,
        second_shift,
        inner_bias,
    )
    bounds = [0]
    for item in vectors:
        bounds.append(bounds[-1] + item.shape[0])
    projections = (query_weight, key_weight, value_weight)
    out_t = out_weight.T
    outer_t = outer_weight.T

    if fast:
        shard = pack_first(projections, vectors)
        far = [swap_dp(shard, d, size) for d in (8, 4, 12)]
        low, high = jnp.stack([shard, far[0]]), jnp.stack(far[1:])
        two_low, one_high = swap_dp(low, 2, size), swap_dp(high, 1, size)
        one_low, two_high = swap_dp(low, 1, size), swap_dp(high, 2, size)
        shard_a = jnp.concatenate([out_t, inner_weight], 1)
        far_a = swap_dp(after(shard_a, low, high), 8, size)
        tokens_t = tokens.T
        pieces = [low, high, one_low, one_high, two_low, two_high]
        pieces += [swap_dp(two_low, 1, size), swap_dp(one_high, 2, size)]
        far_a, *pieces, tokens_t = lax.optimization_barrier((far_a, *pieces, tokens_t))
        low_a = jnp.stack([shard_a, far_a])
        high_a = swap_dp(low_a, 4, size)
        two_low_a, one_low_a = swap_dp(low_a, 2, size), swap_dp(low_a, 1, size)
        wqkv0, vecs, ib = place_first(
            pieces, index, 3, size, (query_bias.shape[0], inner_bias.shape[0])
        )
    else:
        own_vec = jnp.concatenate(vectors)[None, :]
        all_vec = gather_rows(own_vec, orders[0], size, index).astype(f32)
        found = [all_vec[:, a:b].reshape(1, -1) for a, b in zip(bounds[:-1], bounds[1:])]
        vecs = jnp.concatenate(found[:-1] + [jnp.zeros_like(found[0])] * 8, 0)
        ib = found[-1]
        wqkv0 = jnp.stack(
            [gather_rows(w, o, size, index) for w, o in zip(projections, orders)]
        )
        wo0 = gather_rows(out_t, orders[2], size, index)
        wi0 = gather_rows(inner_weight, orders[0], size, index)
        wu0 = gather_rows(outer_t, orders[1], size, index)

    wqkv = (wqkv0, swap_core(wqkv0))
    hidden_half = inner_weight.shape[1]
    ib = (
        jnp.where(core == 0, ib[:, :hidden_half], ib[:, hidden_half:]),
        jnp.where(core == 0, ib[:, hidden_half:], ib[:, :hidden_half]),
    )

    q, k, v, ctx, lse = [], [], [], [], []
    for t in range(2):
        found = project(tokens, wqkv[t], vecs, core, t)
        if fast and t == 0:
            high_a, other, *found = lax.optimization_barrier((high_a, wqkv[1], *found))
            wqkv = (wqkv[0], other)
            one_high_a, two_high_a = swap_dp(high_a, 1, size), swap_dp(high_a, 2, size)
            far_b = swap_dp(after(outer_t, other), 8, size)
        q.append(found[0])
        k.append(found[1])
        v.append(found[2])
    if fast:
        far_b, one_low_a, two_low_a, *q = lax.optimization_barrier(
            (far_b, one_low_a, two_low_a, *q)
        )
        low_b = jnp.stack([outer_t, far_b])
        two_low_b, one_low_b = swap_dp(low_b, 2, size), swap_dp(low_b, 1, size)
        high_b = swap_dp(low_b, 4, size)
    for t in range(2):
        if fast and t == 1:
            q[1] = after(q[1], ctx[0])
        c, s = attend_call(attend_forward_kernel, lens, (q[t], k[t], v[t]), (), seq_count)
        lse.append(s)
        if fast and t == 0:
            pieces_a = [low_a, high_a, one_low_a, one_high_a, two_low_a, two_high_a]
            *pieces_a, high_b, two_low_b, one_low_b, c = lax.optimization_barrier(
                (*pieces_a, high_b, two_low_b, one_low_b, c)
            )
            pieces_a += [swap_dp(pieces_a[4], 1, size), swap_dp(pieces_a[3], 2, size)]
        if fast and t == 1:
            *pieces_a, c = lax.optimization_barrier((*pieces_a, c))
            one_high_b, two_high_b = swap_dp(high_b, 1, size), swap_dp(high_b, 2, size)
            pieces_b = [low_b, high_b, one_low_b, one_high_b, two_low_b, two_high_b]
            pieces_b.append(swap_dp(two_low_b, 1, size))
            wo0, wi0 = place_cols(pieces_a, index, (half, inner_weight.shape[1]), size)
        ctx.append(c)

    wo = (wo0, swap_core(wo0))
    wi = (wi0, swap_core(wi0))
    first_in, hidden = first_block(tokens, ctx, wo, vecs)
    if fast:
        *pieces_b, hidden = lax.optimization_barrier((*pieces_b, hidden))
        pieces_b.append(swap_dp(pieces_b[3], 2, size))
    act, slope = [], []
    for t in range(2):
        u = dot(hidden, wi[t], NN) + ib[t]
        cdf = 0.5 * (1.0 + lax.erf(u * (0.5**0.5)))
        act.append((u * cdf).astype(bf16))
        pdf = jnp.exp(-0.5 * u * u) * 0.3989422804014327
        slope.append((cdf + u * pdf).astype(bf16))
        if fast and t == 0:
            *pieces_b, act[0] = lax.optimization_barrier((*pieces_b, act[0]))
            (wu0,) = place_cols(pieces_b, index, (inner_weight.shape[1],), size)
            hidden = after(hidden, wu0)
    wu = (wu0, swap_core(wu0))
    layer_out, second_delta, feed_delta, second_sums = outer_block(
        hidden, cotangent, act, wu, vecs
    )

    def product(left, right):
        other = dot(left, right[1], TN).astype(bf16)
        other = swap_core(other)
        return dot(left, right[0], TN).astype(bf16), other

    gu = product(feed_delta, act)
    feed_delta, *gu = lax.optimization_barrier((feed_delta, *gu))
    inner_delta = [None, None]
    for t in (1, 0):
        inner_delta[t] = (dot(feed_delta, wu[t], NN) * slope[t].astype(f32)).astype(bf16)
    gi = product(hidden, inner_delta)
    inner_delta[0], inner_delta[1], *gi = lax.optimization_barrier((*inner_delta, *gi))
    if fast:
        parts_u = split_cols([gu, gi], index, size, 2 * step)
        first_u = corner_back(parts_u, size)
        inner_delta[0], inner_delta[1] = [after(d, parts_u[4]) for d in inner_delta]
    first_delta, branch_delta, first_sums, inner_sums = inner_back(
        second_delta, inner_delta, first_in, wi, vecs
    )
    go = product(branch_delta, ctx)
    ctx_delta = [dot(branch_delta, wo[t], NN).astype(bf16) for t in range(2)]

    def joined(pair):
        return jnp.where(
            core == 0, jnp.concatenate(pair, 1), jnp.concatenate(pair[::-1], 1)
        )

    if fast:
        table = pack_table(first_sums, second_sums, inner_sums, core, size, half)
        parts_i = split_cols([go], index, size, step)
        first_i = corner_back(parts_i, size)
        *first_u, ctx_delta[1], _ = lax.optimization_barrier(
            (*first_u, ctx_delta[1], parts_i[4])
        )
        sums_u = corner_add(parts_u, first_u)
        got_u = near_back(sums_u, size)
        ctx_delta[1] = after(ctx_delta[1], table, sums_u[0])

    def attend_back(t):
        return attend_call(
            attend_backward_kernel,
            lens,
            (q[t], k[t], v[t], ctx_delta[t], ctx[t]),
            (lse[t],),
            seq_count,
        )

    deltas = [None, None]
    deltas[1] = attend_back(1)
    if fast:
        arrived = lax.optimization_barrier((*first_i, *got_u, deltas[1]))
        first_i, got_u, deltas[1] = arrived[:2], arrived[2:4], arrived[4]
        last_u = near_add(parts_u[4], first_u, got_u)
        got_u = far_back(last_u, size)
        sums_i = corner_add(parts_i, first_i)
        got_i = near_back(sums_i, size)
        deltas[1] = after(deltas[1], last_u[0], sums_i[0])
        others, other_sums = gradients_other(tokens_t, deltas[1])
        *got_i, others = lax.optimization_barrier((*got_i, others))
        last_i = near_add(parts_i[4], first_i, got_i)
        others = swap_core(others)
        ctx_delta[0] = after(ctx_delta[0], last_i[0])
        deltas[0] = attend_back(0)
        parts_q = gradients_own(
            tokens_t,
            deltas[0],
            others,
            other_sums,
            table,
            index,
            core,
            size,
            query_bias.shape[0],
        )
        *got_u, own = lax.optimization_barrier((*got_u, parts_q[4]))
        parts_q = [*parts_q[:4], own]
        first_q = corner_back(parts_q, size)
        token_grad = token_gradient(
            after(first_delta, parts_q[4]), [after(d, parts_q[4]) for d in deltas], wqkv, 0, 2
        )
        got_i = far_back([after(item, parts_q[4]) for item in last_i], size)
        arrived = lax.optimization_barrier((*first_q, *got_i, token_grad))
        first_q, got_i, token_grad = arrived[:2], arrived[2:5], arrived[5]

        def total(last, got):
            return last[0] + got[0].astype(f32) + got[1].astype(f32) + got[2].astype(f32)

        out_ui = total(last_u, got_u)
        hidden_half = out_ui.shape[1] // 2
        out_gu = out_ui[:, :hidden_half].T
        out_gi = out_ui[:, hidden_half:]
        out_go = total(last_i, got_i).T
        sums_q = corner_add(parts_q, first_q)
        got_q = near_back(sums_q, size)
        last_q = near_add(parts_q[4], first_q, got_q)
        got_q = far_back(last_q, size)
        token_grad = token_gradient(token_grad, [after(d, last_q[0]) for d in deltas], wqkv, 1, 2)
        out_q = total(last_q, got_q)
        n = query_weight.shape[0]
        out_qkv = [out_q[g * n : (g + 1) * n] for g in range(3)]
        vec = out_q[3 * n :]
        vec = vec + swap_core(vec)
        vec_out = [vec[i, : item.shape[0]] for i, item in enumerate(vectors)]
    else:
        deltas[0] = attend_back(0)
        token_grad = token_gradient(first_delta, deltas, wqkv, 0, 1)

        def reduce(pair, order):
            summed = (pair[0].astype(f32) + pair[1].astype(f32)).astype(bf16)
            return scatter_rows(summed, order, size, index)

        out_gu = reduce(gu, orders[1]).T
        out_gi = reduce(gi, orders[0])
        out_go = reduce(go, orders[2]).T
        out_qkv = [
            reduce(product(tokens, [d[g] for d in deltas]), order) for g, order in enumerate(orders)
        ]
        bias_grads = [
            joined([jnp.sum(d[g].astype(f32), axis=0, keepdims=True) for d in deltas]) for g in (0, 2)
        ]
        bias_grads += [s[i : i + 1] for s in (first_sums, second_sums) for i in range(3)]
        bias_grads.append(joined(jnp.split(inner_sums[:1], 2, 1)))
        packed = jnp.concatenate([item.reshape(size, -1) for item in bias_grads], axis=1)
        packed = packed + swap_core(packed)
        own = scatter_rows(packed, orders[0], size, index).reshape(-1)
        vec_out = [own[a:b] for a, b in zip(bounds[:-1], bounds[1:])]
    return (
        layer_out,
        token_grad,
        out_qkv[0],
        out_qkv[1],
        out_qkv[2],
        out_go,
        vec_out[0],
        vec_out[1],
        vec_out[2],
        vec_out[3],
        vec_out[4],
        out_gi,
        vec_out[8],
        out_gu,
        vec_out[5],
        vec_out[6],
        vec_out[7],
    )


def solution(mesh):
    both = P(("dp", "tensor"), None)
    cols = P("dp", "tensor")
    rows = P("tensor", "dp")
    vec = P("dp")
    in_specs = (
        both, both, vec, cols, cols, cols, rows, vec, vec, vec, vec, vec, cols, vec, rows, vec, vec, vec,
    )
    out_specs = (
        both, both, cols, cols, cols, rows, vec, vec, vec, vec, vec, cols, vec, rows, vec, vec, vec,
    )
    return jax.shard_map(
        on_device, mesh=mesh, in_specs=in_specs, out_specs=out_specs, check_vma=False
    )
```

```python
import jax
import jax.numpy as jnp
from jax import lax
from jax.experimental import pallas as pl
from jax.experimental.pallas import tpu as pltpu
from jax.sharding import PartitionSpec as P

HD = 64
norm_eps = 1e-12
masked_score = -1000000000.0
score_scale = HD ** (-0.5)
f32 = jnp.float32
bf16 = jnp.bfloat16
NT = (((1,), (1,)), ((), ()))
TN = (((0,), (0,)), ((), ()))
NN = (((1,), (0,)), ((), ()))
ROWS = 256


def dot(left, right, dims):
    return lax.dot_general(left, right, dims, preferred_element_type=f32)


def stage_orders(size):
    up = [1 << k for k in range(size.bit_length() - 1)]
    down = up[::-1]
    return (down, down[:-2] + [down[-1], down[-2]], [down[0]] + up[:-1])


def swap_dp(value, mask, size):
    return lax.ppermute(value, "dp", [(i, i ^ mask) for i in range(size)])


def swap_core(value):
    return lax.ppermute(value, "tensor", [(0, 1), (1, 0)])


def after(value, *others):
    return lax.optimization_barrier((value, *others))[0]


def gather_rows(shard, order, size, index):
    rows, cols = shard.shape
    have = []
    buf = shard
    for mask in order:
        received = swap_dp(buf, mask, size)
        have = sorted(have + [mask], reverse=True)
        axis = have.index(mask)
        buf = jnp.where(
            (index & mask) != 0,
            jnp.stack([received, buf], axis),
            jnp.stack([buf, received], axis),
        )
    return buf.reshape(size * rows, cols)


def scatter_rows(own, order, size, index):
    total, cols = own.shape
    have = sorted(order, reverse=True)
    buf = own.reshape([2] * len(have) + [total // size, cols])
    for mask in order[::-1]:
        axis = have.index(mask)
        bit = ((index & mask) != 0).astype(jnp.int32)
        keep = lax.dynamic_index_in_dim(buf, bit, axis, keepdims=False)
        give = lax.dynamic_index_in_dim(buf, 1 - bit, axis, keepdims=False)
        received = swap_dp(give, mask, size)
        buf = keep.astype(f32) + received.astype(f32)
        have.remove(mask)
        if have:
            buf = buf.astype(own.dtype)
    return buf


BLOCK = 512
PART = 128
HINT = pl.CostEstimate(flops=1, transcendentals=0, bytes_accessed=1)


def distance_of(piece, k):
    return (4 * (piece % 2) + 8 * k) ^ piece // 2


def vmem(shape):
    return pl.BlockSpec(shape, lambda *_: (0,) * len(shape))


def pack_first(weights, vectors):
    rows, cols = weights[0].shape
    count = len(weights)

    def kernel(*refs):
        ins, out_ref, table = refs[: count + len(vectors)], refs[-2], refs[-1]
        for g in range(count):
            out_ref[g * rows : (g + 1) * rows, :] = ins[g][...]
        table[...] = jnp.zeros(table.shape, f32)
        for i, ref in enumerate(ins[count:]):
            table[i : i + 1, : ref.shape[1]] = ref[...].astype(f32)
        out_ref[count * rows :, :] = table[...].astype(bf16)

    return pl.pallas_call(
        kernel,
        out_shape=jax.ShapeDtypeStruct((count * rows + 16, cols), bf16),
        scratch_shapes=[pltpu.VMEM((16, cols), f32)],
        cost_estimate=HINT,
    )(*weights, *[item.reshape(1, -1) for item in vectors])


def place_first(pieces, index, count, size, lengths):
    total_rows, cols = pieces[0].shape[1:]
    rows = (total_rows - 16) // count

    def kernel(index_ref, *refs):
        ins = refs[: len(pieces)]
        w_ref, v_ref, last_ref, table = refs[len(pieces) :]
        for n, ref in enumerate(ins):
            for k in range(ref.shape[0]):
                block = index_ref[0] ^ distance_of(n, k)
                at = pl.ds(pl.multiple_of(block * rows, 16), rows)
                for g in range(count):
                    w_ref[g, at, :] = ref[k, g * rows : (g + 1) * rows, :]
                table[block] = ref[k, count * rows :, :].astype(f32)
        one, last = lengths
        for c in range(size):
            v_ref[:, c * one : (c + 1) * one] = table[c][:, :one]
            last_ref[:, c * last : (c + 1) * last] = table[c][8:9, :last]

    out = [(count, size * rows, cols), (16, size * lengths[0]), (1, size * lengths[1])]
    return pl.pallas_call(
        kernel,
        out_shape=[jax.ShapeDtypeStruct(o, d) for o, d in zip(out, (bf16, f32, f32))],
        grid_spec=pltpu.PrefetchScalarGridSpec(
            num_scalar_prefetch=1,
            grid=(1,),
            in_specs=[vmem(p.shape) for p in pieces],
            out_specs=[vmem(o) for o in out],
            scratch_shapes=[pltpu.VMEM((size, 16, cols), f32)],
        ),
        cost_estimate=HINT,
    )(index[None], *pieces)


def place_cols(pieces, index, widths, size):
    rows = pieces[0].shape[1]

    def kernel(index_ref, *refs):
        ins, outs = refs[: len(pieces)], refs[len(pieces) :]
        for n, ref in enumerate(ins):
            for k in range(ref.shape[0]):
                block = index_ref[0] ^ distance_of(n, k)
                at = 0
                for out_ref, width in zip(outs, widths):
                    here = pl.ds(pl.multiple_of(block * rows, 16), rows)
                    out_ref[here, :] = ref[k, :, at : at + width]
                    at += width

    out = [(size * rows, w) for w in widths]
    return pl.pallas_call(
        kernel,
        out_shape=[jax.ShapeDtypeStruct(o, bf16) for o in out],
        grid_spec=pltpu.PrefetchScalarGridSpec(
            num_scalar_prefetch=1,
            grid=(1,),
            in_specs=[vmem(p.shape) for p in pieces],
            out_specs=[vmem(o) for o in out],
        ),
        cost_estimate=HINT,
    )(index[None], *pieces)


PARTS = (
    ((3, (0, 1)), (1, (0, 1))),
    ((3, (2, 3)), (2, (2, 3))),
    ((1, (2, 3)),),
    ((2, (0, 1)),),
    ((0, (0, 1, 2, 3)),),
)


def split_out_specs(rows, step):
    return [
        pl.BlockSpec((sum(len(ks) for _, ks in part), rows, step), lambda i, *_: (0, 0, i))
        for part in PARTS
    ]


def split_shapes(rows, cols):
    return [
        jax.ShapeDtypeStruct(
            (sum(len(ks) for _, ks in part), rows, cols), bf16
        )
        for part in PARTS
    ]


def split_cols(pairs, index, size, step):
    total = pairs[0][0].shape[0]
    rows = total // size
    counts = [a.shape[1] // step for a, _ in pairs]
    starts = [sum(counts[:i]) for i in range(len(counts))]

    def kernel(index_ref, *refs):
        ins, outs = refs[: 2 * len(pairs)], refs[2 * len(pairs) :]
        for n, (first, count) in enumerate(zip(starts, counts)):

            @pl.when((pl.program_id(0) >= first) & (pl.program_id(0) < first + count))
            def _(n=n):
                for part, out_ref in zip(PARTS, outs):
                    at = 0
                    for offset, ks in part:
                        for k in ks:
                            block = index_ref[0] ^ (4 * k ^ offset)
                            here = pl.ds(pl.multiple_of(block * rows, 16), rows)
                            out_ref[at] = ins[2 * n][here, :] + ins[2 * n + 1][here, :]
                            at += 1

    specs = []
    for a, n in zip(starts, counts):
        spec = pl.BlockSpec((total, step), lambda i, *_, a=a, n=n: (0, jnp.clip(i - a, 0, n - 1)))
        specs += [spec, spec]
    return pl.pallas_call(
        kernel,
        out_shape=split_shapes(rows, sum(counts) * step),
        grid_spec=pltpu.PrefetchScalarGridSpec(
            num_scalar_prefetch=1,
            grid=(sum(counts),),
            in_specs=specs,
            out_specs=split_out_specs(rows, step),
        ),
        cost_estimate=HINT,
    )(index[None], *[item for pair in pairs for item in pair])


def gradients_other(tokens_t, deltas):
    width, rows = tokens_t.shape
    count, _, cols = deltas.shape

    def kernel(t_ref, d_ref, o_ref, s_ref):
        o_ref[0] = dot(t_ref[...], d_ref[0], NN).astype(bf16)
        s_ref[0] = dot(jnp.ones((8, rows), bf16), d_ref[0], NN)

    return pl.pallas_call(
        kernel,
        out_shape=[
            jax.ShapeDtypeStruct((count, width, cols), bf16),
            jax.ShapeDtypeStruct((count, 8, cols), f32),
        ],
        grid=(count,),
        in_specs=[vmem(tokens_t.shape), pl.BlockSpec((1, rows, cols), lambda g: (g, 0, 0))],
        out_specs=[
            pl.BlockSpec((1, width, cols), lambda g: (g, 0, 0)),
            pl.BlockSpec((1, 8, cols), lambda g: (g, 0, 0)),
        ],
        cost_estimate=HINT,
    )(tokens_t, deltas)


def gradients_own(
    tokens_t, deltas, others, other_sums, ready, table, index, core, size, one
):
    width, rows = tokens_t.shape
    count, _, cols = deltas.shape
    part_rows = width // size
    height = (count + 1) * part_rows + 16

    def kernel(at_ref, t_ref, d_ref, other_ref, sums_ref, r0_ref, r1_ref, table_ref, *refs):
        outs, total, own_sums, vec = refs[: len(PARTS)], refs[-3], refs[-2], refs[-1]
        g = pl.program_id(0)
        total[...] = dot(t_ref[...], d_ref[0], NN) + other_ref[0].astype(f32)
        own_sums[g] = dot(jnp.ones((8, rows), bf16), d_ref[0], NN)

        def blocks():
            for part, out_ref in zip(PARTS, outs):
                at = 0
                for offset, ks in part:
                    for k in ks:
                        yield at_ref[0] ^ (4 * k ^ offset), out_ref, at
                        at += 1

        for block, out_ref, at in blocks():
            value = total[pl.ds(pl.multiple_of(block * part_rows, 16), part_rows), :]
            out_ref[at, pl.ds(pl.multiple_of(g * part_rows, 16), part_rows), :] = value.astype(bf16)

        @pl.when(g == count - 1)
        def _():
            vec[...] = table_ref[...]
            for row, which in ((0, 0), (1, 2)):
                for ref, side in ((own_sums, 0), (sums_ref, 1)):
                    first = (at_ref[1] ^ side) * (size // 2)
                    for j in range(size // 2):
                        vec[first + j, row : row + 1, :one] = ref[which, 0:1, j * one : (j + 1) * one]
            for block, out_ref, at in blocks():
                here = pl.ds(pl.multiple_of(block * part_rows, 16), part_rows)
                value = r0_ref[here, :] + r1_ref[here, :]
                out_ref[at, count * part_rows : (count + 1) * part_rows, :] = value
                out_ref[at, (count + 1) * part_rows :, :] = vec[block].astype(bf16)

    return pl.pallas_call(
        kernel,
        out_shape=split_shapes(height, cols),
        grid_spec=pltpu.PrefetchScalarGridSpec(
            num_scalar_prefetch=1,
            grid=(count,),
            in_specs=[
                vmem(tokens_t.shape),
                pl.BlockSpec((1, rows, cols), lambda g, *_: (g, 0, 0)),
                pl.BlockSpec((1, width, cols), lambda g, *_: (g, 0, 0)),
                vmem(other_sums.shape),
                *[vmem(a.shape) for a in ready],
                vmem(table.shape),
            ],
            out_specs=[vmem(shape.shape) for shape in split_shapes(height, cols)],
            scratch_shapes=[
                pltpu.VMEM((width, cols), f32),
                pltpu.VMEM((count, 8, cols), f32),
                pltpu.VMEM(table.shape, f32),
            ],
        ),
        cost_estimate=HINT,
    )(jnp.stack([index, core]), tokens_t, deltas, others, other_sums, *ready, table)


def pack_table(first_sums, second_sums, inner_sums, core, size, cols):
    one = first_sums.shape[1] // size
    end = inner_sums.shape[1] // size

    def kernel(core_ref, a_ref, b_ref, inner_ref, out_ref, table):
        table[...] = jnp.zeros(table.shape, f32)
        out_ref[...] = jnp.zeros(out_ref.shape, f32)
        table[2:5, :] = a_ref[0:3, :]
        table[5:8, :] = b_ref[0:3, :]
        for c in range(size):
            out_ref[c, :, :one] = table[:, c * one : (c + 1) * one]
            d = (c + size // 2) % size
            here = inner_ref[0:1, c * end : (c + 1) * end]
            there = inner_ref[0:1, d * end : (d + 1) * end]
            out_ref[c, 8:9, :end] = jnp.where(core_ref[0] == 0, here, there)

    ins = (first_sums, second_sums, inner_sums)
    return pl.pallas_call(
        kernel,
        out_shape=jax.ShapeDtypeStruct((size, 16, cols), f32),
        grid_spec=pltpu.PrefetchScalarGridSpec(
            num_scalar_prefetch=1,
            grid=(1,),
            in_specs=[vmem(a.shape) for a in ins],
            out_specs=vmem((size, 16, cols)),
            scratch_shapes=[pltpu.VMEM((16, first_sums.shape[1]), f32)],
        ),
        cost_estimate=HINT,
    )(core[None], *ins)


def whole_call(kernel, outs, ins, blocks):
    return pl.pallas_call(
        kernel,
        out_shape=[jax.ShapeDtypeStruct(o, d) for o, d in outs],
        grid=(1,),
        in_specs=[vmem((n, *a.shape[1:])) for a, n in zip(ins, blocks)],
        out_specs=[vmem(o) for o, _ in outs],
        cost_estimate=HINT,
    )(*ins)


def corner_back(parts, size):
    return swap_dp(parts[0], 1, size), swap_dp(parts[1], 2, size)


def corner_add(parts, got):
    keep = parts[2:4]

    def kernel(one_ref, two_ref, r1_ref, r2_ref, o1_ref, o2_ref):
        o1_ref[...] = one_ref[...] + r2_ref[...]
        o2_ref[...] = two_ref[...] + r1_ref[...]

    return whole_call(
        kernel, [(item.shape, bf16) for item in keep], [*keep, *got], (2, 2, 2, 2)
    )


def near_back(sums, size):
    return swap_dp(sums[0], 1, size), swap_dp(sums[1], 2, size)


def near_add(own, first, got):
    def kernel(own_ref, f1_ref, f2_ref, r1_ref, r2_ref, keep_ref, *outs):
        def total(k):
            early = f1_ref[2 + k] if k < 2 else f2_ref[k]
            late = r2_ref[k] if k < 2 else r1_ref[k - 2]
            return own_ref[k].astype(f32) + early.astype(f32) + late.astype(f32)

        keep_ref[...] = total(0)
        for k in (1, 2, 3):
            outs[k - 1][...] = total(k).astype(bf16)

    shape = own.shape[1:]
    return whole_call(
        kernel, [(shape, f32)] + [(shape, bf16)] * 3, [own, *first, *got], (4, 4, 4, 2, 2)
    )


def far_back(sums, size):
    return [swap_dp(item, 4 * (k + 1), size) for k, item in enumerate(sums[1:])]


def project(tokens, weights, vectors, core, side):
    rows, width = tokens.shape
    cols = weights.shape[2]

    def kernel(core_ref, x_ref, w_ref, v_ref, q_out, k_out, v_out):
        half = core_ref[0] ^ side
        bias = jnp.where(half == 0, v_ref[0:8, :cols], v_ref[0:8, cols:])
        x = x_ref[...]
        q_out[...] = (dot(x, w_ref[0], NN) + bias[0:1]).astype(bf16)
        k_out[...] = dot(x, w_ref[1], NN).astype(bf16)
        v_out[...] = (dot(x, w_ref[2], NN) + bias[1:2]).astype(bf16)

    tile = pl.BlockSpec((ROWS, cols), lambda i, *_: (i, 0))
    return pl.pallas_call(
        kernel,
        out_shape=[jax.ShapeDtypeStruct((rows, cols), bf16)] * 3,
        grid_spec=pltpu.PrefetchScalarGridSpec(
            num_scalar_prefetch=1,
            grid=(rows // ROWS,),
            in_specs=[
                pl.BlockSpec((ROWS, width), lambda i, *_: (i, 0)),
                vmem(weights.shape),
                vmem(vectors.shape),
            ],
            out_specs=[tile] * 3,
        ),
        cost_estimate=HINT,
    )(core[None], tokens, weights, vectors)


def token_gradient(first_delta, deltas, weights, part, parts):
    count, rows, cols = deltas[0].shape
    width = weights[0].shape[1]
    steps = rows // BLOCK // parts

    def kernel(f_ref, d0_ref, d1_ref, w0_ref, w1_ref, *refs):
        o_ref = refs[-1]
        total = f_ref[...]
        for d_ref, w_ref in ((d0_ref, w0_ref), (d1_ref, w1_ref)):
            for g in range(count):
                total = total + dot(d_ref[g], w_ref[g], NT)
        o_ref[...] = total

    tile = pl.BlockSpec((BLOCK, width), lambda i: (i + part * steps, 0))
    delta_part = pl.BlockSpec((count, BLOCK, cols), lambda i: (0, i + part * steps, 0))
    return pl.pallas_call(
        kernel,
        out_shape=jax.ShapeDtypeStruct((rows, width), f32),
        grid=(steps,),
        in_specs=[tile, delta_part, delta_part] + [vmem(weights[0].shape)] * 2,
        out_specs=tile,
        input_output_aliases={0: 0},
        cost_estimate=pl.CostEstimate(
            flops=4 * count * rows * width * cols // parts,
            transcendentals=0,
            bytes_accessed=16 * rows * cols // parts,
        ),
    )(first_delta, *deltas, *weights)


def center(values):
    mean = jnp.mean(values, axis=-1, keepdims=True)
    centred = values - mean
    var = jnp.mean(centred * centred, axis=-1, keepdims=True)
    rinv = lax.rsqrt(var + norm_eps)
    return centred * rinv, rinv


def norm_back(grad, normed, rinv, gain):
    scaled = grad * gain
    return rinv * (
        scaled
        - jnp.mean(scaled, axis=-1, keepdims=True)
        - normed * jnp.mean(scaled * normed, axis=-1, keepdims=True)
    )


def add_rows(ref, items):
    for i, item in enumerate(items):
        ref[i : i + 1, : item.shape[1]] += jnp.sum(item, axis=0, keepdims=True)


def clear(*refs):
    @pl.when(pl.program_id(0) == 0)
    def _():
        for ref in refs:
            ref[...] = jnp.zeros(ref.shape, f32)


def in_parts(total, finish):
    def body(i, carry):
        at = pl.ds(pl.multiple_of(i * PART, PART), PART)
        finish(at, total[at, :])
        return carry

    lax.fori_loop(0, BLOCK // PART, body, 0)


def row_call(kernel, tiles, wholes, outs, sums):
    rows = tiles[0].shape[0]

    def tile(cols):
        return pl.BlockSpec((BLOCK, cols), lambda i: (i, 0))

    return pl.pallas_call(
        kernel,
        out_shape=[jax.ShapeDtypeStruct((rows, n), d) for n, d in outs]
        + [jax.ShapeDtypeStruct((8, n), f32) for n in sums],
        grid=(rows // BLOCK,),
        in_specs=[tile(a.shape[1]) for a in tiles] + [vmem(a.shape) for a in wholes],
        out_specs=[tile(n) for n, _ in outs] + [vmem((8, n)) for n in sums],
        scratch_shapes=[pltpu.VMEM((BLOCK, outs[0][0]), f32)],
        cost_estimate=HINT,
    )(*tiles, *wholes)


def first_block(tokens, context, weights, vectors):
    def kernel(x_ref, c0_ref, c1_ref, w0_ref, w1_ref, v_ref, out, low, products):
        products[...] = dot(c0_ref[...], w0_ref[...], NT) + dot(c1_ref[...], w1_ref[...], NT)

        def finish(at, total):
            total = x_ref[at, :].astype(f32) + total + v_ref[2:3]
            out[at, :] = total
            low[at, :] = (center(total)[0] * v_ref[3:4] + v_ref[4:5]).astype(bf16)

        in_parts(products, finish)

    width = tokens.shape[1]
    return row_call(
        kernel, [tokens, *context], [*weights, vectors], [(width, f32), (width, bf16)], ()
    )


def outer_block(hidden, cotangent, act, weights, vectors):
    def kernel(
        h_ref, c_ref, a0_ref, a1_ref, w0_ref, w1_ref, v_ref, out, delta, low, sums, products
    ):
        clear(sums)

        products[...] = dot(a0_ref[...], w0_ref[...], NT) + dot(a1_ref[...], w1_ref[...], NT)

        def finish(at, feed):
            normed, rinv = center(h_ref[at, :].astype(f32) + (v_ref[5:6] + feed))
            out[at, :] = normed * v_ref[6:7] + v_ref[7:8]
            cot = c_ref[at, :].astype(f32)
            found = norm_back(cot, normed, rinv, v_ref[6:7])
            delta[at, :] = found
            low[at, :] = found.astype(bf16)
            add_rows(sums, (found, cot * normed, cot))

        in_parts(products, finish)

    width = hidden.shape[1]
    return row_call(
        kernel,
        [hidden, cotangent, *act],
        [*weights, vectors],
        [(width, f32), (width, f32), (width, bf16)],
        (width,),
    )


def inner_back(second_delta, inner_delta, first_in, weights, vectors):
    def kernel(
        s_ref, d0_ref, d1_ref, f_ref, w0_ref, w1_ref, v_ref, delta, low, sums, inner, products
    ):
        clear(sums, inner)
        ones = jnp.ones((8, BLOCK), bf16)
        half = d0_ref.shape[1]
        inner[:, :half] += dot(ones, d0_ref[...], NN)
        inner[:, half:] += dot(ones, d1_ref[...], NN)

        products[...] = dot(d0_ref[...], w0_ref[...], NT) + dot(d1_ref[...], w1_ref[...], NT)

        def finish(at, grad):
            grad = s_ref[at, :] + grad
            normed, rinv = center(f_ref[at, :])
            found = norm_back(grad, normed, rinv, v_ref[3:4])
            delta[at, :] = found
            low[at, :] = found.astype(bf16)
            add_rows(sums, (found, grad * normed, grad))

        in_parts(products, finish)

    width = first_in.shape[1]
    return row_call(
        kernel,
        [second_delta, *inner_delta, first_in],
        [*weights, vectors],
        [(width, f32), (width, bf16)],
        (width, 2 * inner_delta[0].shape[1]),
    )


def three_parts(row):
    high = row.astype(bf16).astype(f32)
    middle = (row - high).astype(bf16).astype(f32)
    return [high, middle, row - high - middle]


def extra_lanes(shape, keys_valid):
    lane = lax.broadcasted_iota(jnp.int32, shape, 1) % HD
    row = lax.broadcasted_iota(jnp.int32, shape, 0)
    bias = jnp.where(row < keys_valid, 0.0, masked_score)
    return jnp.where(lane == 0, bias, jnp.where(lane < 4, 1.0, 0.0)).astype(bf16)


def extra_rows(first, row, length):
    rows = [jnp.full((1, length), first, f32)]
    rows += three_parts(row) if row is not None else []
    rows.append(jnp.zeros((16 - len(rows), length), f32))
    return jnp.concatenate(rows, 0).astype(bf16)


def with_rows(own_t, h, first, row):
    length = own_t.shape[1]
    own = own_t[h * HD : (h + 1) * HD]
    rest = [extra_rows(first, row, length), jnp.zeros((HD - 16, length), bf16)]
    return jnp.concatenate([own] + rest if h == 0 else rest + [own], 0)


def attend_forward_kernel(lens, q_ref, k_ref, v_ref, ctx_ref, lse_ref):
    seq_len, lanes = q_ref.shape
    lane = lax.broadcasted_iota(jnp.int32, (seq_len, lanes), 1)
    extra = extra_lanes((seq_len, lanes), lens[pl.program_id(0)])
    ones = jnp.ones((16, seq_len), bf16)
    loaded = {}

    def scores(h):
        if h == 0:
            query_t = (q_ref[...] * jnp.bfloat16(score_scale)).T
            loaded[0] = (query_t, k_ref[...], v_ref[...].T)
        query_t, keys, _ = loaded[0]
        return dot(jnp.where(lane // HD == h, keys, extra), with_rows(query_t, h, 1.0, None), NN)

    pieces = []
    ahead = scores(0)
    for h in range(2):
        now = ahead
        if h == 0:
            ahead = scores(1)
        top = jnp.max(now, axis=0, keepdims=True)
        expo = jnp.exp(now - top).astype(bf16)
        value_t = loaded[0][2][h * HD : (h + 1) * HD]
        found = dot(jnp.concatenate([value_t, ones], 0), expo, NN)
        total = found[HD : HD + 1]
        pieces.append(found[:HD] / total)
        lse_ref[0, 0, h : h + 1, :] = top + jnp.log(total)
        if h == 1:
            ctx_ref[...] = jnp.concatenate(pieces, 0).T.astype(bf16)
            pieces = []


def attend_backward_kernel(lens, q_ref, k_ref, v_ref, d_ref, c_ref, lse_ref, out_ref):
    seq_len, lanes = q_ref.shape
    lane = lax.broadcasted_iota(jnp.int32, (seq_len, lanes), 1)
    extra = extra_lanes((seq_len, lanes), lens[pl.program_id(0)])
    loaded = {}

    def products(h):
        if h == 0:
            query = q_ref[...] * jnp.bfloat16(score_scale)
            delta = d_ref[...]
            delta_t = delta.T
            inner = delta_t.astype(f32) * c_ref[...].T.astype(f32)
            keys = k_ref[...]
            loaded[0] = (query, query.T, delta, delta_t, inner, keys, keys.T, v_ref[...])
        _, query_t, _, delta_t, inner, keys, _, values = loaded[0]
        own = lane // HD == h
        inner = jnp.sum(inner[h * HD : (h + 1) * HD], axis=0, keepdims=True)
        lse = lse_ref[0, 0, h : h + 1, :]
        logs = dot(jnp.where(own, keys, extra), with_rows(query_t, h, 1.0, -lse), NN)
        centred = dot(jnp.where(own, values, extra), with_rows(delta_t, h, 0.0, -inner), NN)
        return logs, centred

    ahead = products(0)
    for h in range(2):
        logs, centred = ahead
        if h == 0:
            ahead = products(1)
        query, _, delta, _, _, _, keys_t, _ = loaded[0]
        probs = jnp.exp(logs)
        score_delta = (probs * centred).astype(bf16)
        own = lane // HD == h
        part_v = dot(probs.astype(bf16), jnp.where(own, delta, jnp.bfloat16(0)), NN)
        part_k = dot(score_delta, jnp.where(own, query, jnp.bfloat16(0)), NN)
        part_q = dot(keys_t[h * HD : (h + 1) * HD], score_delta, NN)
        if h == 0:
            dv, dk, dq = part_v, part_k, part_q
        else:
            out_ref[0] = (jnp.concatenate([dq, part_q], 0).T * score_scale).astype(bf16)
            out_ref[1] = (dk + part_k).astype(bf16)
            out_ref[2] = (dv + part_v).astype(bf16)


def attend_call(kernel, lens, operands, lse_in, seq_count):
    rows, cols = operands[0].shape
    seq_len = rows // seq_count
    pairs = cols // (2 * HD)
    tile = pl.BlockSpec((seq_len, 2 * HD), lambda s, p, *_: (s, p))
    stat = pl.BlockSpec((1, 1, 2, seq_len), lambda s, p, *_: (s, p, 0, 0))
    if lse_in:
        out_shape = jax.ShapeDtypeStruct((3, rows, cols), bf16)
        out_specs = pl.BlockSpec((3, seq_len, 2 * HD), lambda s, p, *_: (0, s, p))
    else:
        out_shape = [
            jax.ShapeDtypeStruct((rows, cols), bf16),
            jax.ShapeDtypeStruct((seq_count, pairs, 2, seq_len), f32),
        ]
        out_specs = [tile, stat]
    return pl.pallas_call(
        kernel,
        out_shape=out_shape,
        grid_spec=pltpu.PrefetchScalarGridSpec(
            num_scalar_prefetch=1,
            grid=(seq_count, pairs),
            in_specs=[tile] * len(operands) + [stat] * len(lse_in),
            out_specs=out_specs,
        ),
        cost_estimate=HINT,
    )(lens, *operands, *lse_in)


def on_device(
    tokens,
    cotangent,
    lengths,
    query_weight,
    key_weight,
    value_weight,
    out_weight,
    query_bias,
    value_bias,
    out_bias,
    first_gain,
    first_shift,
    inner_weight,
    inner_bias,
    outer_weight,
    outer_bias,
    second_gain,
    second_shift,
):
    size = lax.axis_size("dp")
    index = lax.axis_index("dp")
    core = lax.axis_index("tensor")
    orders = stage_orders(size)
    seq_count = lengths.shape[0] // 2
    lens = lax.dynamic_slice_in_dim(lengths, core * seq_count, seq_count, 0)
    fast = size == 16 and query_weight.shape[0] % 16 == 0
    half = query_weight.shape[1]
    step = half

    vectors = (
        query_bias,
        value_bias,
        out_bias,
        first_gain,
        first_shift,
        outer_bias,
        second_gain,
        second_shift,
        inner_bias,
    )
    bounds = [0]
    for item in vectors:
        bounds.append(bounds[-1] + item.shape[0])
    projections = (query_weight, key_weight, value_weight)
    out_t = out_weight.T
    outer_t = outer_weight.T

    if fast:
        shard = pack_first(projections, vectors)
        far = [swap_dp(shard, d, size) for d in (8, 4, 12)]
        low, high = jnp.stack([shard, far[0]]), jnp.stack(far[1:])
        two_low, one_high = swap_dp(low, 2, size), swap_dp(high, 1, size)
        one_low, two_high = swap_dp(low, 1, size), swap_dp(high, 2, size)
        shard_a = jnp.concatenate([out_t, inner_weight], 1)
        far_a = swap_dp(after(shard_a, low, high), 8, size)
        tokens_t = tokens.T
        pieces = [low, high, one_low, one_high, two_low, two_high]
        pieces += [swap_dp(two_low, 1, size), swap_dp(one_high, 2, size)]
        far_a, *pieces, tokens_t = lax.optimization_barrier((far_a, *pieces, tokens_t))
        low_a = jnp.stack([shard_a, far_a])
        high_a = swap_dp(low_a, 4, size)
        two_low_a, one_low_a = swap_dp(low_a, 2, size), swap_dp(low_a, 1, size)
        wqkv0, vecs, ib = place_first(
            pieces, index, 3, size, (query_bias.shape[0], inner_bias.shape[0])
        )
    else:
        own_vec = jnp.concatenate(vectors)[None, :]
        all_vec = gather_rows(own_vec, orders[0], size, index).astype(f32)
        found = [all_vec[:, a:b].reshape(1, -1) for a, b in zip(bounds[:-1], bounds[1:])]
        vecs = jnp.concatenate(found[:-1] + [jnp.zeros_like(found[0])] * 8, 0)
        ib = found[-1]
        wqkv0 = jnp.stack(
            [gather_rows(w, o, size, index) for w, o in zip(projections, orders)]
        )
        wo0 = gather_rows(out_t, orders[2], size, index)
        wi0 = gather_rows(inner_weight, orders[0], size, index)
        wu0 = gather_rows(outer_t, orders[1], size, index)

    wqkv = (wqkv0, swap_core(wqkv0))
    hidden_half = inner_weight.shape[1]
    ib = (
        jnp.where(core == 0, ib[:, :hidden_half], ib[:, hidden_half:]),
        jnp.where(core == 0, ib[:, hidden_half:], ib[:, :hidden_half]),
    )

    q, k, v, ctx, lse = [], [], [], [], []
    for t in range(2):
        found = project(tokens, wqkv[t], vecs, core, t)
        if fast and t == 0:
            high_a, other, *found = lax.optimization_barrier((high_a, wqkv[1], *found))
            wqkv = (wqkv[0], other)
            one_high_a, two_high_a = swap_dp(high_a, 1, size), swap_dp(high_a, 2, size)
            far_b = swap_dp(after(outer_t, other), 8, size)
        q.append(found[0])
        k.append(found[1])
        v.append(found[2])
    if fast:
        far_b, one_low_a, two_low_a, *q = lax.optimization_barrier(
            (far_b, one_low_a, two_low_a, *q)
        )
        low_b = jnp.stack([outer_t, far_b])
        two_low_b, one_low_b = swap_dp(low_b, 2, size), swap_dp(low_b, 1, size)
        high_b = swap_dp(low_b, 4, size)
    for t in range(2):
        if fast and t == 1:
            q[1] = after(q[1], ctx[0])
        c, s = attend_call(attend_forward_kernel, lens, (q[t], k[t], v[t]), (), seq_count)
        lse.append(s)
        if fast and t == 0:
            pieces_a = [low_a, high_a, one_low_a, one_high_a, two_low_a, two_high_a]
            *pieces_a, high_b, two_low_b, one_low_b, c = lax.optimization_barrier(
                (*pieces_a, high_b, two_low_b, one_low_b, c)
            )
            pieces_a += [swap_dp(pieces_a[4], 1, size), swap_dp(pieces_a[3], 2, size)]
        if fast and t == 1:
            *pieces_a, c = lax.optimization_barrier((*pieces_a, c))
            one_high_b, two_high_b = swap_dp(high_b, 1, size), swap_dp(high_b, 2, size)
            pieces_b = [low_b, high_b, one_low_b, one_high_b, two_low_b, two_high_b]
            pieces_b.append(swap_dp(two_low_b, 1, size))
            wo0, wi0 = place_cols(pieces_a, index, (half, inner_weight.shape[1]), size)
        ctx.append(c)

    wo = (wo0, swap_core(wo0))
    wi = (wi0, swap_core(wi0))
    first_in, hidden = first_block(tokens, ctx, wo, vecs)
    if fast:
        *pieces_b, hidden = lax.optimization_barrier((*pieces_b, hidden))
        pieces_b.append(swap_dp(pieces_b[3], 2, size))
    act, slope = [], []
    for t in range(2):
        u = dot(hidden, wi[t], NN) + ib[t]
        cdf = 0.5 * (1.0 + lax.erf(u * (0.5**0.5)))
        act.append((u * cdf).astype(bf16))
        pdf = jnp.exp(-0.5 * u * u) * 0.3989422804014327
        slope.append((cdf + u * pdf).astype(bf16))
        if fast and t == 0:
            *pieces_b, act[0] = lax.optimization_barrier((*pieces_b, act[0]))
            (wu0,) = place_cols(pieces_b, index, (inner_weight.shape[1],), size)
            hidden = after(hidden, wu0)
    wu = (wu0, swap_core(wu0))
    layer_out, second_delta, feed_delta, second_sums = outer_block(
        hidden, cotangent, act, wu, vecs
    )

    def product(left, right):
        other = dot(left, right[1], TN).astype(bf16)
        other = swap_core(other)
        return dot(left, right[0], TN).astype(bf16), other

    gu = product(feed_delta, act)
    feed_delta, *gu = lax.optimization_barrier((feed_delta, *gu))
    inner_delta = [None, None]
    for t in (1, 0):
        inner_delta[t] = (dot(feed_delta, wu[t], NN) * slope[t].astype(f32)).astype(bf16)
    gi = product(hidden, inner_delta)
    inner_delta[0], inner_delta[1], *gi = lax.optimization_barrier((*inner_delta, *gi))
    if fast:
        parts_u = split_cols([gu, gi], index, size, 2 * step)
        first_u = corner_back(parts_u, size)
        inner_delta[0], inner_delta[1] = [after(d, parts_u[4]) for d in inner_delta]
    first_delta, branch_delta, first_sums, inner_sums = inner_back(
        second_delta, inner_delta, first_in, wi, vecs
    )
    go = list(product(branch_delta, ctx))
    ctx_delta = [dot(branch_delta, wo[t], NN).astype(bf16) for t in range(2)]

    def joined(pair):
        return jnp.where(
            core == 0, jnp.concatenate(pair, 1), jnp.concatenate(pair[::-1], 1)
        )

    if fast:
        table = pack_table(first_sums, second_sums, inner_sums, core, size, half)
        *first_u, ctx_delta[1], go[0], go[1] = lax.optimization_barrier(
            (*first_u, ctx_delta[1], *go)
        )
        sums_u = corner_add(parts_u, first_u)
        got_u = near_back(sums_u, size)
        ctx_delta[1] = after(ctx_delta[1], table, sums_u[0])

    def attend_back(t):
        return attend_call(
            attend_backward_kernel,
            lens,
            (q[t], k[t], v[t], ctx_delta[t], ctx[t]),
            (lse[t],),
            seq_count,
        )

    deltas = [None, None]
    deltas[1] = attend_back(1)
    if fast:
        *got_u, deltas[1] = lax.optimization_barrier((*got_u, deltas[1]))
        last_u = near_add(parts_u[4], first_u, got_u)
        got_u = far_back(last_u, size)
        deltas[1] = after(deltas[1], last_u[0])
        others, other_sums = gradients_other(tokens_t, deltas[1])
        ctx_delta[0] = after(ctx_delta[0], others)
        others = swap_core(others)
        deltas[0] = attend_back(0)
        parts_q = gradients_own(
            tokens_t,
            deltas[0],
            others,
            other_sums,
            go,
            table,
            index,
            core,
            size,
            query_bias.shape[0],
        )
        *got_u, own = lax.optimization_barrier((*got_u, parts_q[4]))
        parts_q = [*parts_q[:4], own]
        first_q = corner_back(parts_q, size)
        token_grad = token_gradient(
            after(first_delta, parts_q[4]), [after(d, parts_q[4]) for d in deltas], wqkv, 0, 2
        )
        *first_q, token_grad = lax.optimization_barrier((*first_q, token_grad))

        def total(last, got):
            return last[0] + got[0].astype(f32) + got[1].astype(f32) + got[2].astype(f32)

        out_ui = total(last_u, got_u)
        hidden_half = out_ui.shape[1] // 2
        out_gu = out_ui[:, :hidden_half].T
        out_gi = out_ui[:, hidden_half:]
        sums_q = corner_add(parts_q, first_q)
        got_q = near_back(sums_q, size)
        last_q = near_add(parts_q[4], first_q, got_q)
        got_q = far_back(last_q, size)
        token_grad = token_gradient(token_grad, [after(d, last_q[0]) for d in deltas], wqkv, 1, 2)
        out_q = total(last_q, got_q)
        n = query_weight.shape[0]
        out_qkv = [out_q[g * n : (g + 1) * n] for g in range(3)]
        out_go = out_q[3 * n : 4 * n].T
        vec = out_q[4 * n :]
        vec = vec + swap_core(vec)
        vec_out = [vec[i, : item.shape[0]] for i, item in enumerate(vectors)]
    else:
        deltas[0] = attend_back(0)
        token_grad = token_gradient(first_delta, deltas, wqkv, 0, 1)

        def reduce(pair, order):
            summed = (pair[0].astype(f32) + pair[1].astype(f32)).astype(bf16)
            return scatter_rows(summed, order, size, index)

        out_gu = reduce(gu, orders[1]).T
        out_gi = reduce(gi, orders[0])
        out_go = reduce(go, orders[2]).T
        out_qkv = [
            reduce(product(tokens, [d[g] for d in deltas]), order) for g, order in enumerate(orders)
        ]
        bias_grads = [
            joined([jnp.sum(d[g].astype(f32), axis=0, keepdims=True) for d in deltas]) for g in (0, 2)
        ]
        bias_grads += [s[i : i + 1] for s in (first_sums, second_sums) for i in range(3)]
        bias_grads.append(joined(jnp.split(inner_sums[:1], 2, 1)))
        packed = jnp.concatenate([item.reshape(size, -1) for item in bias_grads], axis=1)
        packed = packed + swap_core(packed)
        own = scatter_rows(packed, orders[0], size, index).reshape(-1)
        vec_out = [own[a:b] for a, b in zip(bounds[:-1], bounds[1:])]
    return (
        layer_out,
        token_grad,
        out_qkv[0],
        out_qkv[1],
        out_qkv[2],
        out_go,
        vec_out[0],
        vec_out[1],
        vec_out[2],
        vec_out[3],
        vec_out[4],
        out_gi,
        vec_out[8],
        out_gu,
        vec_out[5],
        vec_out[6],
        vec_out[7],
    )


def solution(mesh):
    both = P(("dp", "tensor"), None)
    cols = P("dp", "tensor")
    rows = P("tensor", "dp")
    vec = P("dp")
    in_specs = (
        both, both, vec, cols, cols, cols, rows, vec, vec, vec, vec, vec, cols, vec, rows, vec, vec, vec,
    )
    out_specs = (
        both, both, cols, cols, cols, rows, vec, vec, vec, vec, vec, cols, vec, rows, vec, vec, vec,
    )
    return jax.shard_map(
        on_device, mesh=mesh, in_specs=in_specs, out_specs=out_specs, check_vma=False
    )
```

```python
import jax
import jax.numpy as jnp
from jax import lax
from jax.experimental import pallas as pl
from jax.experimental.pallas import tpu as pltpu
from jax.sharding import PartitionSpec as P

HD = 64
norm_eps = 1e-12
masked_score = -1000000000.0
score_scale = HD ** (-0.5)
f32 = jnp.float32
bf16 = jnp.bfloat16
NT = (((1,), (1,)), ((), ()))
TN = (((0,), (0,)), ((), ()))
NN = (((1,), (0,)), ((), ()))
ROWS = 256


def dot(left, right, dims):
    return lax.dot_general(left, right, dims, preferred_element_type=f32)


def stage_orders(size):
    up = [1 << k for k in range(size.bit_length() - 1)]
    down = up[::-1]
    return (down, down[:-2] + [down[-1], down[-2]], [down[0]] + up[:-1])


def swap_dp(value, mask, size):
    return lax.ppermute(value, "dp", [(i, i ^ mask) for i in range(size)])


def swap_core(value):
    return lax.ppermute(value, "tensor", [(0, 1), (1, 0)])


def after(value, *others):
    return lax.optimization_barrier((value, *others))[0]


def gather_rows(shard, order, size, index):
    rows, cols = shard.shape
    have = []
    buf = shard
    for mask in order:
        received = swap_dp(buf, mask, size)
        have = sorted(have + [mask], reverse=True)
        axis = have.index(mask)
        buf = jnp.where(
            (index & mask) != 0,
            jnp.stack([received, buf], axis),
            jnp.stack([buf, received], axis),
        )
    return buf.reshape(size * rows, cols)


def scatter_rows(own, order, size, index):
    total, cols = own.shape
    have = sorted(order, reverse=True)
    buf = own.reshape([2] * len(have) + [total // size, cols])
    for mask in order[::-1]:
        axis = have.index(mask)
        bit = ((index & mask) != 0).astype(jnp.int32)
        keep = lax.dynamic_index_in_dim(buf, bit, axis, keepdims=False)
        give = lax.dynamic_index_in_dim(buf, 1 - bit, axis, keepdims=False)
        received = swap_dp(give, mask, size)
        buf = keep.astype(f32) + received.astype(f32)
        have.remove(mask)
        if have:
            buf = buf.astype(own.dtype)
    return buf


HINT = pl.CostEstimate(flops=1, transcendentals=0, bytes_accessed=1)


def distance_of(piece, k):
    return (4 * (piece % 2) + 8 * k) ^ piece // 2


def vmem(shape):
    return pl.BlockSpec(shape, lambda *_: (0,) * len(shape))


def pack_first(weights, vectors):
    rows, cols = weights[0].shape
    count = len(weights)

    def kernel(*refs):
        ins, out_ref, table = refs[: count + len(vectors)], refs[-2], refs[-1]
        for g in range(count):
            out_ref[g * rows : (g + 1) * rows, :] = ins[g][...]
        table[...] = jnp.zeros(table.shape, f32)
        for i, ref in enumerate(ins[count:]):
            table[i : i + 1, : ref.shape[1]] = ref[...].astype(f32)
        out_ref[count * rows :, :] = table[...].astype(bf16)

    return pl.pallas_call(
        kernel,
        out_shape=jax.ShapeDtypeStruct((count * rows + 16, cols), bf16),
        scratch_shapes=[pltpu.VMEM((16, cols), f32)],
        cost_estimate=HINT,
    )(*weights, *[item.reshape(1, -1) for item in vectors])


def place_first(pieces, index, count, size, lengths):
    total_rows, cols = pieces[0].shape[1:]
    rows = (total_rows - 16) // count

    def kernel(index_ref, *refs):
        ins = refs[: len(pieces)]
        w_ref, v_ref, last_ref, table = refs[len(pieces) :]
        for n, ref in enumerate(ins):
            for k in range(ref.shape[0]):
                block = index_ref[0] ^ distance_of(n, k)
                at = pl.ds(pl.multiple_of(block * rows, 16), rows)
                for g in range(count):
                    w_ref[g, at, :] = ref[k, g * rows : (g + 1) * rows, :]
                table[block] = ref[k, count * rows :, :].astype(f32)
        one, last = lengths
        for c in range(size):
            v_ref[:, c * one : (c + 1) * one] = table[c][:, :one]
            last_ref[:, c * last : (c + 1) * last] = table[c][8:9, :last]

    out = [(count, size * rows, cols), (16, size * lengths[0]), (1, size * lengths[1])]
    return pl.pallas_call(
        kernel,
        out_shape=[jax.ShapeDtypeStruct(o, d) for o, d in zip(out, (bf16, f32, f32))],
        grid_spec=pltpu.PrefetchScalarGridSpec(
            num_scalar_prefetch=1,
            grid=(1,),
            in_specs=[vmem(p.shape) for p in pieces],
            out_specs=[vmem(o) for o in out],
            scratch_shapes=[pltpu.VMEM((size, 16, cols), f32)],
        ),
        cost_estimate=HINT,
    )(index[None], *pieces)


def place_cols(pieces, index, widths, size):
    rows = pieces[0].shape[1]

    def kernel(index_ref, *refs):
        ins, outs = refs[: len(pieces)], refs[len(pieces) :]
        for n, ref in enumerate(ins):
            for k in range(ref.shape[0]):
                block = index_ref[0] ^ distance_of(n, k)
                at = 0
                for out_ref, width in zip(outs, widths):
                    here = pl.ds(pl.multiple_of(block * rows, 16), rows)
                    out_ref[here, :] = ref[k, :, at : at + width]
                    at += width

    out = [(size * rows, w) for w in widths]
    return pl.pallas_call(
        kernel,
        out_shape=[jax.ShapeDtypeStruct(o, bf16) for o in out],
        grid_spec=pltpu.PrefetchScalarGridSpec(
            num_scalar_prefetch=1,
            grid=(1,),
            in_specs=[vmem(p.shape) for p in pieces],
            out_specs=[vmem(o) for o in out],
        ),
        cost_estimate=HINT,
    )(index[None], *pieces)


PARTS = (
    ((3, (0, 1)), (1, (0, 1))),
    ((3, (2, 3)), (2, (2, 3))),
    ((1, (2, 3)),),
    ((2, (0, 1)),),
    ((0, (0, 1, 2, 3)),),
)


def split_out_specs(rows, step):
    return [
        pl.BlockSpec((sum(len(ks) for _, ks in part), rows, step), lambda i, *_: (0, 0, i))
        for part in PARTS
    ]


def split_shapes(rows, cols):
    return [
        jax.ShapeDtypeStruct(
            (sum(len(ks) for _, ks in part), rows, cols), bf16
        )
        for part in PARTS
    ]


def split_cols(pairs, index, size, step):
    total = pairs[0][0].shape[0]
    rows = total // size
    counts = [a.shape[1] // step for a, _ in pairs]
    starts = [sum(counts[:i]) for i in range(len(counts))]

    def kernel(index_ref, *refs):
        ins, outs = refs[: 2 * len(pairs)], refs[2 * len(pairs) :]
        for n, (first, count) in enumerate(zip(starts, counts)):

            @pl.when((pl.program_id(0) >= first) & (pl.program_id(0) < first + count))
            def _(n=n):
                for part, out_ref in zip(PARTS, outs):
                    at = 0
                    for offset, ks in part:
                        for k in ks:
                            block = index_ref[0] ^ (4 * k ^ offset)
                            here = pl.ds(pl.multiple_of(block * rows, 16), rows)
                            out_ref[at] = ins[2 * n][here, :] + ins[2 * n + 1][here, :]
                            at += 1

    specs = []
    for a, n in zip(starts, counts):
        spec = pl.BlockSpec((total, step), lambda i, *_, a=a, n=n: (0, jnp.clip(i - a, 0, n - 1)))
        specs += [spec, spec]
    return pl.pallas_call(
        kernel,
        out_shape=split_shapes(rows, sum(counts) * step),
        grid_spec=pltpu.PrefetchScalarGridSpec(
            num_scalar_prefetch=1,
            grid=(sum(counts),),
            in_specs=specs,
            out_specs=split_out_specs(rows, step),
        ),
        cost_estimate=HINT,
    )(index[None], *[item for pair in pairs for item in pair])


def gradients_other(tokens_t, deltas):
    width, rows = tokens_t.shape
    count, _, cols = deltas.shape

    def kernel(t_ref, d_ref, o_ref, s_ref):
        o_ref[0] = dot(t_ref[...], d_ref[0], NN).astype(bf16)
        s_ref[0] = dot(jnp.ones((8, rows), bf16), d_ref[0], NN)

    return pl.pallas_call(
        kernel,
        out_shape=[
            jax.ShapeDtypeStruct((count, width, cols), bf16),
            jax.ShapeDtypeStruct((count, 8, cols), f32),
        ],
        grid=(count,),
        in_specs=[vmem(tokens_t.shape), pl.BlockSpec((1, rows, cols), lambda g: (g, 0, 0))],
        out_specs=[
            pl.BlockSpec((1, width, cols), lambda g: (g, 0, 0)),
            pl.BlockSpec((1, 8, cols), lambda g: (g, 0, 0)),
        ],
        cost_estimate=HINT,
    )(tokens_t, deltas)


def gradients_own(
    tokens_t, deltas, others, other_sums, ready, table, index, core, size, one
):
    width, rows = tokens_t.shape
    count, _, cols = deltas.shape
    part_rows = width // size
    height = (count + 1) * part_rows + 16

    def kernel(at_ref, t_ref, d_ref, other_ref, sums_ref, r0_ref, r1_ref, table_ref, *refs):
        outs, total, own_sums, vec = refs[: len(PARTS)], refs[-3], refs[-2], refs[-1]
        g = pl.program_id(0)
        total[...] = dot(t_ref[...], d_ref[0], NN) + other_ref[0].astype(f32)
        own_sums[g] = dot(jnp.ones((8, rows), bf16), d_ref[0], NN)

        def blocks():
            for part, out_ref in zip(PARTS, outs):
                at = 0
                for offset, ks in part:
                    for k in ks:
                        yield at_ref[0] ^ (4 * k ^ offset), out_ref, at
                        at += 1

        for block, out_ref, at in blocks():
            value = total[pl.ds(pl.multiple_of(block * part_rows, 16), part_rows), :]
            out_ref[at, pl.ds(pl.multiple_of(g * part_rows, 16), part_rows), :] = value.astype(bf16)

        @pl.when(g == count - 1)
        def _():
            vec[...] = table_ref[...]
            for row, which in ((0, 0), (1, 2)):
                for ref, side in ((own_sums, 0), (sums_ref, 1)):
                    first = (at_ref[1] ^ side) * (size // 2)
                    for j in range(size // 2):
                        vec[first + j, row : row + 1, :one] = ref[which, 0:1, j * one : (j + 1) * one]
            for block, out_ref, at in blocks():
                here = pl.ds(pl.multiple_of(block * part_rows, 16), part_rows)
                value = r0_ref[here, :] + r1_ref[here, :]
                out_ref[at, count * part_rows : (count + 1) * part_rows, :] = value
                out_ref[at, (count + 1) * part_rows :, :] = vec[block].astype(bf16)

    return pl.pallas_call(
        kernel,
        out_shape=split_shapes(height, cols),
        grid_spec=pltpu.PrefetchScalarGridSpec(
            num_scalar_prefetch=1,
            grid=(count,),
            in_specs=[
                vmem(tokens_t.shape),
                pl.BlockSpec((1, rows, cols), lambda g, *_: (g, 0, 0)),
                pl.BlockSpec((1, width, cols), lambda g, *_: (g, 0, 0)),
                vmem(other_sums.shape),
                *[vmem(a.shape) for a in ready],
                vmem(table.shape),
            ],
            out_specs=[vmem(shape.shape) for shape in split_shapes(height, cols)],
            scratch_shapes=[
                pltpu.VMEM((width, cols), f32),
                pltpu.VMEM((count, 8, cols), f32),
                pltpu.VMEM(table.shape, f32),
            ],
        ),
        cost_estimate=HINT,
    )(jnp.stack([index, core]), tokens_t, deltas, others, other_sums, *ready, table)


def pack_table(first_sums, second_sums, inner_sums, core, size, cols):
    one = first_sums.shape[1] // size
    end = inner_sums.shape[1] // size

    def kernel(core_ref, a_ref, b_ref, inner_ref, out_ref, table):
        table[...] = jnp.zeros(table.shape, f32)
        out_ref[...] = jnp.zeros(out_ref.shape, f32)
        table[2:5, :] = a_ref[0:3, :]
        table[5:8, :] = b_ref[0:3, :]
        for c in range(size):
            out_ref[c, :, :one] = table[:, c * one : (c + 1) * one]
            d = (c + size // 2) % size
            here = inner_ref[0:1, c * end : (c + 1) * end]
            there = inner_ref[0:1, d * end : (d + 1) * end]
            out_ref[c, 8:9, :end] = jnp.where(core_ref[0] == 0, here, there)

    ins = (first_sums, second_sums, inner_sums)
    return pl.pallas_call(
        kernel,
        out_shape=jax.ShapeDtypeStruct((size, 16, cols), f32),
        grid_spec=pltpu.PrefetchScalarGridSpec(
            num_scalar_prefetch=1,
            grid=(1,),
            in_specs=[vmem(a.shape) for a in ins],
            out_specs=vmem((size, 16, cols)),
            scratch_shapes=[pltpu.VMEM((16, first_sums.shape[1]), f32)],
        ),
        cost_estimate=HINT,
    )(core[None], *ins)


def whole_call(kernel, outs, ins, blocks):
    return pl.pallas_call(
        kernel,
        out_shape=[jax.ShapeDtypeStruct(o, d) for o, d in outs],
        grid=(1,),
        in_specs=[vmem((n, *a.shape[1:])) for a, n in zip(ins, blocks)],
        out_specs=[vmem(o) for o, _ in outs],
        cost_estimate=HINT,
    )(*ins)


def corner_back(parts, size):
    return swap_dp(parts[0], 1, size), swap_dp(parts[1], 2, size)


def corner_add(parts, got):
    keep = parts[2:4]

    def kernel(one_ref, two_ref, r1_ref, r2_ref, o1_ref, o2_ref):
        o1_ref[...] = one_ref[...] + r2_ref[...]
        o2_ref[...] = two_ref[...] + r1_ref[...]

    return whole_call(
        kernel, [(item.shape, bf16) for item in keep], [*keep, *got], (2, 2, 2, 2)
    )


def near_back(sums, size):
    return swap_dp(sums[0], 1, size), swap_dp(sums[1], 2, size)


def near_add(own, first, got):
    def kernel(own_ref, f1_ref, f2_ref, r1_ref, r2_ref, keep_ref, *outs):
        def total(k):
            early = f1_ref[2 + k] if k < 2 else f2_ref[k]
            late = r2_ref[k] if k < 2 else r1_ref[k - 2]
            return own_ref[k].astype(f32) + early.astype(f32) + late.astype(f32)

        keep_ref[...] = total(0)
        for k in (1, 2, 3):
            outs[k - 1][...] = total(k).astype(bf16)

    shape = own.shape[1:]
    return whole_call(
        kernel, [(shape, f32)] + [(shape, bf16)] * 3, [own, *first, *got], (4, 4, 4, 2, 2)
    )


def far_back(sums, size):
    return [swap_dp(item, 4 * (k + 1), size) for k, item in enumerate(sums[1:])]


def project(tokens, weights, vectors, core, side):
    rows, width = tokens.shape
    cols = weights.shape[2]

    def kernel(core_ref, x_ref, w_ref, v_ref, q_out, k_out, v_out):
        half = core_ref[0] ^ side
        bias = jnp.where(half == 0, v_ref[0:8, :cols], v_ref[0:8, cols:])
        x = x_ref[...]
        q_out[...] = (dot(x, w_ref[0], NN) + bias[0:1]).astype(bf16)
        k_out[...] = dot(x, w_ref[1], NN).astype(bf16)
        v_out[...] = (dot(x, w_ref[2], NN) + bias[1:2]).astype(bf16)

    tile = pl.BlockSpec((ROWS, cols), lambda i, *_: (i, 0))
    return pl.pallas_call(
        kernel,
        out_shape=[jax.ShapeDtypeStruct((rows, cols), bf16)] * 3,
        grid_spec=pltpu.PrefetchScalarGridSpec(
            num_scalar_prefetch=1,
            grid=(rows // ROWS,),
            in_specs=[
                pl.BlockSpec((ROWS, width), lambda i, *_: (i, 0)),
                vmem(weights.shape),
                vmem(vectors.shape),
            ],
            out_specs=[tile] * 3,
        ),
        cost_estimate=HINT,
    )(core[None], tokens, weights, vectors)


def token_gradient(first_delta, deltas, weights, part, parts):
    count, rows, cols = deltas[0].shape
    width = weights[0].shape[1]
    steps = rows // ROWS // parts

    def kernel(f_ref, d0_ref, d1_ref, w0_ref, w1_ref, *refs):
        o_ref = refs[-1]
        total = f_ref[...]
        for d_ref, w_ref in ((d0_ref, w0_ref), (d1_ref, w1_ref)):
            for g in range(count):
                total = total + dot(d_ref[g], w_ref[g], NT)
        o_ref[...] = total

    tile = pl.BlockSpec((ROWS, width), lambda i: (i + part * steps, 0))
    delta_part = pl.BlockSpec((count, ROWS, cols), lambda i: (0, i + part * steps, 0))
    return pl.pallas_call(
        kernel,
        out_shape=jax.ShapeDtypeStruct((rows, width), f32),
        grid=(steps,),
        in_specs=[tile, delta_part, delta_part] + [vmem(weights[0].shape)] * 2,
        out_specs=tile,
        input_output_aliases={0: 0},
        cost_estimate=pl.CostEstimate(
            flops=4 * count * rows * width * cols // parts,
            transcendentals=0,
            bytes_accessed=16 * rows * cols // parts,
        ),
    )(first_delta, *deltas, *weights)


def center(values):
    mean = jnp.mean(values, axis=-1, keepdims=True)
    centred = values - mean
    var = jnp.mean(centred * centred, axis=-1, keepdims=True)
    rinv = lax.rsqrt(var + norm_eps)
    return centred * rinv, rinv


def norm_back(grad, normed, rinv, gain):
    scaled = grad * gain
    return rinv * (
        scaled
        - jnp.mean(scaled, axis=-1, keepdims=True)
        - normed * jnp.mean(scaled * normed, axis=-1, keepdims=True)
    )


def add_rows(ref, items):
    for i, item in enumerate(items):
        ref[i : i + 1, : item.shape[1]] += jnp.sum(item, axis=0, keepdims=True)


def clear(*refs):
    @pl.when(pl.program_id(0) == 0)
    def _():
        for ref in refs:
            ref[...] = jnp.zeros(ref.shape, f32)


def row_call(kernel, tiles, wholes, outs, sums):
    rows = tiles[0].shape[0]

    def tile(cols):
        return pl.BlockSpec((ROWS, cols), lambda i: (i, 0))

    return pl.pallas_call(
        kernel,
        out_shape=[jax.ShapeDtypeStruct((rows, n), d) for n, d in outs]
        + [jax.ShapeDtypeStruct((8, n), f32) for n in sums],
        grid=(rows // ROWS,),
        in_specs=[tile(a.shape[1]) for a in tiles] + [vmem(a.shape) for a in wholes],
        out_specs=[tile(n) for n, _ in outs] + [vmem((8, n)) for n in sums],
        cost_estimate=HINT,
    )(*tiles, *wholes)


def first_block(tokens, context, weights, vectors):
    def kernel(x_ref, c0_ref, c1_ref, w0_ref, w1_ref, v_ref, out, low):
        total = dot(c0_ref[...], w0_ref[...], NT) + dot(c1_ref[...], w1_ref[...], NT)
        total = x_ref[...].astype(f32) + total + v_ref[2:3]
        out[...] = total
        low[...] = (center(total)[0] * v_ref[3:4] + v_ref[4:5]).astype(bf16)

    width = tokens.shape[1]
    return row_call(
        kernel, [tokens, *context], [*weights, vectors], [(width, f32), (width, bf16)], ()
    )


def outer_block(hidden, cotangent, act, weights, vectors):
    def kernel(
        h_ref, c_ref, a0_ref, a1_ref, w0_ref, w1_ref, v_ref, out, delta, low, sums
    ):
        clear(sums)

        feed = dot(a0_ref[...], w0_ref[...], NT) + dot(a1_ref[...], w1_ref[...], NT)
        normed, rinv = center(h_ref[...].astype(f32) + (v_ref[5:6] + feed))
        out[...] = normed * v_ref[6:7] + v_ref[7:8]
        cot = c_ref[...].astype(f32)
        found = norm_back(cot, normed, rinv, v_ref[6:7])
        delta[...] = found
        low[...] = found.astype(bf16)
        add_rows(sums, (found, cot * normed, cot))

    width = hidden.shape[1]
    return row_call(
        kernel,
        [hidden, cotangent, *act],
        [*weights, vectors],
        [(width, f32), (width, f32), (width, bf16)],
        (width,),
    )


def inner_back(second_delta, inner_delta, first_in, weights, vectors):
    def kernel(
        s_ref, d0_ref, d1_ref, f_ref, w0_ref, w1_ref, v_ref, delta, low, sums, inner
    ):
        clear(sums, inner)
        ones = jnp.ones((8, ROWS), bf16)
        half = d0_ref.shape[1]
        inner[:, :half] += dot(ones, d0_ref[...], NN)
        inner[:, half:] += dot(ones, d1_ref[...], NN)

        grad = dot(d0_ref[...], w0_ref[...], NT) + dot(d1_ref[...], w1_ref[...], NT)
        grad = s_ref[...] + grad
        normed, rinv = center(f_ref[...])
        found = norm_back(grad, normed, rinv, v_ref[3:4])
        delta[...] = found
        low[...] = found.astype(bf16)
        add_rows(sums, (found, grad * normed, grad))

    width = first_in.shape[1]
    return row_call(
        kernel,
        [second_delta, *inner_delta, first_in],
        [*weights, vectors],
        [(width, f32), (width, bf16)],
        (width, 2 * inner_delta[0].shape[1]),
    )


def three_parts(row):
    high = row.astype(bf16).astype(f32)
    middle = (row - high).astype(bf16).astype(f32)
    return [high, middle, row - high - middle]


def extra_lanes(shape, keys_valid):
    lane = lax.broadcasted_iota(jnp.int32, shape, 1) % HD
    row = lax.broadcasted_iota(jnp.int32, shape, 0)
    bias = jnp.where(row < keys_valid, 0.0, masked_score)
    return jnp.where(lane == 0, bias, jnp.where(lane < 4, 1.0, 0.0)).astype(bf16)


def extra_rows(first, row, length):
    rows = [jnp.full((1, length), first, f32)]
    rows += three_parts(row) if row is not None else []
    rows.append(jnp.zeros((16 - len(rows), length), f32))
    return jnp.concatenate(rows, 0).astype(bf16)


def with_rows(own_t, h, first, row):
    length = own_t.shape[1]
    own = own_t[h * HD : (h + 1) * HD]
    rest = [extra_rows(first, row, length), jnp.zeros((HD - 16, length), bf16)]
    return jnp.concatenate([own] + rest if h == 0 else rest + [own], 0)


def attend_forward_kernel(lens, q_ref, k_ref, v_ref, ctx_ref, lse_ref):
    seq_len, lanes = q_ref.shape
    lane = lax.broadcasted_iota(jnp.int32, (seq_len, lanes), 1)
    extra = extra_lanes((seq_len, lanes), lens[pl.program_id(0)])
    ones = jnp.ones((16, seq_len), bf16)
    loaded = {}

    def scores(h):
        if h == 0:
            query_t = (q_ref[...] * jnp.bfloat16(score_scale)).T
            loaded[0] = (query_t, k_ref[...], v_ref[...].T)
        query_t, keys, _ = loaded[0]
        return dot(jnp.where(lane // HD == h, keys, extra), with_rows(query_t, h, 1.0, None), NN)

    pieces = []
    ahead = scores(0)
    for h in range(2):
        now = ahead
        if h == 0:
            ahead = scores(1)
        top = jnp.max(now, axis=0, keepdims=True)
        expo = jnp.exp(now - top).astype(bf16)
        value_t = loaded[0][2][h * HD : (h + 1) * HD]
        found = dot(jnp.concatenate([value_t, ones], 0), expo, NN)
        total = found[HD : HD + 1]
        pieces.append(found[:HD] / total)
        lse_ref[0, 0, h : h + 1, :] = top + jnp.log(total)
        if h == 1:
            ctx_ref[...] = jnp.concatenate(pieces, 0).T.astype(bf16)
            pieces = []


def attend_backward_kernel(lens, q_ref, k_ref, v_ref, d_ref, c_ref, lse_ref, out_ref):
    seq_len, lanes = q_ref.shape
    lane = lax.broadcasted_iota(jnp.int32, (seq_len, lanes), 1)
    extra = extra_lanes((seq_len, lanes), lens[pl.program_id(0)])
    loaded = {}

    def products(h):
        if h == 0:
            query = q_ref[...] * jnp.bfloat16(score_scale)
            delta = d_ref[...]
            delta_t = delta.T
            inner = delta_t.astype(f32) * c_ref[...].T.astype(f32)
            keys = k_ref[...]
            loaded[0] = (query, query.T, delta, delta_t, inner, keys, keys.T, v_ref[...])
        _, query_t, _, delta_t, inner, keys, _, values = loaded[0]
        own = lane // HD == h
        inner = jnp.sum(inner[h * HD : (h + 1) * HD], axis=0, keepdims=True)
        lse = lse_ref[0, 0, h : h + 1, :]
        logs = dot(jnp.where(own, keys, extra), with_rows(query_t, h, 1.0, -lse), NN)
        centred = dot(jnp.where(own, values, extra), with_rows(delta_t, h, 0.0, -inner), NN)
        return logs, centred

    ahead = products(0)
    for h in range(2):
        logs, centred = ahead
        if h == 0:
            ahead = products(1)
        query, _, delta, _, _, _, keys_t, _ = loaded[0]
        probs = jnp.exp(logs)
        score_delta = (probs * centred).astype(bf16)
        own = lane // HD == h
        part_v = dot(probs.astype(bf16), jnp.where(own, delta, jnp.bfloat16(0)), NN)
        part_k = dot(score_delta, jnp.where(own, query, jnp.bfloat16(0)), NN)
        part_q = dot(keys_t[h * HD : (h + 1) * HD], score_delta, NN)
        if h == 0:
            dv, dk, dq = part_v, part_k, part_q
        else:
            out_ref[0] = (jnp.concatenate([dq, part_q], 0).T * score_scale).astype(bf16)
            out_ref[1] = (dk + part_k).astype(bf16)
            out_ref[2] = (dv + part_v).astype(bf16)


def attend_call(kernel, lens, operands, lse_in, seq_count):
    rows, cols = operands[0].shape
    seq_len = rows // seq_count
    pairs = cols // (2 * HD)
    tile = pl.BlockSpec((seq_len, 2 * HD), lambda s, p, *_: (s, p))
    stat = pl.BlockSpec((1, 1, 2, seq_len), lambda s, p, *_: (s, p, 0, 0))
    if lse_in:
        out_shape = jax.ShapeDtypeStruct((3, rows, cols), bf16)
        out_specs = pl.BlockSpec((3, seq_len, 2 * HD), lambda s, p, *_: (0, s, p))
    else:
        out_shape = [
            jax.ShapeDtypeStruct((rows, cols), bf16),
            jax.ShapeDtypeStruct((seq_count, pairs, 2, seq_len), f32),
        ]
        out_specs = [tile, stat]
    return pl.pallas_call(
        kernel,
        out_shape=out_shape,
        grid_spec=pltpu.PrefetchScalarGridSpec(
            num_scalar_prefetch=1,
            grid=(seq_count, pairs),
            in_specs=[tile] * len(operands) + [stat] * len(lse_in),
            out_specs=out_specs,
        ),
        cost_estimate=HINT,
    )(lens, *operands, *lse_in)


def on_device(
    tokens,
    cotangent,
    lengths,
    query_weight,
    key_weight,
    value_weight,
    out_weight,
    query_bias,
    value_bias,
    out_bias,
    first_gain,
    first_shift,
    inner_weight,
    inner_bias,
    outer_weight,
    outer_bias,
    second_gain,
    second_shift,
):
    size = lax.axis_size("dp")
    index = lax.axis_index("dp")
    core = lax.axis_index("tensor")
    orders = stage_orders(size)
    seq_count = lengths.shape[0] // 2
    lens = lax.dynamic_slice_in_dim(lengths, core * seq_count, seq_count, 0)
    fast = size == 16 and query_weight.shape[0] % 16 == 0
    half = query_weight.shape[1]
    step = half

    vectors = (
        query_bias,
        value_bias,
        out_bias,
        first_gain,
        first_shift,
        outer_bias,
        second_gain,
        second_shift,
        inner_bias,
    )
    bounds = [0]
    for item in vectors:
        bounds.append(bounds[-1] + item.shape[0])
    projections = (query_weight, key_weight, value_weight)
    out_t = out_weight.T
    outer_t = outer_weight.T

    if fast:
        shard = pack_first(projections, vectors)
        far = [swap_dp(shard, d, size) for d in (8, 4, 12)]
        low, high = jnp.stack([shard, far[0]]), jnp.stack(far[1:])
        two_low, one_high = swap_dp(low, 2, size), swap_dp(high, 1, size)
        one_low, two_high = swap_dp(low, 1, size), swap_dp(high, 2, size)
        shard_a = jnp.concatenate([out_t, inner_weight], 1)
        far_a = swap_dp(after(shard_a, low, high), 8, size)
        tokens_t = tokens.T
        pieces = [low, high, one_low, one_high, two_low, two_high]
        pieces += [swap_dp(two_low, 1, size), swap_dp(one_high, 2, size)]
        far_a, *pieces, tokens_t = lax.optimization_barrier((far_a, *pieces, tokens_t))
        low_a = jnp.stack([shard_a, far_a])
        high_a = swap_dp(low_a, 4, size)
        two_low_a, one_low_a = swap_dp(low_a, 2, size), swap_dp(low_a, 1, size)
        wqkv0, vecs, ib = place_first(
            pieces, index, 3, size, (query_bias.shape[0], inner_bias.shape[0])
        )
    else:
        own_vec = jnp.concatenate(vectors)[None, :]
        all_vec = gather_rows(own_vec, orders[0], size, index).astype(f32)
        found = [all_vec[:, a:b].reshape(1, -1) for a, b in zip(bounds[:-1], bounds[1:])]
        vecs = jnp.concatenate(found[:-1] + [jnp.zeros_like(found[0])] * 8, 0)
        ib = found[-1]
        wqkv0 = jnp.stack(
            [gather_rows(w, o, size, index) for w, o in zip(projections, orders)]
        )
        wo0 = gather_rows(out_t, orders[2], size, index)
        wi0 = gather_rows(inner_weight, orders[0], size, index)
        wu0 = gather_rows(outer_t, orders[1], size, index)

    wqkv = (wqkv0, swap_core(wqkv0))
    hidden_half = inner_weight.shape[1]
    ib = (
        jnp.where(core == 0, ib[:, :hidden_half], ib[:, hidden_half:]),
        jnp.where(core == 0, ib[:, hidden_half:], ib[:, :hidden_half]),
    )

    q, k, v, ctx, lse = [], [], [], [], []
    for t in range(2):
        found = project(tokens, wqkv[t], vecs, core, t)
        if fast and t == 0:
            high_a, other, *found = lax.optimization_barrier((high_a, wqkv[1], *found))
            wqkv = (wqkv[0], other)
            one_high_a, two_high_a = swap_dp(high_a, 1, size), swap_dp(high_a, 2, size)
            far_b = swap_dp(after(outer_t, other), 8, size)
        q.append(found[0])
        k.append(found[1])
        v.append(found[2])
    if fast:
        far_b, one_low_a, two_low_a, *q = lax.optimization_barrier(
            (far_b, one_low_a, two_low_a, *q)
        )
        low_b = jnp.stack([outer_t, far_b])
        two_low_b, one_low_b = swap_dp(low_b, 2, size), swap_dp(low_b, 1, size)
        high_b = swap_dp(low_b, 4, size)
    for t in range(2):
        if fast and t == 1:
            q[1] = after(q[1], ctx[0])
        c, s = attend_call(attend_forward_kernel, lens, (q[t], k[t], v[t]), (), seq_count)
        lse.append(s)
        if fast and t == 0:
            pieces_a = [low_a, high_a, one_low_a, one_high_a, two_low_a, two_high_a]
            *pieces_a, high_b, two_low_b, one_low_b, c = lax.optimization_barrier(
                (*pieces_a, high_b, two_low_b, one_low_b, c)
            )
            pieces_a += [swap_dp(pieces_a[4], 1, size), swap_dp(pieces_a[3], 2, size)]
        if fast and t == 1:
            *pieces_a, c = lax.optimization_barrier((*pieces_a, c))
            one_high_b, two_high_b = swap_dp(high_b, 1, size), swap_dp(high_b, 2, size)
            wo0, wi0 = place_cols(pieces_a, index, (half, inner_weight.shape[1]), size)
        ctx.append(c)

    wo = (wo0, swap_core(wo0))
    wi = (wi0, swap_core(wi0))
    first_in, hidden = first_block(tokens, ctx, wo, vecs)
    if fast:
        one_high_b, two_low_b, hidden = lax.optimization_barrier((one_high_b, two_low_b, hidden))
        pieces_b = [low_b, high_b, one_low_b, one_high_b, two_low_b, two_high_b]
        pieces_b += [swap_dp(two_low_b, 1, size), swap_dp(one_high_b, 2, size)]
    act, slope = [], []
    for t in range(2):
        u = dot(hidden, wi[t], NN) + ib[t]
        cdf = 0.5 * (1.0 + lax.erf(u * (0.5**0.5)))
        act.append((u * cdf).astype(bf16))
        pdf = jnp.exp(-0.5 * u * u) * 0.3989422804014327
        slope.append((cdf + u * pdf).astype(bf16))
        if fast and t == 0:
            *pieces_b, act[0] = lax.optimization_barrier((*pieces_b, act[0]))
            (wu0,) = place_cols(pieces_b, index, (inner_weight.shape[1],), size)
            hidden = after(hidden, wu0)
    wu = (wu0, swap_core(wu0))
    layer_out, second_delta, feed_delta, second_sums = outer_block(
        hidden, cotangent, act, wu, vecs
    )

    def product(left, right):
        other = dot(left, right[1], TN).astype(bf16)
        other = swap_core(other)
        return dot(left, right[0], TN).astype(bf16), other

    gu = product(feed_delta, act)
    feed_delta, *gu = lax.optimization_barrier((feed_delta, *gu))
    inner_delta = [None, None]
    for t in (1, 0):
        inner_delta[t] = (dot(feed_delta, wu[t], NN) * slope[t].astype(f32)).astype(bf16)
    gi = product(hidden, inner_delta)
    inner_delta[0], inner_delta[1], *gi = lax.optimization_barrier((*inner_delta, *gi))
    if fast:
        parts_u = split_cols([gu, gi], index, size, 2 * step)
        first_u = corner_back(parts_u, size)
        inner_delta[0], inner_delta[1] = [after(d, parts_u[4]) for d in inner_delta]
    first_delta, branch_delta, first_sums, inner_sums = inner_back(
        second_delta, inner_delta, first_in, wi, vecs
    )
    go = list(product(branch_delta, ctx))
    ctx_delta = [dot(branch_delta, wo[t], NN).astype(bf16) for t in range(2)]

    def joined(pair):
        return jnp.where(
            core == 0, jnp.concatenate(pair, 1), jnp.concatenate(pair[::-1], 1)
        )

    if fast:
        table = pack_table(first_sums, second_sums, inner_sums, core, size, half)
        *first_u, table, ctx_delta[0], ctx_delta[1], go[0], go[1] = lax.optimization_barrier(
            (*first_u, table, *ctx_delta, *go)
        )
        sums_u = corner_add(parts_u, first_u)
        got_u = near_back(sums_u, size)
        ctx_delta[1] = after(ctx_delta[1], table, sums_u[0])

    def attend_back(t):
        return attend_call(
            attend_backward_kernel,
            lens,
            (q[t], k[t], v[t], ctx_delta[t], ctx[t]),
            (lse[t],),
            seq_count,
        )

    deltas = [None, None]
    deltas[1] = attend_back(1)
    if fast:
        *got_u, deltas[1] = lax.optimization_barrier((*got_u, deltas[1]))
        last_u = near_add(parts_u[4], first_u, got_u)
        got_u = far_back(last_u, size)
        deltas[1] = after(deltas[1], last_u[0])
        others, other_sums = gradients_other(tokens_t, deltas[1])
        ctx_delta[0] = after(ctx_delta[0], others)
        others = swap_core(others)
        deltas[0] = attend_back(0)
        parts_q = gradients_own(
            tokens_t,
            deltas[0],
            others,
            other_sums,
            go,
            table,
            index,
            core,
            size,
            query_bias.shape[0],
        )
        *got_u, own = lax.optimization_barrier((*got_u, parts_q[4]))
        parts_q = [*parts_q[:4], own]
        first_q = corner_back(parts_q, size)
        token_grad = token_gradient(
            after(first_delta, parts_q[4]), [after(d, parts_q[4]) for d in deltas], wqkv, 0, 2
        )
        *first_q, token_grad = lax.optimization_barrier((*first_q, token_grad))

        def total(last, got):
            return last[0] + got[0].astype(f32) + got[1].astype(f32) + got[2].astype(f32)

        out_ui = total(last_u, got_u)
        hidden_half = out_ui.shape[1] // 2
        out_gu = out_ui[:, :hidden_half].T
        out_gi = out_ui[:, hidden_half:]
        sums_q = corner_add(parts_q, first_q)
        got_q = near_back(sums_q, size)
        last_q = near_add(parts_q[4], first_q, got_q)
        got_q = far_back(last_q, size)
        token_grad = token_gradient(token_grad, [after(d, last_q[0]) for d in deltas], wqkv, 1, 2)
        out_q = total(last_q, got_q)
        n = query_weight.shape[0]
        out_qkv = [out_q[g * n : (g + 1) * n] for g in range(3)]
        out_go = out_q[3 * n : 4 * n].T
        vec = out_q[4 * n :]
        vec = vec + swap_core(vec)
        vec_out = [vec[i, : item.shape[0]] for i, item in enumerate(vectors)]
    else:
        deltas[0] = attend_back(0)
        token_grad = token_gradient(first_delta, deltas, wqkv, 0, 1)

        def reduce(pair, order):
            summed = (pair[0].astype(f32) + pair[1].astype(f32)).astype(bf16)
            return scatter_rows(summed, order, size, index)

        out_gu = reduce(gu, orders[1]).T
        out_gi = reduce(gi, orders[0])
        out_go = reduce(go, orders[2]).T
        out_qkv = [
            reduce(product(tokens, [d[g] for d in deltas]), order) for g, order in enumerate(orders)
        ]
        bias_grads = [
            joined([jnp.sum(d[g].astype(f32), axis=0, keepdims=True) for d in deltas]) for g in (0, 2)
        ]
        bias_grads += [s[i : i + 1] for s in (first_sums, second_sums) for i in range(3)]
        bias_grads.append(joined(jnp.split(inner_sums[:1], 2, 1)))
        packed = jnp.concatenate([item.reshape(size, -1) for item in bias_grads], axis=1)
        packed = packed + swap_core(packed)
        own = scatter_rows(packed, orders[0], size, index).reshape(-1)
        vec_out = [own[a:b] for a, b in zip(bounds[:-1], bounds[1:])]
    return (
        layer_out,
        token_grad,
        out_qkv[0],
        out_qkv[1],
        out_qkv[2],
        out_go,
        vec_out[0],
        vec_out[1],
        vec_out[2],
        vec_out[3],
        vec_out[4],
        out_gi,
        vec_out[8],
        out_gu,
        vec_out[5],
        vec_out[6],
        vec_out[7],
    )


def solution(mesh):
    both = P(("dp", "tensor"), None)
    cols = P("dp", "tensor")
    rows = P("tensor", "dp")
    vec = P("dp")
    in_specs = (
        both, both, vec, cols, cols, cols, rows, vec, vec, vec, vec, vec, cols, vec, rows, vec, vec, vec,
    )
    out_specs = (
        both, both, cols, cols, cols, rows, vec, vec, vec, vec, vec, cols, vec, rows, vec, vec, vec,
    )
    return jax.shard_map(
        on_device, mesh=mesh, in_specs=in_specs, out_specs=out_specs, check_vma=False
    )
```

```python
import jax
import jax.numpy as jnp
from jax import lax
from jax.experimental import pallas as pl
from jax.experimental.pallas import tpu as pltpu
from jax.sharding import PartitionSpec as P

HD = 64
norm_eps = 1e-12
masked_score = -1000000000.0
score_scale = HD ** (-0.5)
f32 = jnp.float32
bf16 = jnp.bfloat16
NT = (((1,), (1,)), ((), ()))
TN = (((0,), (0,)), ((), ()))
NN = (((1,), (0,)), ((), ()))
ROWS = 256


def dot(left, right, dims):
    return lax.dot_general(left, right, dims, preferred_element_type=f32)


def stage_orders(size):
    up = [1 << k for k in range(size.bit_length() - 1)]
    down = up[::-1]
    return (down, down[:-2] + [down[-1], down[-2]], [down[0]] + up[:-1])


def swap_dp(value, mask, size):
    return lax.ppermute(value, "dp", [(i, i ^ mask) for i in range(size)])


def swap_core(value):
    return lax.ppermute(value, "tensor", [(0, 1), (1, 0)])


def after(value, *others):
    return lax.optimization_barrier((value, *others))[0]


def gather_rows(shard, order, size, index):
    rows, cols = shard.shape
    have = []
    buf = shard
    for mask in order:
        received = swap_dp(buf, mask, size)
        have = sorted(have + [mask], reverse=True)
        axis = have.index(mask)
        buf = jnp.where(
            (index & mask) != 0,
            jnp.stack([received, buf], axis),
            jnp.stack([buf, received], axis),
        )
    return buf.reshape(size * rows, cols)


def scatter_rows(own, order, size, index):
    total, cols = own.shape
    have = sorted(order, reverse=True)
    buf = own.reshape([2] * len(have) + [total // size, cols])
    for mask in order[::-1]:
        axis = have.index(mask)
        bit = ((index & mask) != 0).astype(jnp.int32)
        keep = lax.dynamic_index_in_dim(buf, bit, axis, keepdims=False)
        give = lax.dynamic_index_in_dim(buf, 1 - bit, axis, keepdims=False)
        received = swap_dp(give, mask, size)
        buf = keep.astype(f32) + received.astype(f32)
        have.remove(mask)
        if have:
            buf = buf.astype(own.dtype)
    return buf


HINT = pl.CostEstimate(flops=1, transcendentals=0, bytes_accessed=1)


def distance_of(piece, k):
    return (4 * (piece % 2) + 8 * k) ^ piece // 2


def vmem(shape):
    return pl.BlockSpec(shape, lambda *_: (0,) * len(shape))


def pack_first(weights, vectors):
    rows, cols = weights[0].shape
    count = len(weights)

    def kernel(*refs):
        ins, out_ref, table = refs[: count + len(vectors)], refs[-2], refs[-1]
        for g in range(count):
            out_ref[g * rows : (g + 1) * rows, :] = ins[g][...]
        table[...] = jnp.zeros(table.shape, f32)
        for i, ref in enumerate(ins[count:]):
            table[i : i + 1, : ref.shape[0]] = ref[...].astype(f32)[None, :]
        out_ref[count * rows :, :] = table[...].astype(bf16)

    return pl.pallas_call(
        kernel,
        out_shape=jax.ShapeDtypeStruct((count * rows + 16, cols), bf16),
        scratch_shapes=[pltpu.VMEM((16, cols), f32)],
        cost_estimate=HINT,
    )(*weights, *vectors)


def place_first(pieces, index, count, size, lengths):
    total_rows, cols = pieces[0].shape[1:]
    rows = (total_rows - 16) // count

    def kernel(index_ref, *refs):
        ins = refs[: len(pieces)]
        w_ref, v_ref, last_ref, table = refs[len(pieces) :]
        for n, ref in enumerate(ins):
            for k in range(ref.shape[0]):
                block = index_ref[0] ^ distance_of(n, k)
                at = pl.ds(pl.multiple_of(block * rows, 16), rows)
                for g in range(count):
                    w_ref[g, at, :] = ref[k, g * rows : (g + 1) * rows, :]
                table[block] = ref[k, count * rows :, :].astype(f32)
        one, last = lengths
        for c in range(size):
            v_ref[:, c * one : (c + 1) * one] = table[c][:, :one]
            last_ref[:, c * last : (c + 1) * last] = table[c][8:9, :last]

    out = [(count, size * rows, cols), (16, size * lengths[0]), (1, size * lengths[1])]
    return pl.pallas_call(
        kernel,
        out_shape=[jax.ShapeDtypeStruct(o, d) for o, d in zip(out, (bf16, f32, f32))],
        grid_spec=pltpu.PrefetchScalarGridSpec(
            num_scalar_prefetch=1,
            grid=(1,),
            in_specs=[vmem(p.shape) for p in pieces],
            out_specs=[vmem(o) for o in out],
            scratch_shapes=[pltpu.VMEM((size, 16, cols), f32)],
        ),
        cost_estimate=HINT,
    )(index[None], *pieces)


def place_cols(pieces, index, widths, size):
    rows = pieces[0].shape[1]

    def kernel(index_ref, *refs):
        ins, outs = refs[: len(pieces)], refs[len(pieces) :]
        for n, ref in enumerate(ins):
            for k in range(ref.shape[0]):
                block = index_ref[0] ^ distance_of(n, k)
                at = 0
                for out_ref, width in zip(outs, widths):
                    here = pl.ds(pl.multiple_of(block * rows, 16), rows)
                    out_ref[here, :] = ref[k, :, at : at + width]
                    at += width

    out = [(size * rows, w) for w in widths]
    return pl.pallas_call(
        kernel,
        out_shape=[jax.ShapeDtypeStruct(o, bf16) for o in out],
        grid_spec=pltpu.PrefetchScalarGridSpec(
            num_scalar_prefetch=1,
            grid=(1,),
            in_specs=[vmem(p.shape) for p in pieces],
            out_specs=[vmem(o) for o in out],
        ),
        cost_estimate=HINT,
    )(index[None], *pieces)


PARTS = (
    ((3, (0, 1)), (1, (0, 1))),
    ((3, (2, 3)), (2, (2, 3))),
    ((1, (2, 3)),),
    ((2, (0, 1)),),
    ((0, (0, 1, 2, 3)),),
)


def split_out_specs(rows, step):
    return [
        pl.BlockSpec((sum(len(ks) for _, ks in part), rows, step), lambda i, *_: (0, 0, i))
        for part in PARTS
    ]


def split_shapes(rows, cols):
    return [
        jax.ShapeDtypeStruct(
            (sum(len(ks) for _, ks in part), rows, cols), bf16
        )
        for part in PARTS
    ]


def split_cols(pairs, index, size, step):
    total = pairs[0][0].shape[0]
    rows = total // size
    counts = [a.shape[1] // step for a, _ in pairs]
    starts = [sum(counts[:i]) for i in range(len(counts))]

    def kernel(index_ref, *refs):
        ins, outs = refs[: 2 * len(pairs)], refs[2 * len(pairs) :]
        for n, (first, count) in enumerate(zip(starts, counts)):

            @pl.when((pl.program_id(0) >= first) & (pl.program_id(0) < first + count))
            def _(n=n):
                for part, out_ref in zip(PARTS, outs):
                    at = 0
                    for offset, ks in part:
                        for k in ks:
                            block = index_ref[0] ^ (4 * k ^ offset)
                            here = pl.ds(pl.multiple_of(block * rows, 16), rows)
                            out_ref[at] = ins[2 * n][here, :] + ins[2 * n + 1][here, :]
                            at += 1

    specs = []
    for a, n in zip(starts, counts):
        spec = pl.BlockSpec((total, step), lambda i, *_, a=a, n=n: (0, jnp.clip(i - a, 0, n - 1)))
        specs += [spec, spec]
    return pl.pallas_call(
        kernel,
        out_shape=split_shapes(rows, sum(counts) * step),
        grid_spec=pltpu.PrefetchScalarGridSpec(
            num_scalar_prefetch=1,
            grid=(sum(counts),),
            in_specs=specs,
            out_specs=split_out_specs(rows, step),
        ),
        cost_estimate=HINT,
    )(index[None], *[item for pair in pairs for item in pair])


def gradients_other(tokens_t, deltas):
    width, rows = tokens_t.shape
    count, _, cols = deltas.shape

    def kernel(t_ref, d_ref, o_ref, s_ref):
        o_ref[0] = dot(t_ref[...], d_ref[0], NN).astype(bf16)
        s_ref[0] = dot(jnp.ones((8, rows), bf16), d_ref[0], NN)

    return pl.pallas_call(
        kernel,
        out_shape=[
            jax.ShapeDtypeStruct((count, width, cols), bf16),
            jax.ShapeDtypeStruct((count, 8, cols), f32),
        ],
        grid=(count,),
        in_specs=[vmem(tokens_t.shape), pl.BlockSpec((1, rows, cols), lambda g: (g, 0, 0))],
        out_specs=[
            pl.BlockSpec((1, width, cols), lambda g: (g, 0, 0)),
            pl.BlockSpec((1, 8, cols), lambda g: (g, 0, 0)),
        ],
        cost_estimate=HINT,
    )(tokens_t, deltas)


def gradients_own(
    tokens_t, deltas, others, other_sums, ready, table, index, core, size, one
):
    width, rows = tokens_t.shape
    count, _, cols = deltas.shape
    part_rows = width // size
    height = (count + 1) * part_rows + 16

    def kernel(at_ref, t_ref, d_ref, other_ref, sums_ref, r0_ref, r1_ref, table_ref, *refs):
        outs, total, own_sums, vec = refs[: len(PARTS)], refs[-3], refs[-2], refs[-1]
        g = pl.program_id(0)
        total[...] = dot(t_ref[...], d_ref[0], NN) + other_ref[0].astype(f32)
        own_sums[g] = dot(jnp.ones((8, rows), bf16), d_ref[0], NN)

        def blocks():
            for part, out_ref in zip(PARTS, outs):
                at = 0
                for offset, ks in part:
                    for k in ks:
                        yield at_ref[0] ^ (4 * k ^ offset), out_ref, at
                        at += 1

        for block, out_ref, at in blocks():
            value = total[pl.ds(pl.multiple_of(block * part_rows, 16), part_rows), :]
            out_ref[at, pl.ds(pl.multiple_of(g * part_rows, 16), part_rows), :] = value.astype(bf16)

        @pl.when(g == count - 1)
        def _():
            vec[...] = table_ref[...]
            for row, which in ((0, 0), (1, 2)):
                for ref, side in ((own_sums, 0), (sums_ref, 1)):
                    first = (at_ref[1] ^ side) * (size // 2)
                    for j in range(size // 2):
                        vec[first + j, row : row + 1, :one] = ref[which, 0:1, j * one : (j + 1) * one]
            for block, out_ref, at in blocks():
                here = pl.ds(pl.multiple_of(block * part_rows, 16), part_rows)
                value = r0_ref[here, :] + r1_ref[here, :]
                out_ref[at, count * part_rows : (count + 1) * part_rows, :] = value
                out_ref[at, (count + 1) * part_rows :, :] = vec[block].astype(bf16)

    return pl.pallas_call(
        kernel,
        out_shape=split_shapes(height, cols),
        grid_spec=pltpu.PrefetchScalarGridSpec(
            num_scalar_prefetch=1,
            grid=(count,),
            in_specs=[
                vmem(tokens_t.shape),
                pl.BlockSpec((1, rows, cols), lambda g, *_: (g, 0, 0)),
                pl.BlockSpec((1, width, cols), lambda g, *_: (g, 0, 0)),
                vmem(other_sums.shape),
                *[vmem(a.shape) for a in ready],
                vmem(table.shape),
            ],
            out_specs=[vmem(shape.shape) for shape in split_shapes(height, cols)],
            scratch_shapes=[
                pltpu.VMEM((width, cols), f32),
                pltpu.VMEM((count, 8, cols), f32),
                pltpu.VMEM(table.shape, f32),
            ],
        ),
        cost_estimate=HINT,
    )(jnp.stack([index, core]), tokens_t, deltas, others, other_sums, *ready, table)


def pack_table(first_sums, second_sums, inner_sums, core, size, cols):
    one = first_sums.shape[1] // size
    end = inner_sums.shape[1] // size

    def kernel(core_ref, a_ref, b_ref, inner_ref, out_ref, table):
        table[...] = jnp.zeros(table.shape, f32)
        out_ref[...] = jnp.zeros(out_ref.shape, f32)
        table[2:5, :] = a_ref[0:3, :]
        table[5:8, :] = b_ref[0:3, :]
        for c in range(size):
            out_ref[c, :, :one] = table[:, c * one : (c + 1) * one]
            d = (c + size // 2) % size
            here = inner_ref[0:1, c * end : (c + 1) * end]
            there = inner_ref[0:1, d * end : (d + 1) * end]
            out_ref[c, 8:9, :end] = jnp.where(core_ref[0] == 0, here, there)

    ins = (first_sums, second_sums, inner_sums)
    return pl.pallas_call(
        kernel,
        out_shape=jax.ShapeDtypeStruct((size, 16, cols), f32),
        grid_spec=pltpu.PrefetchScalarGridSpec(
            num_scalar_prefetch=1,
            grid=(1,),
            in_specs=[vmem(a.shape) for a in ins],
            out_specs=vmem((size, 16, cols)),
            scratch_shapes=[pltpu.VMEM((16, first_sums.shape[1]), f32)],
        ),
        cost_estimate=HINT,
    )(core[None], *ins)


def whole_call(kernel, outs, ins, blocks):
    return pl.pallas_call(
        kernel,
        out_shape=[jax.ShapeDtypeStruct(o, d) for o, d in outs],
        grid=(1,),
        in_specs=[vmem((n, *a.shape[1:])) for a, n in zip(ins, blocks)],
        out_specs=[vmem(o) for o, _ in outs],
        cost_estimate=HINT,
    )(*ins)


def corner_back(parts, size):
    return swap_dp(parts[0], 1, size), swap_dp(parts[1], 2, size)


def corner_add(parts, got):
    keep = parts[2:4]

    def kernel(one_ref, two_ref, r1_ref, r2_ref, o1_ref, o2_ref):
        o1_ref[...] = one_ref[...] + r2_ref[...]
        o2_ref[...] = two_ref[...] + r1_ref[...]

    return whole_call(
        kernel, [(item.shape, bf16) for item in keep], [*keep, *got], (2, 2, 2, 2)
    )


def near_back(sums, size):
    return swap_dp(sums[0], 1, size), swap_dp(sums[1], 2, size)


def near_add(own, first, got):
    def kernel(own_ref, f1_ref, f2_ref, r1_ref, r2_ref, keep_ref, *outs):
        def total(k):
            early = f1_ref[2 + k] if k < 2 else f2_ref[k]
            late = r2_ref[k] if k < 2 else r1_ref[k - 2]
            return own_ref[k].astype(f32) + early.astype(f32) + late.astype(f32)

        keep_ref[...] = total(0)
        for k in (1, 2, 3):
            outs[k - 1][...] = total(k).astype(bf16)

    shape = own.shape[1:]
    return whole_call(
        kernel, [(shape, f32)] + [(shape, bf16)] * 3, [own, *first, *got], (4, 4, 4, 2, 2)
    )


def far_back(sums, size):
    return [swap_dp(item, 4 * (k + 1), size) for k, item in enumerate(sums[1:])]


def project(tokens, weights, vectors, core, side):
    rows, width = tokens.shape
    cols = weights.shape[2]

    def kernel(core_ref, x_ref, w_ref, v_ref, q_out, k_out, v_out):
        half = core_ref[0] ^ side
        bias = jnp.where(half == 0, v_ref[0:8, :cols], v_ref[0:8, cols:])
        x = x_ref[...]
        q_out[...] = (dot(x, w_ref[0], NN) + bias[0:1]).astype(bf16)
        k_out[...] = dot(x, w_ref[1], NN).astype(bf16)
        v_out[...] = (dot(x, w_ref[2], NN) + bias[1:2]).astype(bf16)

    tile = pl.BlockSpec((ROWS, cols), lambda i, *_: (i, 0))
    return pl.pallas_call(
        kernel,
        out_shape=[jax.ShapeDtypeStruct((rows, cols), bf16)] * 3,
        grid_spec=pltpu.PrefetchScalarGridSpec(
            num_scalar_prefetch=1,
            grid=(rows // ROWS,),
            in_specs=[
                pl.BlockSpec((ROWS, width), lambda i, *_: (i, 0)),
                vmem(weights.shape),
                vmem(vectors.shape),
            ],
            out_specs=[tile] * 3,
        ),
        cost_estimate=HINT,
    )(core[None], tokens, weights, vectors)


def token_gradient(first_delta, deltas, weights, part, parts):
    count, rows, cols = deltas[0].shape
    width = weights[0].shape[1]
    steps = rows // ROWS // parts

    def kernel(f_ref, d0_ref, d1_ref, w0_ref, w1_ref, *refs):
        o_ref = refs[-1]
        total = f_ref[...]
        for d_ref, w_ref in ((d0_ref, w0_ref), (d1_ref, w1_ref)):
            for g in range(count):
                total = total + dot(d_ref[g], w_ref[g], NT)
        o_ref[...] = total

    tile = pl.BlockSpec((ROWS, width), lambda i: (i + part * steps, 0))
    delta_part = pl.BlockSpec((count, ROWS, cols), lambda i: (0, i + part * steps, 0))
    return pl.pallas_call(
        kernel,
        out_shape=jax.ShapeDtypeStruct((rows, width), f32),
        grid=(steps,),
        in_specs=[tile, delta_part, delta_part] + [vmem(weights[0].shape)] * 2,
        out_specs=tile,
        input_output_aliases={0: 0},
        cost_estimate=pl.CostEstimate(
            flops=4 * count * rows * width * cols // parts,
            transcendentals=0,
            bytes_accessed=16 * rows * cols // parts,
        ),
    )(first_delta, *deltas, *weights)


def center(values):
    mean = jnp.mean(values, axis=-1, keepdims=True)
    centred = values - mean
    var = jnp.mean(centred * centred, axis=-1, keepdims=True)
    rinv = lax.rsqrt(var + norm_eps)
    return centred * rinv, rinv


def norm_back(grad, normed, rinv, gain):
    scaled = grad * gain
    return rinv * (
        scaled
        - jnp.mean(scaled, axis=-1, keepdims=True)
        - normed * jnp.mean(scaled * normed, axis=-1, keepdims=True)
    )


def add_rows(ref, items):
    for i, item in enumerate(items):
        ref[i : i + 1, : item.shape[1]] += jnp.sum(item, axis=0, keepdims=True)


def clear(*refs):
    @pl.when(pl.program_id(0) == 0)
    def _():
        for ref in refs:
            ref[...] = jnp.zeros(ref.shape, f32)


def row_call(kernel, tiles, wholes, outs, sums):
    rows = tiles[0].shape[0]

    def tile(cols):
        return pl.BlockSpec((ROWS, cols), lambda i: (i, 0))

    return pl.pallas_call(
        kernel,
        out_shape=[jax.ShapeDtypeStruct((rows, n), d) for n, d in outs]
        + [jax.ShapeDtypeStruct((8, n), f32) for n in sums],
        grid=(rows // ROWS,),
        in_specs=[tile(a.shape[1]) for a in tiles] + [vmem(a.shape) for a in wholes],
        out_specs=[tile(n) for n, _ in outs] + [vmem((8, n)) for n in sums],
        cost_estimate=HINT,
    )(*tiles, *wholes)


def first_block(tokens, context, weights, vectors):
    def kernel(x_ref, c0_ref, c1_ref, w0_ref, w1_ref, v_ref, out, low):
        total = dot(c0_ref[...], w0_ref[...], NT) + dot(c1_ref[...], w1_ref[...], NT)
        total = x_ref[...].astype(f32) + total + v_ref[2:3]
        out[...] = total
        low[...] = (center(total)[0] * v_ref[3:4] + v_ref[4:5]).astype(bf16)

    width = tokens.shape[1]
    return row_call(
        kernel, [tokens, *context], [*weights, vectors], [(width, f32), (width, bf16)], ()
    )


def outer_block(hidden, cotangent, act, weights, vectors):
    def kernel(
        h_ref, c_ref, a0_ref, a1_ref, w0_ref, w1_ref, v_ref, out, delta, low, sums
    ):
        clear(sums)

        feed = dot(a0_ref[...], w0_ref[...], NT) + dot(a1_ref[...], w1_ref[...], NT)
        normed, rinv = center(h_ref[...].astype(f32) + (v_ref[5:6] + feed))
        out[...] = normed * v_ref[6:7] + v_ref[7:8]
        cot = c_ref[...].astype(f32)
        found = norm_back(cot, normed, rinv, v_ref[6:7])
        delta[...] = found
        low[...] = found.astype(bf16)
        add_rows(sums, (found, cot * normed, cot))

    width = hidden.shape[1]
    return row_call(
        kernel,
        [hidden, cotangent, *act],
        [*weights, vectors],
        [(width, f32), (width, f32), (width, bf16)],
        (width,),
    )


def inner_back(second_delta, inner_delta, first_in, weights, vectors):
    def kernel(
        s_ref, d0_ref, d1_ref, f_ref, w0_ref, w1_ref, v_ref, delta, low, sums, inner
    ):
        clear(sums, inner)
        ones = jnp.ones((8, ROWS), bf16)
        half = d0_ref.shape[1]
        inner[:, :half] += dot(ones, d0_ref[...], NN)
        inner[:, half:] += dot(ones, d1_ref[...], NN)

        grad = dot(d0_ref[...], w0_ref[...], NT) + dot(d1_ref[...], w1_ref[...], NT)
        grad = s_ref[...] + grad
        normed, rinv = center(f_ref[...])
        found = norm_back(grad, normed, rinv, v_ref[3:4])
        delta[...] = found
        low[...] = found.astype(bf16)
        add_rows(sums, (found, grad * normed, grad))

    width = first_in.shape[1]
    return row_call(
        kernel,
        [second_delta, *inner_delta, first_in],
        [*weights, vectors],
        [(width, f32), (width, bf16)],
        (width, 2 * inner_delta[0].shape[1]),
    )


def three_parts(row):
    high = row.astype(bf16).astype(f32)
    middle = (row - high).astype(bf16).astype(f32)
    return [high, middle, row - high - middle]


def extra_lanes(shape, keys_valid):
    lane = lax.broadcasted_iota(jnp.int32, shape, 1) % HD
    row = lax.broadcasted_iota(jnp.int32, shape, 0)
    bias = jnp.where(row < keys_valid, 0.0, masked_score)
    return jnp.where(lane == 0, bias, jnp.where(lane < 4, 1.0, 0.0)).astype(bf16)


def extra_rows(first, row, length):
    rows = [jnp.full((1, length), first, f32)]
    rows += three_parts(row) if row is not None else []
    rows.append(jnp.zeros((16 - len(rows), length), f32))
    return jnp.concatenate(rows, 0).astype(bf16)


def with_rows(own_t, h, first, row):
    length = own_t.shape[1]
    own = own_t[h * HD : (h + 1) * HD]
    rest = [extra_rows(first, row, length), jnp.zeros((HD - 16, length), bf16)]
    return jnp.concatenate([own] + rest if h == 0 else rest + [own], 0)


def attend_forward_kernel(lens, q_ref, k_ref, v_ref, ctx_ref, lse_ref):
    seq_len, lanes = q_ref.shape
    lane = lax.broadcasted_iota(jnp.int32, (seq_len, lanes), 1)
    extra = extra_lanes((seq_len, lanes), lens[pl.program_id(0)])
    ones = jnp.ones((16, seq_len), bf16)
    loaded = {}

    def scores(h):
        if h == 0:
            query_t = (q_ref[...] * jnp.bfloat16(score_scale)).T
            loaded[0] = (query_t, k_ref[...], v_ref[...].T)
        query_t, keys, _ = loaded[0]
        return dot(jnp.where(lane // HD == h, keys, extra), with_rows(query_t, h, 1.0, None), NN)

    pieces = []
    ahead = scores(0)
    for h in range(2):
        now = ahead
        if h == 0:
            ahead = scores(1)
        top = jnp.max(now, axis=0, keepdims=True)
        expo = jnp.exp(now - top).astype(bf16)
        value_t = loaded[0][2][h * HD : (h + 1) * HD]
        found = dot(jnp.concatenate([value_t, ones], 0), expo, NN)
        total = found[HD : HD + 1]
        pieces.append(found[:HD] / total)
        lse_ref[0, 0, h : h + 1, :] = top + jnp.log(total)
        if h == 1:
            ctx_ref[...] = jnp.concatenate(pieces, 0).T.astype(bf16)
            pieces = []


def attend_backward_kernel(lens, q_ref, k_ref, v_ref, d_ref, c_ref, lse_ref, out_ref):
    seq_len, lanes = q_ref.shape
    lane = lax.broadcasted_iota(jnp.int32, (seq_len, lanes), 1)
    extra = extra_lanes((seq_len, lanes), lens[pl.program_id(0)])
    loaded = {}

    def products(h):
        if h == 0:
            query = q_ref[...] * jnp.bfloat16(score_scale)
            delta = d_ref[...]
            delta_t = delta.T
            inner = delta_t.astype(f32) * c_ref[...].T.astype(f32)
            keys = k_ref[...]
            loaded[0] = (query, query.T, delta, delta_t, inner, keys, keys.T, v_ref[...])
        _, query_t, _, delta_t, inner, keys, _, values = loaded[0]
        own = lane // HD == h
        inner = jnp.sum(inner[h * HD : (h + 1) * HD], axis=0, keepdims=True)
        lse = lse_ref[0, 0, h : h + 1, :]
        logs = dot(jnp.where(own, keys, extra), with_rows(query_t, h, 1.0, -lse), NN)
        centred = dot(jnp.where(own, values, extra), with_rows(delta_t, h, 0.0, -inner), NN)
        return logs, centred

    ahead = products(0)
    for h in range(2):
        logs, centred = ahead
        if h == 0:
            ahead = products(1)
        query, _, delta, _, _, _, keys_t, _ = loaded[0]
        probs = jnp.exp(logs)
        score_delta = (probs * centred).astype(bf16)
        own = lane // HD == h
        part_v = dot(probs.astype(bf16), jnp.where(own, delta, jnp.bfloat16(0)), NN)
        part_k = dot(score_delta, jnp.where(own, query, jnp.bfloat16(0)), NN)
        part_q = dot(keys_t[h * HD : (h + 1) * HD], score_delta, NN)
        if h == 0:
            dv, dk, dq = part_v, part_k, part_q
        else:
            out_ref[0] = (jnp.concatenate([dq, part_q], 0).T * score_scale).astype(bf16)
            out_ref[1] = (dk + part_k).astype(bf16)
            out_ref[2] = (dv + part_v).astype(bf16)


def attend_call(kernel, lens, operands, lse_in, seq_count):
    rows, cols = operands[0].shape
    seq_len = rows // seq_count
    pairs = cols // (2 * HD)
    tile = pl.BlockSpec((seq_len, 2 * HD), lambda s, p, *_: (s, p))
    stat = pl.BlockSpec((1, 1, 2, seq_len), lambda s, p, *_: (s, p, 0, 0))
    if lse_in:
        out_shape = jax.ShapeDtypeStruct((3, rows, cols), bf16)
        out_specs = pl.BlockSpec((3, seq_len, 2 * HD), lambda s, p, *_: (0, s, p))
    else:
        out_shape = [
            jax.ShapeDtypeStruct((rows, cols), bf16),
            jax.ShapeDtypeStruct((seq_count, pairs, 2, seq_len), f32),
        ]
        out_specs = [tile, stat]
    return pl.pallas_call(
        kernel,
        out_shape=out_shape,
        grid_spec=pltpu.PrefetchScalarGridSpec(
            num_scalar_prefetch=1,
            grid=(seq_count, pairs),
            in_specs=[tile] * len(operands) + [stat] * len(lse_in),
            out_specs=out_specs,
        ),
        cost_estimate=HINT,
    )(lens, *operands, *lse_in)


def on_device(
    tokens,
    cotangent,
    lengths,
    query_weight,
    key_weight,
    value_weight,
    out_weight,
    query_bias,
    value_bias,
    out_bias,
    first_gain,
    first_shift,
    inner_weight,
    inner_bias,
    outer_weight,
    outer_bias,
    second_gain,
    second_shift,
):
    size = lax.axis_size("dp")
    index = lax.axis_index("dp")
    core = lax.axis_index("tensor")
    orders = stage_orders(size)
    seq_count = lengths.shape[0] // 2
    lens = lax.dynamic_slice_in_dim(lengths, core * seq_count, seq_count, 0)
    fast = size == 16 and query_weight.shape[0] % 16 == 0
    half = query_weight.shape[1]
    step = half

    vectors = (
        query_bias,
        value_bias,
        out_bias,
        first_gain,
        first_shift,
        outer_bias,
        second_gain,
        second_shift,
        inner_bias,
    )
    bounds = [0]
    for item in vectors:
        bounds.append(bounds[-1] + item.shape[0])
    projections = (query_weight, key_weight, value_weight)
    out_t = out_weight.T
    outer_t = outer_weight.T

    if fast:
        shard = pack_first(projections, vectors)
        far = [swap_dp(shard, d, size) for d in (8, 4, 12)]
        low, high = jnp.stack([shard, far[0]]), jnp.stack(far[1:])
        two_low, one_high = swap_dp(low, 2, size), swap_dp(high, 1, size)
        one_low, two_high = swap_dp(low, 1, size), swap_dp(high, 2, size)
        shard_a = jnp.concatenate([out_t, inner_weight], 1)
        far_a = swap_dp(after(shard_a, low, high), 8, size)
        tokens_t = tokens.T
        pieces = [low, high, one_low, one_high, two_low, two_high]
        pieces += [swap_dp(two_low, 1, size), swap_dp(one_high, 2, size)]
        far_a, *pieces, tokens_t = lax.optimization_barrier((far_a, *pieces, tokens_t))
        low_a = jnp.stack([shard_a, far_a])
        high_a = swap_dp(low_a, 4, size)
        two_low_a, one_low_a = swap_dp(low_a, 2, size), swap_dp(low_a, 1, size)
        wqkv0, vecs, ib = place_first(
            pieces, index, 3, size, (query_bias.shape[0], inner_bias.shape[0])
        )
    else:
        own_vec = jnp.concatenate(vectors)[None, :]
        all_vec = gather_rows(own_vec, orders[0], size, index).astype(f32)
        found = [all_vec[:, a:b].reshape(1, -1) for a, b in zip(bounds[:-1], bounds[1:])]
        vecs = jnp.concatenate(found[:-1] + [jnp.zeros_like(found[0])] * 8, 0)
        ib = found[-1]
        wqkv0 = jnp.stack(
            [gather_rows(w, o, size, index) for w, o in zip(projections, orders)]
        )
        wo0 = gather_rows(out_t, orders[2], size, index)
        wi0 = gather_rows(inner_weight, orders[0], size, index)
        wu0 = gather_rows(outer_t, orders[1], size, index)

    wqkv = (wqkv0, swap_core(wqkv0))
    hidden_half = inner_weight.shape[1]
    ib = (
        jnp.where(core == 0, ib[:, :hidden_half], ib[:, hidden_half:]),
        jnp.where(core == 0, ib[:, hidden_half:], ib[:, :hidden_half]),
    )

    q, k, v, ctx, lse = [], [], [], [], []
    for t in range(2):
        found = project(tokens, wqkv[t], vecs, core, t)
        q.append(found[0])
        k.append(found[1])
        v.append(found[2])
    if fast:
        far_b = swap_dp(after(outer_t, wqkv[0]), 8, size)
        high_a, far_b, one_low_a, two_low_a, *q = lax.optimization_barrier(
            (high_a, far_b, one_low_a, two_low_a, *q)
        )
        one_high_a, two_high_a = swap_dp(high_a, 1, size), swap_dp(high_a, 2, size)
        low_b = jnp.stack([outer_t, far_b])
        two_low_b, one_low_b = swap_dp(low_b, 2, size), swap_dp(low_b, 1, size)
        high_b = swap_dp(low_b, 4, size)
    for t in range(2):
        if fast and t == 1:
            q[1] = after(q[1], ctx[0])
        c, s = attend_call(attend_forward_kernel, lens, (q[t], k[t], v[t]), (), seq_count)
        lse.append(s)
        if fast and t == 0:
            pieces_a = [low_a, high_a, one_low_a, one_high_a, two_low_a, two_high_a]
            *pieces_a, high_b, two_low_b, one_low_b, c = lax.optimization_barrier(
                (*pieces_a, high_b, two_low_b, one_low_b, c)
            )
            pieces_a += [swap_dp(pieces_a[4], 1, size), swap_dp(pieces_a[3], 2, size)]
        if fast and t == 1:
            *pieces_a, c = lax.optimization_barrier((*pieces_a, c))
            one_high_b, two_high_b = swap_dp(high_b, 1, size), swap_dp(high_b, 2, size)
            wo0, wi0 = place_cols(pieces_a, index, (half, inner_weight.shape[1]), size)
        ctx.append(c)

    wo = (wo0, swap_core(wo0))
    wi = (wi0, swap_core(wi0))
    first_in, hidden = first_block(tokens, ctx, wo, vecs)
    if fast:
        one_high_b, two_low_b, hidden = lax.optimization_barrier((one_high_b, two_low_b, hidden))
        pieces_b = [low_b, high_b, one_low_b, one_high_b, two_low_b, two_high_b]
        pieces_b += [swap_dp(two_low_b, 1, size), swap_dp(one_high_b, 2, size)]
    act, slope = [], []
    for t in range(2):
        u = dot(hidden, wi[t], NN) + ib[t]
        cdf = 0.5 * (1.0 + lax.erf(u * (0.5**0.5)))
        act.append((u * cdf).astype(bf16))
        pdf = jnp.exp(-0.5 * u * u) * 0.3989422804014327
        slope.append((cdf + u * pdf).astype(bf16))
        if fast and t == 0:
            *pieces_b, act[0] = lax.optimization_barrier((*pieces_b, act[0]))
            (wu0,) = place_cols(pieces_b, index, (inner_weight.shape[1],), size)
            hidden = after(hidden, wu0)
    wu = (wu0, swap_core(wu0))
    layer_out, second_delta, feed_delta, second_sums = outer_block(
        hidden, cotangent, act, wu, vecs
    )

    def product(left, right):
        other = dot(left, right[1], TN).astype(bf16)
        other = swap_core(other)
        return dot(left, right[0], TN).astype(bf16), other

    gu = product(feed_delta, act)
    feed_delta, *gu = lax.optimization_barrier((feed_delta, *gu))
    inner_delta = [None, None]
    for t in (1, 0):
        inner_delta[t] = (dot(feed_delta, wu[t], NN) * slope[t].astype(f32)).astype(bf16)
    gi = product(hidden, inner_delta)
    inner_delta[0], inner_delta[1], *gi = lax.optimization_barrier((*inner_delta, *gi))
    if fast:
        parts_u = split_cols([gu, gi], index, size, 2 * step)
        first_u = corner_back(parts_u, size)
        inner_delta[0], inner_delta[1] = [after(d, parts_u[4]) for d in inner_delta]
    first_delta, branch_delta, first_sums, inner_sums = inner_back(
        second_delta, inner_delta, first_in, wi, vecs
    )
    go = list(product(branch_delta, ctx))
    ctx_delta = [dot(branch_delta, wo[t], NN).astype(bf16) for t in range(2)]

    def joined(pair):
        return jnp.where(
            core == 0, jnp.concatenate(pair, 1), jnp.concatenate(pair[::-1], 1)
        )

    if fast:
        table = pack_table(first_sums, second_sums, inner_sums, core, size, half)
        *first_u, table, ctx_delta[0], ctx_delta[1], go[0], go[1] = lax.optimization_barrier(
            (*first_u, table, *ctx_delta, *go)
        )
        sums_u = corner_add(parts_u, first_u)
        got_u = near_back(sums_u, size)
        ctx_delta[1] = after(ctx_delta[1], table, sums_u[0])

    def attend_back(t):
        return attend_call(
            attend_backward_kernel,
            lens,
            (q[t], k[t], v[t], ctx_delta[t], ctx[t]),
            (lse[t],),
            seq_count,
        )

    deltas = [None, None]
    deltas[1] = attend_back(1)
    if fast:
        *got_u, deltas[1] = lax.optimization_barrier((*got_u, deltas[1]))
        last_u = near_add(parts_u[4], first_u, got_u)
        got_u = far_back(last_u, size)
        deltas[1] = after(deltas[1], last_u[0])
        others, other_sums = gradients_other(tokens_t, deltas[1])
        ctx_delta[0] = after(ctx_delta[0], others)
        others = swap_core(others)
        deltas[0] = attend_back(0)
        parts_q = gradients_own(
            tokens_t,
            deltas[0],
            others,
            other_sums,
            go,
            table,
            index,
            core,
            size,
            query_bias.shape[0],
        )
        *got_u, own = lax.optimization_barrier((*got_u, parts_q[4]))
        parts_q = [*parts_q[:4], own]
        first_q = corner_back(parts_q, size)
        token_grad = token_gradient(
            after(first_delta, parts_q[4]), [after(d, parts_q[4]) for d in deltas], wqkv, 0, 2
        )
        *first_q, token_grad = lax.optimization_barrier((*first_q, token_grad))

        def total(last, got):
            return last[0] + got[0].astype(f32) + got[1].astype(f32) + got[2].astype(f32)

        out_ui = total(last_u, got_u)
        hidden_half = out_ui.shape[1] // 2
        out_gu = out_ui[:, :hidden_half].T
        out_gi = out_ui[:, hidden_half:]
        sums_q = corner_add(parts_q, first_q)
        got_q = near_back(sums_q, size)
        last_q = near_add(parts_q[4], first_q, got_q)
        got_q = far_back(last_q, size)
        token_grad = token_gradient(token_grad, [after(d, last_q[0]) for d in deltas], wqkv, 1, 2)
        out_q = total(last_q, got_q)
        n = query_weight.shape[0]
        out_qkv = [out_q[g * n : (g + 1) * n] for g in range(3)]
        out_go = out_q[3 * n : 4 * n].T
        vec = out_q[4 * n :]
        vec = vec + swap_core(vec)
        vec_out = [vec[i, : item.shape[0]] for i, item in enumerate(vectors)]
    else:
        deltas[0] = attend_back(0)
        token_grad = token_gradient(first_delta, deltas, wqkv, 0, 1)

        def reduce(pair, order):
            summed = (pair[0].astype(f32) + pair[1].astype(f32)).astype(bf16)
            return scatter_rows(summed, order, size, index)

        out_gu = reduce(gu, orders[1]).T
        out_gi = reduce(gi, orders[0])
        out_go = reduce(go, orders[2]).T
        out_qkv = [
            reduce(product(tokens, [d[g] for d in deltas]), order) for g, order in enumerate(orders)
        ]
        bias_grads = [
            joined([jnp.sum(d[g].astype(f32), axis=0, keepdims=True) for d in deltas]) for g in (0, 2)
        ]
        bias_grads += [s[i : i + 1] for s in (first_sums, second_sums) for i in range(3)]
        bias_grads.append(joined(jnp.split(inner_sums[:1], 2, 1)))
        packed = jnp.concatenate([item.reshape(size, -1) for item in bias_grads], axis=1)
        packed = packed + swap_core(packed)
        own = scatter_rows(packed, orders[0], size, index).reshape(-1)
        vec_out = [own[a:b] for a, b in zip(bounds[:-1], bounds[1:])]
    return (
        layer_out,
        token_grad,
        out_qkv[0],
        out_qkv[1],
        out_qkv[2],
        out_go,
        vec_out[0],
        vec_out[1],
        vec_out[2],
        vec_out[3],
        vec_out[4],
        out_gi,
        vec_out[8],
        out_gu,
        vec_out[5],
        vec_out[6],
        vec_out[7],
    )


def solution(mesh):
    both = P(("dp", "tensor"), None)
    cols = P("dp", "tensor")
    rows = P("tensor", "dp")
    vec = P("dp")
    in_specs = (
        both, both, vec, cols, cols, cols, rows, vec, vec, vec, vec, vec, cols, vec, rows, vec, vec, vec,
    )
    out_specs = (
        both, both, cols, cols, cols, rows, vec, vec, vec, vec, vec, cols, vec, rows, vec, vec, vec,
    )
    return jax.shard_map(
        on_device, mesh=mesh, in_specs=in_specs, out_specs=out_specs, check_vma=False
    )
```

```python
import jax
import jax.numpy as jnp
from jax import lax
from jax.experimental import pallas as pl
from jax.experimental.pallas import tpu as pltpu
from jax.sharding import PartitionSpec as P

HD = 64
norm_eps = 1e-12
masked_score = -1000000000.0
score_scale = HD ** (-0.5)
f32 = jnp.float32
bf16 = jnp.bfloat16
NT = (((1,), (1,)), ((), ()))
TN = (((0,), (0,)), ((), ()))
NN = (((1,), (0,)), ((), ()))
ROWS = 256


def dot(left, right, dims):
    return lax.dot_general(left, right, dims, preferred_element_type=f32)


def stage_orders(size):
    up = [1 << k for k in range(size.bit_length() - 1)]
    down = up[::-1]
    return (down, down[:-2] + [down[-1], down[-2]], [down[0]] + up[:-1])


def swap_dp(value, mask, size):
    return lax.ppermute(value, "dp", [(i, i ^ mask) for i in range(size)])


def swap_core(value):
    return lax.ppermute(value, "tensor", [(0, 1), (1, 0)])


def after(value, *others):
    return lax.optimization_barrier((value, *others))[0]


def gather_rows(shard, order, size, index):
    rows, cols = shard.shape
    have = []
    buf = shard
    for mask in order:
        received = swap_dp(buf, mask, size)
        have = sorted(have + [mask], reverse=True)
        axis = have.index(mask)
        buf = jnp.where(
            (index & mask) != 0,
            jnp.stack([received, buf], axis),
            jnp.stack([buf, received], axis),
        )
    return buf.reshape(size * rows, cols)


def scatter_rows(own, order, size, index):
    total, cols = own.shape
    have = sorted(order, reverse=True)
    buf = own.reshape([2] * len(have) + [total // size, cols])
    for mask in order[::-1]:
        axis = have.index(mask)
        bit = ((index & mask) != 0).astype(jnp.int32)
        keep = lax.dynamic_index_in_dim(buf, bit, axis, keepdims=False)
        give = lax.dynamic_index_in_dim(buf, 1 - bit, axis, keepdims=False)
        received = swap_dp(give, mask, size)
        buf = keep.astype(f32) + received.astype(f32)
        have.remove(mask)
        if have:
            buf = buf.astype(own.dtype)
    return buf


HINT = pl.CostEstimate(flops=1, transcendentals=0, bytes_accessed=1)


def distance_of(piece, k):
    return (4 * (piece % 2) + 8 * k) ^ piece // 2


def vmem(shape):
    return pl.BlockSpec(shape, lambda *_: (0,) * len(shape))


def pack_first(weights, vectors):
    rows, cols = weights[0].shape
    count = len(weights)

    def kernel(*refs):
        ins, out_ref, table = refs[: count + len(vectors)], refs[-2], refs[-1]
        for g in range(count):
            out_ref[g * rows : (g + 1) * rows, :] = ins[g][...]
        table[...] = jnp.zeros(table.shape, f32)
        for i, ref in enumerate(ins[count:]):
            table[i : i + 1, : ref.shape[0]] = ref[...].astype(f32)[None, :]
        out_ref[count * rows :, :] = table[...].astype(bf16)

    return pl.pallas_call(
        kernel,
        out_shape=jax.ShapeDtypeStruct((count * rows + 16, cols), bf16),
        scratch_shapes=[pltpu.VMEM((16, cols), f32)],
        cost_estimate=HINT,
    )(*weights, *vectors)


def place_first(pieces, index, count, size, lengths):
    total_rows, cols = pieces[0].shape[1:]
    rows = (total_rows - 16) // count

    def kernel(index_ref, *refs):
        ins = refs[: len(pieces)]
        w_ref, v_ref, last_ref, table = refs[len(pieces) :]
        for n, ref in enumerate(ins):
            for k in range(ref.shape[0]):
                block = index_ref[0] ^ distance_of(n, k)
                at = pl.ds(pl.multiple_of(block * rows, 16), rows)
                for g in range(count):
                    w_ref[g, at, :] = ref[k, g * rows : (g + 1) * rows, :]
                table[block] = ref[k, count * rows :, :].astype(f32)
        one, last = lengths
        for c in range(size):
            v_ref[:, c * one : (c + 1) * one] = table[c][:, :one]
            last_ref[:, c * last : (c + 1) * last] = table[c][8:9, :last]

    out = [(count, size * rows, cols), (16, size * lengths[0]), (1, size * lengths[1])]
    return pl.pallas_call(
        kernel,
        out_shape=[jax.ShapeDtypeStruct(o, d) for o, d in zip(out, (bf16, f32, f32))],
        grid_spec=pltpu.PrefetchScalarGridSpec(
            num_scalar_prefetch=1,
            grid=(1,),
            in_specs=[vmem(p.shape) for p in pieces],
            out_specs=[vmem(o) for o in out],
            scratch_shapes=[pltpu.VMEM((size, 16, cols), f32)],
        ),
        cost_estimate=HINT,
    )(index[None], *pieces)


def place_cols(pieces, index, widths, size):
    rows = pieces[0].shape[1]

    def kernel(index_ref, *refs):
        ins, outs = refs[: len(pieces)], refs[len(pieces) :]
        for n, ref in enumerate(ins):
            for k in range(ref.shape[0]):
                block = index_ref[0] ^ distance_of(n, k)
                at = 0
                for out_ref, width in zip(outs, widths):
                    here = pl.ds(pl.multiple_of(block * rows, 16), rows)
                    out_ref[here, :] = ref[k, :, at : at + width]
                    at += width

    out = [(size * rows, w) for w in widths]
    return pl.pallas_call(
        kernel,
        out_shape=[jax.ShapeDtypeStruct(o, bf16) for o in out],
        grid_spec=pltpu.PrefetchScalarGridSpec(
            num_scalar_prefetch=1,
            grid=(1,),
            in_specs=[vmem(p.shape) for p in pieces],
            out_specs=[vmem(o) for o in out],
        ),
        cost_estimate=HINT,
    )(index[None], *pieces)


PARTS = (
    ((3, (0, 1)), (1, (0, 1))),
    ((3, (2, 3)), (2, (2, 3))),
    ((1, (2, 3)),),
    ((2, (0, 1)),),
    ((0, (0, 1, 2, 3)),),
)


def split_out_specs(rows, step):
    return [
        pl.BlockSpec((sum(len(ks) for _, ks in part), rows, step), lambda i, *_: (0, 0, i))
        for part in PARTS
    ]


def split_shapes(rows, cols):
    return [
        jax.ShapeDtypeStruct(
            (sum(len(ks) for _, ks in part), rows, cols), bf16
        )
        for part in PARTS
    ]


def split_cols(pairs, index, size, step):
    total = pairs[0][0].shape[0]
    rows = total // size
    counts = [a.shape[1] // step for a, _ in pairs]
    starts = [sum(counts[:i]) for i in range(len(counts))]

    def kernel(index_ref, *refs):
        ins, outs = refs[: 2 * len(pairs)], refs[2 * len(pairs) :]
        for n, (first, count) in enumerate(zip(starts, counts)):

            @pl.when((pl.program_id(0) >= first) & (pl.program_id(0) < first + count))
            def _(n=n):
                for part, out_ref in zip(PARTS, outs):
                    at = 0
                    for offset, ks in part:
                        for k in ks:
                            block = index_ref[0] ^ (4 * k ^ offset)
                            here = pl.ds(pl.multiple_of(block * rows, 16), rows)
                            out_ref[at] = ins[2 * n][here, :] + ins[2 * n + 1][here, :]
                            at += 1

    specs = []
    for a, n in zip(starts, counts):
        spec = pl.BlockSpec((total, step), lambda i, *_, a=a, n=n: (0, jnp.clip(i - a, 0, n - 1)))
        specs += [spec, spec]
    return pl.pallas_call(
        kernel,
        out_shape=split_shapes(rows, sum(counts) * step),
        grid_spec=pltpu.PrefetchScalarGridSpec(
            num_scalar_prefetch=1,
            grid=(sum(counts),),
            in_specs=specs,
            out_specs=split_out_specs(rows, step),
        ),
        cost_estimate=HINT,
    )(index[None], *[item for pair in pairs for item in pair])


def gradients_other(tokens_t, deltas):
    width, rows = tokens_t.shape
    count, _, cols = deltas.shape

    def kernel(t_ref, d_ref, o_ref, s_ref):
        o_ref[0] = dot(t_ref[...], d_ref[0], NN).astype(bf16)
        s_ref[0] = dot(jnp.ones((8, rows), bf16), d_ref[0], NN)

    return pl.pallas_call(
        kernel,
        out_shape=[
            jax.ShapeDtypeStruct((count, width, cols), bf16),
            jax.ShapeDtypeStruct((count, 8, cols), f32),
        ],
        grid=(count,),
        in_specs=[vmem(tokens_t.shape), pl.BlockSpec((1, rows, cols), lambda g: (g, 0, 0))],
        out_specs=[
            pl.BlockSpec((1, width, cols), lambda g: (g, 0, 0)),
            pl.BlockSpec((1, 8, cols), lambda g: (g, 0, 0)),
        ],
        cost_estimate=HINT,
    )(tokens_t, deltas)


def gradients_own(
    tokens_t, deltas, others, other_sums, ready, table, index, core, size, one
):
    width, rows = tokens_t.shape
    count, _, cols = deltas.shape
    part_rows = width // size
    height = (count + 1) * part_rows + 16

    def kernel(at_ref, t_ref, d_ref, other_ref, sums_ref, r0_ref, r1_ref, table_ref, *refs):
        outs, total, own_sums, vec = refs[: len(PARTS)], refs[-3], refs[-2], refs[-1]
        g = pl.program_id(0)
        total[...] = dot(t_ref[...], d_ref[0], NN) + other_ref[0].astype(f32)
        own_sums[g] = dot(jnp.ones((8, rows), bf16), d_ref[0], NN)

        def blocks():
            for part, out_ref in zip(PARTS, outs):
                at = 0
                for offset, ks in part:
                    for k in ks:
                        yield at_ref[0] ^ (4 * k ^ offset), out_ref, at
                        at += 1

        for block, out_ref, at in blocks():
            value = total[pl.ds(pl.multiple_of(block * part_rows, 16), part_rows), :]
            out_ref[at, pl.ds(pl.multiple_of(g * part_rows, 16), part_rows), :] = value.astype(bf16)

        @pl.when(g == count - 1)
        def _():
            vec[...] = table_ref[...]
            for row, which in ((0, 0), (1, 2)):
                for ref, side in ((own_sums, 0), (sums_ref, 1)):
                    first = (at_ref[1] ^ side) * (size // 2)
                    for j in range(size // 2):
                        vec[first + j, row : row + 1, :one] = ref[which, 0:1, j * one : (j + 1) * one]
            for block, out_ref, at in blocks():
                here = pl.ds(pl.multiple_of(block * part_rows, 16), part_rows)
                value = r0_ref[here, :] + r1_ref[here, :]
                out_ref[at, count * part_rows : (count + 1) * part_rows, :] = value
                out_ref[at, (count + 1) * part_rows :, :] = vec[block].astype(bf16)

    return pl.pallas_call(
        kernel,
        out_shape=split_shapes(height, cols),
        grid_spec=pltpu.PrefetchScalarGridSpec(
            num_scalar_prefetch=1,
            grid=(count,),
            in_specs=[
                vmem(tokens_t.shape),
                pl.BlockSpec((1, rows, cols), lambda g, *_: (g, 0, 0)),
                pl.BlockSpec((1, width, cols), lambda g, *_: (g, 0, 0)),
                vmem(other_sums.shape),
                *[vmem(a.shape) for a in ready],
                vmem(table.shape),
            ],
            out_specs=[vmem(shape.shape) for shape in split_shapes(height, cols)],
            scratch_shapes=[
                pltpu.VMEM((width, cols), f32),
                pltpu.VMEM((count, 8, cols), f32),
                pltpu.VMEM(table.shape, f32),
            ],
        ),
        cost_estimate=HINT,
    )(jnp.stack([index, core]), tokens_t, deltas, others, other_sums, *ready, table)


def pack_table(first_sums, second_sums, inner_sums, core, size, cols):
    one = first_sums.shape[1] // size
    end = inner_sums.shape[1] // size

    def kernel(core_ref, a_ref, b_ref, inner_ref, out_ref, table):
        table[...] = jnp.zeros(table.shape, f32)
        out_ref[...] = jnp.zeros(out_ref.shape, f32)
        table[2:5, :] = a_ref[0:3, :]
        table[5:8, :] = b_ref[0:3, :]
        for c in range(size):
            out_ref[c, :, :one] = table[:, c * one : (c + 1) * one]
            d = (c + size // 2) % size
            here = inner_ref[0:1, c * end : (c + 1) * end]
            there = inner_ref[0:1, d * end : (d + 1) * end]
            out_ref[c, 8:9, :end] = jnp.where(core_ref[0] == 0, here, there)

    ins = (first_sums, second_sums, inner_sums)
    return pl.pallas_call(
        kernel,
        out_shape=jax.ShapeDtypeStruct((size, 16, cols), f32),
        grid_spec=pltpu.PrefetchScalarGridSpec(
            num_scalar_prefetch=1,
            grid=(1,),
            in_specs=[vmem(a.shape) for a in ins],
            out_specs=vmem((size, 16, cols)),
            scratch_shapes=[pltpu.VMEM((16, first_sums.shape[1]), f32)],
        ),
        cost_estimate=HINT,
    )(core[None], *ins)


def whole_call(kernel, outs, ins, blocks):
    def some(array, n):
        rest = (0,) * (array.ndim - 1)
        return pl.BlockSpec((abs(n), *array.shape[1:]), lambda *_: (int(n < 0), *rest))

    return pl.pallas_call(
        kernel,
        out_shape=[jax.ShapeDtypeStruct(o, d) for o, d in outs],
        grid=(1,),
        in_specs=[some(a, n) for a, n in zip(ins, blocks)],
        out_specs=[vmem(o) for o, _ in outs],
        cost_estimate=HINT,
    )(*ins)


def corner_back(parts, size):
    return swap_dp(parts[0], 1, size), swap_dp(parts[1], 2, size)


def corner_add(parts, got):
    keep = parts[2:4]

    def kernel(one_ref, two_ref, r1_ref, r2_ref, o1_ref, o2_ref):
        o1_ref[...] = one_ref[...] + r2_ref[...]
        o2_ref[...] = two_ref[...] + r1_ref[...]

    return whole_call(
        kernel, [(item.shape, bf16) for item in keep], [*keep, *got], (2, 2, 2, 2)
    )


def near_back(sums, size):
    return swap_dp(sums[0], 1, size), swap_dp(sums[1], 2, size)


def near_add(own, first, got):
    def kernel(own_ref, f1_ref, f2_ref, r1_ref, r2_ref, keep_ref, *outs):
        def total(k):
            early = f1_ref[k] if k < 2 else f2_ref[k - 2]
            late = r2_ref[k] if k < 2 else r1_ref[k - 2]
            return own_ref[k].astype(f32) + early.astype(f32) + late.astype(f32)

        keep_ref[...] = total(0)
        for k in (1, 2, 3):
            outs[k - 1][...] = total(k).astype(bf16)

    shape = own.shape[1:]
    return whole_call(
        kernel, [(shape, f32)] + [(shape, bf16)] * 3, [own, *first, *got], (4, -2, -2, 2, 2)
    )


def far_back(sums, size):
    return [swap_dp(item, 4 * (k + 1), size) for k, item in enumerate(sums[1:])]


def project(tokens, weights, vectors, core, side):
    rows, width = tokens.shape
    cols = weights.shape[2]

    def kernel(core_ref, x_ref, w_ref, v_ref, q_out, k_out, v_out):
        half = core_ref[0] ^ side
        bias = jnp.where(half == 0, v_ref[0:8, :cols], v_ref[0:8, cols:])
        x = x_ref[...]
        q_out[...] = (dot(x, w_ref[0], NN) + bias[0:1]).astype(bf16)
        k_out[...] = dot(x, w_ref[1], NN).astype(bf16)
        v_out[...] = (dot(x, w_ref[2], NN) + bias[1:2]).astype(bf16)

    tile = pl.BlockSpec((ROWS, cols), lambda i, *_: (i, 0))
    return pl.pallas_call(
        kernel,
        out_shape=[jax.ShapeDtypeStruct((rows, cols), bf16)] * 3,
        grid_spec=pltpu.PrefetchScalarGridSpec(
            num_scalar_prefetch=1,
            grid=(rows // ROWS,),
            in_specs=[
                pl.BlockSpec((ROWS, width), lambda i, *_: (i, 0)),
                vmem(weights.shape),
                vmem(vectors.shape),
            ],
            out_specs=[tile] * 3,
        ),
        cost_estimate=HINT,
    )(core[None], tokens, weights, vectors)


def token_gradient(first_delta, deltas, weights, part, parts):
    count, rows, cols = deltas[0].shape
    width = weights[0].shape[1]
    steps = rows // ROWS // parts

    def kernel(f_ref, d0_ref, d1_ref, w0_ref, w1_ref, *refs):
        o_ref = refs[-1]
        total = f_ref[...]
        for d_ref, w_ref in ((d0_ref, w0_ref), (d1_ref, w1_ref)):
            for g in range(count):
                total = total + dot(d_ref[g], w_ref[g], NT)
        o_ref[...] = total

    tile = pl.BlockSpec((ROWS, width), lambda i: (i + part * steps, 0))
    delta_part = pl.BlockSpec((count, ROWS, cols), lambda i: (0, i + part * steps, 0))
    return pl.pallas_call(
        kernel,
        out_shape=jax.ShapeDtypeStruct((rows, width), f32),
        grid=(steps,),
        in_specs=[tile, delta_part, delta_part] + [vmem(weights[0].shape)] * 2,
        out_specs=tile,
        input_output_aliases={0: 0},
        cost_estimate=pl.CostEstimate(
            flops=4 * count * rows * width * cols // parts,
            transcendentals=0,
            bytes_accessed=16 * rows * cols // parts,
        ),
    )(first_delta, *deltas, *weights)


def center(values):
    mean = jnp.mean(values, axis=-1, keepdims=True)
    centred = values - mean
    var = jnp.mean(centred * centred, axis=-1, keepdims=True)
    rinv = lax.rsqrt(var + norm_eps)
    return centred * rinv, rinv


def norm_back(grad, normed, rinv, gain):
    scaled = grad * gain
    return rinv * (
        scaled
        - jnp.mean(scaled, axis=-1, keepdims=True)
        - normed * jnp.mean(scaled * normed, axis=-1, keepdims=True)
    )


def add_rows(ref, items):
    for i, item in enumerate(items):
        ref[i : i + 1, : item.shape[1]] += jnp.sum(item, axis=0, keepdims=True)


def clear(*refs):
    @pl.when(pl.program_id(0) == 0)
    def _():
        for ref in refs:
            ref[...] = jnp.zeros(ref.shape, f32)


def row_call(kernel, tiles, wholes, outs, sums):
    rows = tiles[0].shape[0]

    def tile(cols):
        return pl.BlockSpec((ROWS, cols), lambda i: (i, 0))

    return pl.pallas_call(
        kernel,
        out_shape=[jax.ShapeDtypeStruct((rows, n), d) for n, d in outs]
        + [jax.ShapeDtypeStruct((8, n), f32) for n in sums],
        grid=(rows // ROWS,),
        in_specs=[tile(a.shape[1]) for a in tiles] + [vmem(a.shape) for a in wholes],
        out_specs=[tile(n) for n, _ in outs] + [vmem((8, n)) for n in sums],
        cost_estimate=HINT,
    )(*tiles, *wholes)


def first_block(tokens, context, weights, vectors):
    def kernel(x_ref, c0_ref, c1_ref, w0_ref, w1_ref, v_ref, out, low):
        total = dot(c0_ref[...], w0_ref[...], NT) + dot(c1_ref[...], w1_ref[...], NT)
        total = x_ref[...].astype(f32) + total + v_ref[2:3]
        out[...] = total
        low[...] = (center(total)[0] * v_ref[3:4] + v_ref[4:5]).astype(bf16)

    width = tokens.shape[1]
    return row_call(
        kernel, [tokens, *context], [*weights, vectors], [(width, f32), (width, bf16)], ()
    )


def outer_block(hidden, cotangent, act, weights, vectors):
    def kernel(
        h_ref, c_ref, a0_ref, a1_ref, w0_ref, w1_ref, v_ref, out, delta, low, sums
    ):
        clear(sums)

        feed = dot(a0_ref[...], w0_ref[...], NT) + dot(a1_ref[...], w1_ref[...], NT)
        normed, rinv = center(h_ref[...].astype(f32) + (v_ref[5:6] + feed))
        out[...] = normed * v_ref[6:7] + v_ref[7:8]
        cot = c_ref[...].astype(f32)
        found = norm_back(cot, normed, rinv, v_ref[6:7])
        delta[...] = found
        low[...] = found.astype(bf16)
        add_rows(sums, (found, cot * normed, cot))

    width = hidden.shape[1]
    return row_call(
        kernel,
        [hidden, cotangent, *act],
        [*weights, vectors],
        [(width, f32), (width, f32), (width, bf16)],
        (width,),
    )


def inner_back(second_delta, inner_delta, first_in, weights, vectors):
    def kernel(
        s_ref, d0_ref, d1_ref, f_ref, w0_ref, w1_ref, v_ref, delta, low, sums, inner
    ):
        clear(sums, inner)
        ones = jnp.ones((8, ROWS), bf16)
        half = d0_ref.shape[1]
        inner[:, :half] += dot(ones, d0_ref[...], NN)
        inner[:, half:] += dot(ones, d1_ref[...], NN)

        grad = dot(d0_ref[...], w0_ref[...], NT) + dot(d1_ref[...], w1_ref[...], NT)
        grad = s_ref[...] + grad
        normed, rinv = center(f_ref[...])
        found = norm_back(grad, normed, rinv, v_ref[3:4])
        delta[...] = found
        low[...] = found.astype(bf16)
        add_rows(sums, (found, grad * normed, grad))

    width = first_in.shape[1]
    return row_call(
        kernel,
        [second_delta, *inner_delta, first_in],
        [*weights, vectors],
        [(width, f32), (width, bf16)],
        (width, 2 * inner_delta[0].shape[1]),
    )


def three_parts(row):
    high = row.astype(bf16).astype(f32)
    middle = (row - high).astype(bf16).astype(f32)
    return [high, middle, row - high - middle]


def extra_lanes(shape, keys_valid):
    lane = lax.broadcasted_iota(jnp.int32, shape, 1) % HD
    row = lax.broadcasted_iota(jnp.int32, shape, 0)
    bias = jnp.where(row < keys_valid, 0.0, masked_score)
    return jnp.where(lane == 0, bias, jnp.where(lane < 4, 1.0, 0.0)).astype(bf16)


def extra_rows(first, row, length):
    rows = [jnp.full((1, length), first, f32)]
    rows += three_parts(row) if row is not None else []
    rows.append(jnp.zeros((16 - len(rows), length), f32))
    return jnp.concatenate(rows, 0).astype(bf16)


def with_rows(own_t, h, first, row):
    length = own_t.shape[1]
    own = own_t[h * HD : (h + 1) * HD]
    rest = [extra_rows(first, row, length), jnp.zeros((HD - 16, length), bf16)]
    return jnp.concatenate([own] + rest if h == 0 else rest + [own], 0)


def attend_forward_kernel(lens, q_ref, k_ref, v_ref, ctx_ref, lse_ref):
    seq_len, lanes = q_ref.shape
    lane = lax.broadcasted_iota(jnp.int32, (seq_len, lanes), 1)
    extra = extra_lanes((seq_len, lanes), lens[pl.program_id(0)])
    ones = jnp.ones((16, seq_len), bf16)
    loaded = {}

    def scores(h):
        if h == 0:
            query_t = (q_ref[...] * jnp.bfloat16(score_scale)).T
            loaded[0] = (query_t, k_ref[...], v_ref[...].T)
        query_t, keys, _ = loaded[0]
        return dot(jnp.where(lane // HD == h, keys, extra), with_rows(query_t, h, 1.0, None), NN)

    pieces = []
    ahead = scores(0)
    for h in range(2):
        now = ahead
        if h == 0:
            ahead = scores(1)
        top = jnp.max(now, axis=0, keepdims=True)
        expo = jnp.exp(now - top).astype(bf16)
        value_t = loaded[0][2][h * HD : (h + 1) * HD]
        found = dot(jnp.concatenate([value_t, ones], 0), expo, NN)
        total = found[HD : HD + 1]
        pieces.append(found[:HD] / total)
        lse_ref[0, 0, h : h + 1, :] = top + jnp.log(total)
        if h == 1:
            ctx_ref[...] = jnp.concatenate(pieces, 0).T.astype(bf16)
            pieces = []


def attend_backward_kernel(lens, q_ref, k_ref, v_ref, d_ref, c_ref, lse_ref, out_ref):
    seq_len, lanes = q_ref.shape
    lane = lax.broadcasted_iota(jnp.int32, (seq_len, lanes), 1)
    extra = extra_lanes((seq_len, lanes), lens[pl.program_id(0)])
    loaded = {}

    def products(h):
        if h == 0:
            query = q_ref[...] * jnp.bfloat16(score_scale)
            delta = d_ref[...]
            delta_t = delta.T
            inner = delta_t.astype(f32) * c_ref[...].T.astype(f32)
            keys = k_ref[...]
            loaded[0] = (query, query.T, delta, delta_t, inner, keys, keys.T, v_ref[...])
        _, query_t, _, delta_t, inner, keys, _, values = loaded[0]
        own = lane // HD == h
        inner = jnp.sum(inner[h * HD : (h + 1) * HD], axis=0, keepdims=True)
        lse = lse_ref[0, 0, h : h + 1, :]
        logs = dot(jnp.where(own, keys, extra), with_rows(query_t, h, 1.0, -lse), NN)
        centred = dot(jnp.where(own, values, extra), with_rows(delta_t, h, 0.0, -inner), NN)
        return logs, centred

    ahead = products(0)
    for h in range(2):
        logs, centred = ahead
        if h == 0:
            ahead = products(1)
        query, _, delta, _, _, _, keys_t, _ = loaded[0]
        probs = jnp.exp(logs)
        score_delta = (probs * centred).astype(bf16)
        own = lane // HD == h
        part_v = dot(probs.astype(bf16), jnp.where(own, delta, jnp.bfloat16(0)), NN)
        part_k = dot(score_delta, jnp.where(own, query, jnp.bfloat16(0)), NN)
        part_q = dot(keys_t[h * HD : (h + 1) * HD], score_delta, NN)
        if h == 0:
            dv, dk, dq = part_v, part_k, part_q
        else:
            out_ref[0] = (jnp.concatenate([dq, part_q], 0).T * score_scale).astype(bf16)
            out_ref[1] = (dk + part_k).astype(bf16)
            out_ref[2] = (dv + part_v).astype(bf16)


def attend_call(kernel, lens, operands, lse_in, seq_count):
    rows, cols = operands[0].shape
    seq_len = rows // seq_count
    pairs = cols // (2 * HD)
    tile = pl.BlockSpec((seq_len, 2 * HD), lambda s, p, *_: (s, p))
    stat = pl.BlockSpec((1, 1, 2, seq_len), lambda s, p, *_: (s, p, 0, 0))
    if lse_in:
        out_shape = jax.ShapeDtypeStruct((3, rows, cols), bf16)
        out_specs = pl.BlockSpec((3, seq_len, 2 * HD), lambda s, p, *_: (0, s, p))
    else:
        out_shape = [
            jax.ShapeDtypeStruct((rows, cols), bf16),
            jax.ShapeDtypeStruct((seq_count, pairs, 2, seq_len), f32),
        ]
        out_specs = [tile, stat]
    return pl.pallas_call(
        kernel,
        out_shape=out_shape,
        grid_spec=pltpu.PrefetchScalarGridSpec(
            num_scalar_prefetch=1,
            grid=(seq_count, pairs),
            in_specs=[tile] * len(operands) + [stat] * len(lse_in),
            out_specs=out_specs,
        ),
        cost_estimate=HINT,
    )(lens, *operands, *lse_in)


def on_device(
    tokens,
    cotangent,
    lengths,
    query_weight,
    key_weight,
    value_weight,
    out_weight,
    query_bias,
    value_bias,
    out_bias,
    first_gain,
    first_shift,
    inner_weight,
    inner_bias,
    outer_weight,
    outer_bias,
    second_gain,
    second_shift,
):
    size = lax.axis_size("dp")
    index = lax.axis_index("dp")
    core = lax.axis_index("tensor")
    orders = stage_orders(size)
    seq_count = lengths.shape[0] // 2
    lens = lax.dynamic_slice_in_dim(lengths, core * seq_count, seq_count, 0)
    fast = size == 16 and query_weight.shape[0] % 16 == 0
    half = query_weight.shape[1]
    step = half

    vectors = (
        query_bias,
        value_bias,
        out_bias,
        first_gain,
        first_shift,
        outer_bias,
        second_gain,
        second_shift,
        inner_bias,
    )
    bounds = [0]
    for item in vectors:
        bounds.append(bounds[-1] + item.shape[0])
    projections = (query_weight, key_weight, value_weight)
    out_t = out_weight.T
    outer_t = outer_weight.T

    if fast:
        shard = pack_first(projections, vectors)
        far = [swap_dp(shard, d, size) for d in (8, 4, 12)]
        low, high = jnp.stack([shard, far[0]]), jnp.stack(far[1:])
        two_low, one_high = swap_dp(low, 2, size), swap_dp(high, 1, size)
        one_low, two_high = swap_dp(low, 1, size), swap_dp(high, 2, size)
        shard_a = jnp.concatenate([out_t, inner_weight], 1)
        far_a = swap_dp(after(shard_a, low, high), 8, size)
        tokens_t = tokens.T
        pieces = [low, high, one_low, one_high, two_low, two_high]
        pieces += [swap_dp(two_low, 1, size), swap_dp(one_high, 2, size)]
        far_a, *pieces, tokens_t = lax.optimization_barrier((far_a, *pieces, tokens_t))
        low_a = jnp.stack([shard_a, far_a])
        high_a = swap_dp(low_a, 4, size)
        two_low_a, one_low_a = swap_dp(low_a, 2, size), swap_dp(low_a, 1, size)
        wqkv0, vecs, ib = place_first(
            pieces, index, 3, size, (query_bias.shape[0], inner_bias.shape[0])
        )
    else:
        own_vec = jnp.concatenate(vectors)[None, :]
        all_vec = gather_rows(own_vec, orders[0], size, index).astype(f32)
        found = [all_vec[:, a:b].reshape(1, -1) for a, b in zip(bounds[:-1], bounds[1:])]
        vecs = jnp.concatenate(found[:-1] + [jnp.zeros_like(found[0])] * 8, 0)
        ib = found[-1]
        wqkv0 = jnp.stack(
            [gather_rows(w, o, size, index) for w, o in zip(projections, orders)]
        )
        wo0 = gather_rows(out_t, orders[2], size, index)
        wi0 = gather_rows(inner_weight, orders[0], size, index)
        wu0 = gather_rows(outer_t, orders[1], size, index)

    wqkv = (wqkv0, swap_core(wqkv0))
    hidden_half = inner_weight.shape[1]
    ib = (
        jnp.where(core == 0, ib[:, :hidden_half], ib[:, hidden_half:]),
        jnp.where(core == 0, ib[:, hidden_half:], ib[:, :hidden_half]),
    )

    q, k, v, ctx, lse = [], [], [], [], []
    for t in range(2):
        found = project(tokens, wqkv[t], vecs, core, t)
        q.append(found[0])
        k.append(found[1])
        v.append(found[2])
    if fast:
        far_b = swap_dp(after(outer_t, wqkv[0]), 8, size)
        high_a, far_b, one_low_a, two_low_a, *q = lax.optimization_barrier(
            (high_a, far_b, one_low_a, two_low_a, *q)
        )
        one_high_a, two_high_a = swap_dp(high_a, 1, size), swap_dp(high_a, 2, size)
        low_b = jnp.stack([outer_t, far_b])
        two_low_b, one_low_b = swap_dp(low_b, 2, size), swap_dp(low_b, 1, size)
        high_b = swap_dp(low_b, 4, size)
    for t in range(2):
        if fast and t == 1:
            q[1] = after(q[1], ctx[0])
        c, s = attend_call(attend_forward_kernel, lens, (q[t], k[t], v[t]), (), seq_count)
        lse.append(s)
        if fast and t == 0:
            pieces_a = [low_a, high_a, one_low_a, one_high_a, two_low_a, two_high_a]
            *pieces_a, high_b, two_low_b, one_low_b, c = lax.optimization_barrier(
                (*pieces_a, high_b, two_low_b, one_low_b, c)
            )
            pieces_a += [swap_dp(pieces_a[4], 1, size), swap_dp(pieces_a[3], 2, size)]
        if fast and t == 1:
            *pieces_a, c = lax.optimization_barrier((*pieces_a, c))
            one_high_b, two_high_b = swap_dp(high_b, 1, size), swap_dp(high_b, 2, size)
            wo0, wi0 = place_cols(pieces_a, index, (half, inner_weight.shape[1]), size)
        ctx.append(c)

    wo = (wo0, swap_core(wo0))
    wi = (wi0, swap_core(wi0))
    first_in, hidden = first_block(tokens, ctx, wo, vecs)
    if fast:
        one_high_b, two_low_b, hidden = lax.optimization_barrier((one_high_b, two_low_b, hidden))
        pieces_b = [low_b, high_b, one_low_b, one_high_b, two_low_b, two_high_b]
        pieces_b += [swap_dp(two_low_b, 1, size), swap_dp(one_high_b, 2, size)]
    act, slope = [], []
    for t in range(2):
        u = dot(hidden, wi[t], NN) + ib[t]
        cdf = 0.5 * (1.0 + lax.erf(u * (0.5**0.5)))
        act.append((u * cdf).astype(bf16))
        pdf = jnp.exp(-0.5 * u * u) * 0.3989422804014327
        slope.append((cdf + u * pdf).astype(bf16))
        if fast and t == 0:
            *pieces_b, act[0] = lax.optimization_barrier((*pieces_b, act[0]))
            (wu0,) = place_cols(pieces_b, index, (inner_weight.shape[1],), size)
            hidden = after(hidden, wu0)
    wu = (wu0, swap_core(wu0))
    layer_out, second_delta, feed_delta, second_sums = outer_block(
        hidden, cotangent, act, wu, vecs
    )

    def product(left, right):
        other = dot(left, right[1], TN).astype(bf16)
        other = swap_core(other)
        return dot(left, right[0], TN).astype(bf16), other

    gu = product(feed_delta, act)
    feed_delta, *gu = lax.optimization_barrier((feed_delta, *gu))
    inner_delta = [None, None]
    for t in (1, 0):
        inner_delta[t] = (dot(feed_delta, wu[t], NN) * slope[t].astype(f32)).astype(bf16)
    gi = product(hidden, inner_delta)
    inner_delta[0], inner_delta[1], *gi = lax.optimization_barrier((*inner_delta, *gi))
    if fast:
        parts_u = split_cols([gu, gi], index, size, 2 * step)
        first_u = corner_back(parts_u, size)
        inner_delta[0], inner_delta[1] = [after(d, parts_u[4]) for d in inner_delta]
    first_delta, branch_delta, first_sums, inner_sums = inner_back(
        second_delta, inner_delta, first_in, wi, vecs
    )
    go = list(product(branch_delta, ctx))
    ctx_delta = [dot(branch_delta, wo[t], NN).astype(bf16) for t in range(2)]

    def joined(pair):
        return jnp.where(
            core == 0, jnp.concatenate(pair, 1), jnp.concatenate(pair[::-1], 1)
        )

    if fast:
        table = pack_table(first_sums, second_sums, inner_sums, core, size, half)
        *first_u, table, ctx_delta[0], ctx_delta[1], go[0], go[1] = lax.optimization_barrier(
            (*first_u, table, *ctx_delta, *go)
        )
        sums_u = corner_add(parts_u, first_u)
        got_u = near_back(sums_u, size)
        ctx_delta[1] = after(ctx_delta[1], table, sums_u[0])

    def attend_back(t):
        return attend_call(
            attend_backward_kernel,
            lens,
            (q[t], k[t], v[t], ctx_delta[t], ctx[t]),
            (lse[t],),
            seq_count,
        )

    deltas = [None, None]
    deltas[1] = attend_back(1)
    if fast:
        *got_u, deltas[1] = lax.optimization_barrier((*got_u, deltas[1]))
        last_u = near_add(parts_u[4], first_u, got_u)
        got_u = far_back(last_u, size)
        deltas[1] = after(deltas[1], last_u[0])
        others, other_sums = gradients_other(tokens_t, deltas[1])
        ctx_delta[0] = after(ctx_delta[0], others)
        others = swap_core(others)
        deltas[0] = attend_back(0)
        parts_q = gradients_own(
            tokens_t,
            deltas[0],
            others,
            other_sums,
            go,
            table,
            index,
            core,
            size,
            query_bias.shape[0],
        )
        *got_u, own = lax.optimization_barrier((*got_u, parts_q[4]))
        parts_q = [*parts_q[:4], own]
        first_q = corner_back(parts_q, size)
        token_grad = token_gradient(
            after(first_delta, parts_q[4]), [after(d, parts_q[4]) for d in deltas], wqkv, 0, 2
        )
        *first_q, token_grad = lax.optimization_barrier((*first_q, token_grad))

        def total(last, got):
            return last[0] + got[0].astype(f32) + got[1].astype(f32) + got[2].astype(f32)

        out_ui = total(last_u, got_u)
        hidden_half = out_ui.shape[1] // 2
        out_gu = out_ui[:, :hidden_half].T
        out_gi = out_ui[:, hidden_half:]
        sums_q = corner_add(parts_q, first_q)
        got_q = near_back(sums_q, size)
        last_q = near_add(parts_q[4], first_q, got_q)
        got_q = far_back(last_q, size)
        token_grad = token_gradient(token_grad, [after(d, last_q[0]) for d in deltas], wqkv, 1, 2)
        out_q = total(last_q, got_q)
        n = query_weight.shape[0]
        out_qkv = [out_q[g * n : (g + 1) * n] for g in range(3)]
        out_go = out_q[3 * n : 4 * n].T
        vec = out_q[4 * n :]
        vec = vec + swap_core(vec)
        vec_out = [vec[i, : item.shape[0]] for i, item in enumerate(vectors)]
    else:
        deltas[0] = attend_back(0)
        token_grad = token_gradient(first_delta, deltas, wqkv, 0, 1)

        def reduce(pair, order):
            summed = (pair[0].astype(f32) + pair[1].astype(f32)).astype(bf16)
            return scatter_rows(summed, order, size, index)

        out_gu = reduce(gu, orders[1]).T
        out_gi = reduce(gi, orders[0])
        out_go = reduce(go, orders[2]).T
        out_qkv = [
            reduce(product(tokens, [d[g] for d in deltas]), order) for g, order in enumerate(orders)
        ]
        bias_grads = [
            joined([jnp.sum(d[g].astype(f32), axis=0, keepdims=True) for d in deltas]) for g in (0, 2)
        ]
        bias_grads += [s[i : i + 1] for s in (first_sums, second_sums) for i in range(3)]
        bias_grads.append(joined(jnp.split(inner_sums[:1], 2, 1)))
        packed = jnp.concatenate([item.reshape(size, -1) for item in bias_grads], axis=1)
        packed = packed + swap_core(packed)
        own = scatter_rows(packed, orders[0], size, index).reshape(-1)
        vec_out = [own[a:b] for a, b in zip(bounds[:-1], bounds[1:])]
    return (
        layer_out,
        token_grad,
        out_qkv[0],
        out_qkv[1],
        out_qkv[2],
        out_go,
        vec_out[0],
        vec_out[1],
        vec_out[2],
        vec_out[3],
        vec_out[4],
        out_gi,
        vec_out[8],
        out_gu,
        vec_out[5],
        vec_out[6],
        vec_out[7],
    )


def solution(mesh):
    both = P(("dp", "tensor"), None)
    cols = P("dp", "tensor")
    rows = P("tensor", "dp")
    vec = P("dp")
    in_specs = (
        both, both, vec, cols, cols, cols, rows, vec, vec, vec, vec, vec, cols, vec, rows, vec, vec, vec,
    )
    out_specs = (
        both, both, cols, cols, cols, rows, vec, vec, vec, vec, vec, cols, vec, rows, vec, vec, vec,
    )
    return jax.shard_map(
        on_device, mesh=mesh, in_specs=in_specs, out_specs=out_specs, check_vma=False
    )
```
